512 devices in a mesh: dp: 16 (over y_hi, x, core), fsdp: 32 (over y_lo, z).
Axes of the slice: x: 4, y: 4 (y_hi: 2, y_lo: 2; y = y_hi * 2 + y_lo), z: 16, core: 2. Of those that a mesh axis runs over, the one named last changes fastest.
Arguments:
- hidden: bfloat16 [512, 256, 4096], P(('dp', 'fsdp')), may hold values from -40 to 40
- lengths: int32 [512], P(('dp', 'fsdp')), may hold values from 64 to 256
- list_ids: int32 [512], P('dp'), may hold values from 0 to 1023, as said below
- list_owner: int32 [1024], replicated, may hold values from 0 to 15, as said below
- attn_gain: float32 [4096], replicated, may hold values from 0.25 to 1.75
- final_gain: float32 [4096], replicated, may hold values from 0.25 to 1.75
- w_query: bfloat16 [4096, 2048], P('fsdp'), may hold values from -24 to 24
- w_key: bfloat16 [4096, 512], P('fsdp'), may hold values from -1 to 1
- w_value: bfloat16 [4096, 512], P('fsdp'), may hold values from -0.09375 to 0.09375
- w_out: bfloat16 [2048, 4096], P('fsdp'), may hold values from -0.125 to 0.125
Outputs:
- inbox: bfloat16 [16, 16, 4, 4096], P('dp', None, None, 'fsdp')
The draws below stay inside these ranges and needn't reach their ends.
Inputs may be any that keep to these rules, and one draw needn't show every extreme that they name: Positions from lengths[p] on are padding. `list_ids`: in each aligned block of 32 passages (those of one index of dp), at most 4 passages name lists of one owner, and in every block some owner is named by exactly 4 passages. `list_owner`: every owner holds exactly 64 lists.
All inputs are finite; a program needn't handle non-finite values.
Results may differ from the reference program's by a relative error of at most 0.0029.
The reference program's roundings to bfloat16 on the way (of `normed`, `key_rows`, `queries`, `weights`, `context` and `embedded`) count: a program that leaves them out, or rounds other values in their place, can miss the bound.
Values may be sent and summed in bfloat16 or wider, within the bound.
No kernel may reach another device: no remote copies, remote signals or barrier semaphores. Data moves between devices by JAX's collectives and lax.ppermute only.
A program may use at most 64 MiB of HBM per device.

```python
import math
import jax
import jax.numpy as jnp
from jax import lax

D = 4096
HEADS = 16
KV_HEADS = 4
HEAD = 128
LEN = 256
PASSAGES = 512
LISTS = 1024
CAP = 4
N_DP = 16


def owner_order(key):
    return jax.random.permutation(jax.random.fold_in(key, 7), LISTS)


def draw_list_owner(key, part):
    return (owner_order(key) % N_DP).astype(jnp.int32)


def draw_list_ids(key, part):
    inverse = jnp.argsort(owner_order(key))
    block_size = PASSAGES // N_DP
    slot_count = N_DP * CAP
    slot_owner = jnp.arange(slot_count) // CAP
    crowded = jax.random.randint(jax.random.fold_in(key, 8), (), 0, N_DP)

    def one_block(index):
        block_key = jax.random.fold_in(jax.random.fold_in(key, 9), index)
        noise = jax.random.randint(jax.random.fold_in(block_key, 1), (slot_count,), 0, 1 << 20)
        ranking = jnp.where(slot_owner == crowded, jnp.arange(slot_count), (noise + 1) * slot_count + jnp.arange(slot_count))
        chosen = slot_owner[jnp.argsort(ranking)[:block_size]]
        mixing = jax.random.randint(jax.random.fold_in(block_key, 2), (block_size,), 0, 1 << 20) * block_size + jnp.arange(block_size)
        owners = chosen[jnp.argsort(mixing)]
        choice_in_owner = jax.random.randint(jax.random.fold_in(block_key, 3), (block_size,), 0, LISTS // N_DP)
        return inverse[owners + N_DP * choice_in_owner]
    return jax.vmap(one_block)(jnp.arange(N_DP)).reshape(PASSAGES).astype(jnp.int32)


def key_base(key):
    drawn = jax.random.normal(jax.random.fold_in(key, 21), (D, KV_HEADS * HEAD), jnp.float32)
    return jnp.clip(drawn, -6.0, 6.0) / math.sqrt(D)


def draw_w_key(key, part):
    return key_base(key).astype(jnp.bfloat16)


def draw_w_query(key, part):
    drawn = jax.random.normal(jax.random.fold_in(key, 22), (D, HEADS * HEAD), jnp.float32)
    own_part = jnp.clip(drawn, -6.0, 6.0) / math.sqrt(D)
    return own_part.astype(jnp.bfloat16)


def draw_hidden(key, part):
    drawn = jax.random.normal(jax.random.fold_in(key, 31), (PASSAGES, LEN, D), jnp.float32)
    return jnp.clip(drawn, -6.0, 6.0).astype(jnp.bfloat16)


def set_ends(values, rng, low, largest):
    extent = values.shape
    index_at = [jax.random.randint(jax.random.fold_in(rng, axis), (), 0, extent[axis]) for axis in range(len(extent))]
    values = values.at[tuple(index_at)].set(low)
    longest = extent.index(max(extent))
    index_at[longest] = (index_at[longest] + 1) % extent[longest]
    return values.at[tuple(index_at)].set(largest)


def levels(own_key, extent, cuts, low, largest):
    factor_of, own = 1.0, jax.random.fold_in(own_key, 6)
    for dim, blocks in cuts:
        steps = jnp.exp(jax.random.uniform(jax.random.fold_in(own, dim), (blocks,), jnp.float32, low / len(cuts), largest / len(cuts)))
        factor_of = factor_of * jnp.repeat(steps, extent[dim] // blocks).reshape([-1 if axis == dim else 1 for axis in range(len(extent))])
    return factor_of


def centred(key, extent, scale, limit, split=(), kind=jnp.bfloat16):
    result = jax.random.normal(key, extent, jnp.float32) * scale
    if len(split) > 0:
        result = levels(key, extent, split, -0.22, 0.18) * result
    return jnp.clip(result, min=-limit, max=limit).astype(kind)


def setup_inputs(seed: int = 0) -> dict:
    seeds = jax.random.split(jax.random.key(seed), 11)
    return {
        "hidden": draw_hidden(jax.random.fold_in(seeds[10], 71), 0),
        "lengths": set_ends(jax.random.randint(seeds[1], (PASSAGES,), LEN // 4, LEN + 1), jax.random.fold_in(seeds[1], 1), LEN // 4, LEN).astype(jnp.int32),
        "list_ids": draw_list_ids(jax.random.fold_in(seeds[10], 71), 0),
        "list_owner": draw_list_owner(jax.random.fold_in(seeds[10], 71), 0),
        "attn_gain": jnp.clip(1.0 + 0.15 * jax.random.normal(seeds[4], (D,), jnp.float32), 0.25, 1.75),
        "final_gain": jnp.clip(1.0 + 0.15 * jax.random.normal(seeds[5], (D,), jnp.float32), 0.25, 1.75),
        "w_query": draw_w_query(jax.random.fold_in(seeds[10], 71), 0),
        "w_key": draw_w_key(jax.random.fold_in(seeds[10], 71), 0),
        "w_value": centred(seeds[8], (D, KV_HEADS * HEAD), D ** -0.5, 0.09375, ((0, 32),)),
        "w_out": centred(seeds[9], (HEADS * HEAD, D), (HEADS * HEAD) ** -0.5, 0.125, ((0, 32),)),
    }


def rope_tables(positions, head_width):
    halfway = head_width // 2
    frequency = 10000.0 ** (-jnp.arange(halfway, dtype=jnp.float32) * 2.0 / head_width)
    angles = positions.astype(jnp.float32)[..., None] * frequency
    return (jnp.cos(angles), jnp.sin(angles))

def rotate(vectors, cosine_table, sine_table):
    halfway = vectors.shape[-1] // 2
    first_half = vectors[..., :halfway]
    second_half = vectors[..., halfway:]
    return jnp.concatenate([first_half * cosine_table - second_half * sine_table, second_half * cosine_table + first_half * sine_table], axis=-1)

def reference(hidden, lengths, list_ids, list_owner, attn_gain, final_gain, w_query, w_key, w_value, w_out):
    cosine_table, sine_table = rope_tables(jnp.arange(LEN), HEAD)

    def embed_one(inputs):
        passage, length = inputs
        floats = passage.astype(jnp.float32)
        normed = (floats * lax.rsqrt(lax.optimization_barrier(jnp.mean(floats * floats, axis=-1, keepdims=True)) + 1e-05) * attn_gain).astype(jnp.bfloat16)
        key_sum = jnp.dot(normed, w_key, preferred_element_type=jnp.float32).reshape(LEN, KV_HEADS, HEAD)
        key_rows = rotate(key_sum, cosine_table[:, None, :], sine_table[:, None, :]).astype(jnp.bfloat16)
        value_rows = jnp.dot(normed, w_value, preferred_element_type=jnp.float32).reshape(LEN, KV_HEADS, HEAD)
        last_position = length - 1
        last_normed = lax.dynamic_index_in_dim(normed, last_position, 0, keepdims=False)
        last_input = lax.dynamic_index_in_dim(passage, last_position, 0, keepdims=False).astype(jnp.float32)
        query_sum = jnp.dot(last_normed, w_query, preferred_element_type=jnp.float32).reshape(HEADS, HEAD)
        query_cos, query_sin = rope_tables(last_position[None], HEAD)
        queries = (rotate(query_sum, query_cos, query_sin) * (1.0 / math.sqrt(HEAD))).astype(jnp.bfloat16)
        grouped = queries.reshape(KV_HEADS, HEADS // KV_HEADS, HEAD).astype(jnp.float32)
        scores = jnp.einsum('kgd,tkd->kgt', grouped, key_rows.astype(jnp.float32))
        visible = jnp.arange(LEN)[None, None, :] < length
        scores = jnp.where(visible, scores, -jnp.inf)
        powers = jnp.exp(scores - lax.optimization_barrier(jnp.max(scores, axis=-1, keepdims=True)))
        weights = (powers / lax.optimization_barrier(jnp.sum(powers, axis=-1, keepdims=True))).astype(jnp.bfloat16)
        context = jnp.einsum('kgt,tkd->kgd', weights.astype(jnp.float32), value_rows, precision=lax.Precision.HIGHEST)
        context = context.reshape(HEADS * HEAD).astype(jnp.bfloat16)
        residual = last_input + jnp.dot(context, w_out, preferred_element_type=jnp.float32)
        scaled = residual * final_gain
        return (scaled * lax.rsqrt(jnp.mean(scaled * scaled) + 1e-06)).astype(jnp.bfloat16)
    embedded = lax.map(embed_one, (hidden, lengths))
    block_size = PASSAGES // N_DP
    owners = list_owner[list_ids].reshape(N_DP, block_size)
    owner_marks = (owners[:, :, None] == jnp.arange(N_DP)[None, None, :]).astype(jnp.int32)
    slot_rank = lax.optimization_barrier(jnp.sum((jnp.cumsum(owner_marks, axis=1) - owner_marks) * owner_marks, axis=2))
    select = ((owners[:, None, None, :] == jnp.arange(N_DP)[None, :, None, None]) & (slot_rank[:, None, None, :] == jnp.arange(CAP)[None, None, :, None])).astype(jnp.float32)
    grouped_rows = embedded.reshape(N_DP, block_size, D).astype(jnp.float32)
    inbox = jnp.einsum('josr,jrd->ojsd', select, grouped_rows, precision=lax.Precision.HIGHEST)
    return inbox.astype(jnp.bfloat16)
```

```python
import math

import jax
import jax.numpy as jnp
from jax import lax
from jax.experimental import pallas as pl
from jax.experimental.pallas import tpu as pltpu
from jax.sharding import PartitionSpec as P

HEADS = 16
KV_HEADS = 4
HEAD = 128
X = 4
Y_LO = 2
Z = 16
BOTH = ("dp", "fsdp")

bf16 = jnp.bfloat16
f32 = jnp.float32


def dp_index(y_hi, x, core):
    return (y_hi * X + x) * 2 + core


def fsdp_index(y_lo, z):
    return y_lo * Z + z


Z_GROUPS = [[fsdp_index(yl, z) for z in range(Z)] for yl in range(Y_LO)]
CORE_SWAP = [(d, d ^ 1) for d in range(16)]
Y_LO_SWAP = [(i, i ^ Z) for i in range(32)]


def x_shift(step):
    return [
        (dp_index(yh, x, c), dp_index(yh, (x + step) % X, c))
        for yh in range(2)
        for x in range(X)
        for c in range(2)
    ]


def y_shift(step):
    pairs = []
    for y in range(4):
        to = (y + step) % 4
        for x in range(X):
            for z in range(Z):
                for c in range(2):
                    pairs.append(
                        (
                            dp_index(y // 2, x, c) * 32 + fsdp_index(y % 2, z),
                            dp_index(to // 2, x, c) * 32 + fsdp_index(to % 2, z),
                        )
                    )
    return pairs


def rope_tables(positions, head_width):
    halfway = head_width // 2
    frequency = 10000.0 ** (-jnp.arange(halfway, dtype=f32) * 2.0 / head_width)
    angles = positions.astype(f32)[..., None] * frequency
    cosine, sine = jnp.cos(angles), jnp.sin(angles)
    return (
        jnp.concatenate([cosine, cosine], axis=-1),
        jnp.concatenate([-sine, sine], axis=-1),
    )


def plane_gather(piece, x):
    plus = lax.ppermute(piece, "dp", x_shift(1))
    minus = lax.ppermute(piece, "dp", x_shift(-1))
    far = lax.ppermute(piece, "dp", x_shift(2))
    received = jnp.stack([piece, plus, far, minus])
    own = jnp.take(received, (x - jnp.arange(X)) % X, axis=0)
    low = lax.ppermute(own[:2], BOTH, y_shift(-1))
    high = lax.ppermute(own[2:], BOTH, y_shift(1))
    return own, low, high


def fill(scratch, own, low, high, y_lo, sem):
    copies = []
    for x in range(X):
        copies.append(
            pltpu.make_async_copy(own.at[x], scratch.at[y_lo, :, x], sem.at[x])
        )
        half = low if x < 2 else high
        copies.append(
            pltpu.make_async_copy(half.at[x % 2], scratch.at[1 - y_lo, :, x], sem.at[X + x])
        )
    for copy in copies:
        copy.start()
    for copy in copies:
        copy.wait()


def attend_body(
    y_lo_ref, len_ref, normed_ref, other_ref, q_ref, cos_ref, sin_ref, own, low, high, u_ref, w_ref, sem
):
    y_lo = y_lo_ref[0]
    fill(w_ref, own, low, high, y_lo, sem)
    weight = w_ref[...].reshape(Y_LO * Z * X * 32, 256)
    cosine, sine = cos_ref[...], sin_ref[...]
    for p, rows_ref in enumerate((normed_ref, other_ref)):
        rows = rows_ref[...]
        keys = jnp.dot(rows, weight, preferred_element_type=f32)
        scores = []
        for g in range(2):
            part = keys[:, g * HEAD : (g + 1) * HEAD]
            turned = (part * cosine + pltpu.roll(part, HEAD // 2, 1) * sine).astype(bf16)
            scores.append(
                lax.dot_general(
                    q_ref[p, g], turned, (((1,), (1,)), ((), ())), preferred_element_type=f32
                )[:4]
            )
        scores = jnp.concatenate(scores, axis=0)
        place = lax.broadcasted_iota(jnp.int32, scores.shape, 1)
        scores = jnp.where(place < len_ref[p], scores, -jnp.inf)
        powers = jnp.exp(scores - jnp.max(scores, axis=-1, keepdims=True))
        weights = (powers / jnp.sum(powers, axis=-1, keepdims=True)).astype(bf16)
        u_ref[p] = jnp.dot(weights, rows, preferred_element_type=f32)


def attend(y_lo, lengths, normed, other, q, cosine, sine, pieces):
    vmem = pl.BlockSpec(memory_space=pltpu.VMEM)
    smem = pl.BlockSpec(memory_space=pltpu.SMEM)
    anywhere = pl.BlockSpec(memory_space=pl.ANY)
    return pl.pallas_call(
        attend_body,
        out_shape=jax.ShapeDtypeStruct((2, 8, normed.shape[1]), f32),
        in_specs=[smem, smem, vmem, vmem, vmem, vmem, vmem, anywhere, anywhere, anywhere],
        out_specs=vmem,
        scratch_shapes=[
            pltpu.VMEM((Y_LO, Z, X, 32, 256), bf16),
            pltpu.SemaphoreType.DMA((2 * X,)),
        ],
        compiler_params=pltpu.CompilerParams(vmem_limit_bytes=40 << 20),
        name="attend",
    )(y_lo, lengths, normed, other, q, cosine, sine, *pieces)


def weigh_body(y_lo_ref, u_ref, own, low, high, out_ref, w_ref, sem):
    fill(w_ref, own, low, high, y_lo_ref[0], sem)
    weight = w_ref[...].reshape(Y_LO * Z * X * 32, 256)
    u = u_ref[...].reshape(16, -1)
    first = u.astype(bf16)
    rest = u - first.astype(f32)
    second = rest.astype(bf16)
    third = (rest - second.astype(f32)).astype(bf16)
    parts = [jnp.dot(t, weight, preferred_element_type=f32) for t in (third, second, first)]
    total = parts[0] + parts[1] + parts[2]
    kind = (lax.broadcasted_iota(jnp.int32, (16, HEAD), 0) // 4) % 2
    out_ref[...] = jnp.where(kind == 0, total[:, :HEAD], total[:, HEAD:]).astype(bf16)


def weigh(y_lo, u, pieces):
    vmem = pl.BlockSpec(memory_space=pltpu.VMEM)
    smem = pl.BlockSpec(memory_space=pltpu.SMEM)
    anywhere = pl.BlockSpec(memory_space=pl.ANY)
    return pl.pallas_call(
        weigh_body,
        out_shape=jax.ShapeDtypeStruct((16, HEAD), bf16),
        in_specs=[smem, vmem, anywhere, anywhere, anywhere],
        out_specs=vmem,
        scratch_shapes=[
            pltpu.VMEM((Y_LO, Z, X, 32, 256), bf16),
            pltpu.SemaphoreType.DMA((2 * X,)),
        ],
        compiler_params=pltpu.CompilerParams(vmem_limit_bytes=40 << 20),
        name="weigh",
    )(y_lo, u, *pieces)


def local(
    hidden, lengths, list_ids, list_owner, attn_gain, final_gain, w_query, w_key, w_value, w_out
):
    _, seq_len, width = hidden.shape
    dp, fsdp = lax.axis_index("dp"), lax.axis_index("fsdp")
    core, x = dp % 2, (dp // 2) % X
    y_lo = fsdp // Z
    last = lengths[0] - 1

    w_query_other = lax.ppermute(w_query, "fsdp", Y_LO_SWAP)
    last_input = lax.dynamic_slice(hidden, (0, last, 0), (1, 1, width))[0]

    def norm(rows):
        floats = rows.astype(f32)
        return (
            floats * lax.rsqrt(jnp.mean(floats * floats, axis=-1, keepdims=True) + 1e-05) * attn_gain
        ).astype(bf16)

    last_normed = norm(last_input)
    halves = last_normed.reshape(Y_LO, Z, HEAD)
    halves = jnp.where(y_lo == 0, halves, halves[::-1])
    features = jnp.transpose(halves, (1, 0, 2)).reshape(Z, 1, 2 * HEAD)

    units = jnp.concatenate(
        [lax.dynamic_slice(w, (x * 32, core * 256), (32, 256)) for w in (w_key, w_value)], axis=0
    )
    outgoing = jnp.concatenate(
        [
            jnp.broadcast_to(units, (Z, 64, 256)),
            jnp.broadcast_to(features, (Z, 16, 256)),
        ],
        axis=1,
    )
    arrived = lax.all_to_all(outgoing, "fsdp", 0, 0, tiled=True, axis_index_groups=Z_GROUPS)
    key_piece, value_piece, rows = arrived[:, :32], arrived[:, 32:64], arrived[:, 64]

    query_parts = jnp.dot(rows[:, :HEAD], w_query, preferred_element_type=f32) + jnp.dot(
        rows[:, HEAD:], w_query_other, preferred_element_type=f32
    )
    query_sum = jnp.sum(
        lax.all_to_all(
            query_parts.reshape(Z, HEADS, HEAD), "fsdp", 0, 0, tiled=True, axis_index_groups=Z_GROUPS
        ),
        axis=0,
    )
    query_cos, query_sin = rope_tables(last[None], HEAD)
    turned = query_sum * query_cos + jnp.roll(query_sum, HEAD // 2, axis=1) * query_sin
    queries = (turned * (1.0 / math.sqrt(HEAD))).astype(bf16).reshape(2, 8, HEAD)
    mine = lax.dynamic_index_in_dim(queries, core, 0, keepdims=False)
    give = jnp.concatenate(
        [
            lax.dynamic_index_in_dim(queries, 1 - core, 0, keepdims=False),
            jnp.broadcast_to(lengths.astype(bf16)[:, None], (8, HEAD)),
        ],
        axis=0,
    )
    got = lax.ppermute(give, "dp", CORE_SWAP)
    both_queries = jnp.stack([mine, got[:8]]).reshape(2, 2, 4, HEAD)
    both_queries = jnp.concatenate([both_queries, both_queries], axis=2)
    both_lengths = jnp.concatenate([lengths, got[8, :1].astype(jnp.int32)])

    normed = norm(hidden[0])
    other = lax.ppermute(normed, "dp", CORE_SWAP)
    key_pieces = plane_gather(key_piece, x)
    value_pieces = plane_gather(value_piece, x)
    cosine, sine = rope_tables(jnp.arange(seq_len), HEAD)
    y_lo_one = y_lo[None].astype(jnp.int32)
    u = attend(y_lo_one, both_lengths, normed, other, both_queries, cosine, sine, key_pieces)
    context = weigh(y_lo_one, u, value_pieces)
    swapped = lax.ppermute(context[8:], "dp", CORE_SWAP)
    halves = (context[:8], swapped)
    context = jnp.where(
        core == 0, jnp.concatenate(halves, axis=0), jnp.concatenate(halves[::-1], axis=0)
    ).reshape(1, HEADS * HEAD)

    slabs = width // HEAD
    columns = jnp.transpose(w_out.reshape(-1, slabs, HEAD), (1, 0, 2))
    columns = jnp.concatenate(
        [columns, jnp.broadcast_to(last_input.reshape(slabs, 1, HEAD), (slabs, 16, HEAD))], axis=1
    )
    columns = lax.all_to_all(columns, "fsdp", 0, 0, tiled=True)
    out_weight = columns[:, :-16].reshape(HEADS * HEAD, HEAD)
    slab_input = columns[:, -16].astype(f32)

    contexts = lax.all_to_all(
        jnp.broadcast_to(context.reshape(1, HEADS, HEAD), (slabs, HEADS, HEAD)), "fsdp", 0, 0, tiled=True
    ).reshape(slabs, HEADS * HEAD)
    residual = slab_input + jnp.dot(contexts, out_weight, preferred_element_type=f32)
    gain = lax.dynamic_slice(final_gain, (fsdp * HEAD,), (HEAD,))
    scaled = residual * gain
    partial = jnp.sum(scaled * scaled, axis=-1)
    squares = lax.all_to_all(
        jnp.broadcast_to(partial[None, None, :], (slabs, 1, slabs)), "fsdp", 0, 0, tiled=True
    )
    mean = jnp.sum(squares, axis=0)[0] / width
    slab = (scaled * lax.rsqrt(mean + 1e-06)[:, None]).astype(bf16)

    owner_count = lax.axis_size("dp")
    capacity = 4
    list_index = jnp.arange(list_owner.shape[0])
    owners = jnp.sum(
        jnp.where(list_ids[:, None] == list_index[None, :], list_owner[None, :], 0), axis=1
    )
    owner_marks = (owners[:, None] == jnp.arange(owner_count)[None, :]).astype(jnp.int32)
    slot_rank = jnp.sum((jnp.cumsum(owner_marks, axis=0) - owner_marks) * owner_marks, axis=1)
    select = (
        (owners[None, None, :] == jnp.arange(owner_count)[:, None, None])
        & (slot_rank[None, None, :] == jnp.arange(capacity)[None, :, None])
    ).astype(bf16)
    outgoing = jnp.einsum("osr,rd->osd", select, slab, preferred_element_type=f32).astype(bf16)
    return lax.all_to_all(outgoing[:, None], "dp", split_axis=0, concat_axis=1, tiled=True)


def solution(mesh):
    in_specs = (
        P(("dp", "fsdp"), None, None),
        P(("dp", "fsdp")),
        P("dp"),
        P(),
        P(),
        P(),
        P("fsdp", None),
        P("fsdp", None),
        P("fsdp", None),
        P("fsdp", None),
    )
    out_specs = P("dp", None, None, "fsdp")
    return jax.shard_map(local, mesh=mesh, in_specs=in_specs, out_specs=out_specs, check_vma=False)
```

```python
import math

import jax
import jax.numpy as jnp
from jax import lax
from jax.experimental import pallas as pl
from jax.experimental.pallas import tpu as pltpu
from jax.sharding import PartitionSpec as P

HEADS = 16
KV_HEADS = 4
HEAD = 128
X = 4
Y_LO = 2
Z = 16
BOTH = ("dp", "fsdp")

bf16 = jnp.bfloat16
f32 = jnp.float32
VMEM = pl.BlockSpec(memory_space=pltpu.VMEM)
SMEM = pl.BlockSpec(memory_space=pltpu.SMEM)
HBM = pl.BlockSpec(memory_space=pltpu.HBM)


def dp_index(y_hi, x, core):
    return (y_hi * X + x) * 2 + core


def fsdp_index(y_lo, z):
    return y_lo * Z + z


Z_GROUPS = [[fsdp_index(yl, z) for z in range(Z)] for yl in range(Y_LO)]
CORE_Z_GROUPS = [
    [dp_index(yh, x, c) * 32 + fsdp_index(yl, z) for c in range(2) for z in range(Z)]
    for yh in range(2)
    for x in range(X)
    for yl in range(Y_LO)
]
CROSS_SWAP = [
    (
        dp_index(yh, x, c) * 32 + fsdp_index(1 - c, z),
        dp_index(yh, x, 1 - c) * 32 + fsdp_index(c, z),
    )
    for yh in range(2)
    for x in range(X)
    for c in range(2)
    for z in range(Z)
]
CORE_SWAP = [(d, d ^ 1) for d in range(16)]
Y_LO_SWAP = [(i, i ^ Z) for i in range(32)]


def x_shift(step):
    return [
        (dp_index(yh, x, c), dp_index(yh, (x + step) % X, c))
        for yh in range(2)
        for x in range(X)
        for c in range(2)
    ]


def y_shift(step):
    pairs = []
    for y in range(4):
        to = (y + step) % 4
        for x in range(X):
            for z in range(Z):
                for c in range(2):
                    pairs.append(
                        (
                            dp_index(y // 2, x, c) * 32 + fsdp_index(y % 2, z),
                            dp_index(to // 2, x, c) * 32 + fsdp_index(to % 2, z),
                        )
                    )
    return pairs


def rope_tables(positions, head_width):
    halfway = head_width // 2
    frequency = 10000.0 ** (-jnp.arange(halfway, dtype=f32) * 2.0 / head_width)
    angles = positions.astype(f32)[..., None] * frequency
    cosine, sine = jnp.cos(angles), jnp.sin(angles)
    return (
        jnp.concatenate([cosine, cosine], axis=-1),
        jnp.concatenate([-sine, sine], axis=-1),
    )


PIECE = 136


def open_body(place_ref, hidden, gain_ref, w_key, w_value, out_ref, last_ref, block, keys, values, sem):
    last, x, core, y_lo = place_ref[0], place_ref[1], place_ref[2], place_ref[3]
    first = pl.multiple_of((last >> 3) << 3, 8)
    rows = pl.ds(pl.multiple_of(x * 32, 32), 32)
    columns = pl.ds(pl.multiple_of(core * 256, 256), 256)
    copies = [
        pltpu.make_async_copy(hidden.at[0, pl.ds(first, 8)], block, sem.at[0]),
        pltpu.make_async_copy(w_key.at[rows, columns], keys, sem.at[1]),
        pltpu.make_async_copy(w_value.at[rows, columns], values, sem.at[2]),
    ]
    for copy in copies:
        copy.start()
    copies[0].wait()
    floats = block[...].astype(f32)
    pick = lax.broadcasted_iota(jnp.int32, floats.shape, 0) == (last & 7)
    row = jnp.sum(jnp.where(pick, floats, 0.0), axis=0, keepdims=True)
    last_ref[...] = row.astype(bf16)
    normed = row * lax.rsqrt(jnp.mean(row * row, axis=-1, keepdims=True) + 1e-05) * gain_ref[...]
    normed = normed.astype(bf16).astype(f32)
    half = normed.shape[1] // 2
    place = lax.broadcasted_iota(jnp.int32, (8, HEAD), 0)
    copies[1].wait()
    copies[2].wait()
    unit = jnp.concatenate(
        [w[:, g * HEAD : (g + 1) * HEAD] for w in (keys[...], values[...]) for g in range(2)], axis=0
    )
    for z in range(Z):
        low = normed[:, z * HEAD : (z + 1) * HEAD]
        high = normed[:, half + z * HEAD : half + (z + 1) * HEAD]
        mine = jnp.where(y_lo == 0, low, high)
        other = jnp.where(y_lo == 0, high, low)
        tile = jnp.where(place == 0, mine, jnp.where(place == 1, other, 0.0))
        out_ref[z, :128, :] = unit
        out_ref[z, 128:, :] = tile.astype(bf16)


def open_payload(place, hidden, gain, w_key, w_value):
    width = hidden.shape[2]
    return pl.pallas_call(
        open_body,
        out_shape=(
            jax.ShapeDtypeStruct((Z, PIECE, HEAD), bf16),
            jax.ShapeDtypeStruct((1, width), bf16),
        ),
        in_specs=[SMEM, HBM, VMEM, HBM, HBM],
        out_specs=(VMEM, VMEM),
        scratch_shapes=[
            pltpu.VMEM((8, width), bf16),
            pltpu.VMEM((32, 256), bf16),
            pltpu.VMEM((32, 256), bf16),
            pltpu.SemaphoreType.DMA((3,)),
        ],
        compiler_params=pltpu.CompilerParams(vmem_limit_bytes=8 << 20),
        name="open",
    )(place, hidden, gain[None, :], w_key, w_value)


ROWS = 56
QUERY_ROW = 32
HIDDEN_ROW = 48


def fill_body(place_ref, w_out_ref, near_ref, far_ref, out_ref):
    core, y_lo = place_ref[2], place_ref[3]
    weight = w_out_ref[...].astype(f32)
    weight = jnp.where(core == 0, weight[:32], weight[32:]).astype(bf16)
    row = lax.broadcasted_iota(jnp.int32, (8, HEAD), 0)
    half = Z * HEAD
    near, far = (
        jnp.where(y_lo == 0, rows[:, :half], rows[:, half:])
        for rows in (near_ref[...].astype(f32), far_ref[...].astype(f32))
    )
    zeros = jnp.zeros((HIDDEN_ROW - QUERY_ROW, HEAD), bf16)
    for z in range(Z):
        cut = slice(z * HEAD, (z + 1) * HEAD)
        tile = jnp.where(row == 0, near[:, cut], jnp.where(row == 1, far[:, cut], 0.0)).astype(bf16)
        for c in range(2):
            n = c * Z + z
            out_ref[n, :QUERY_ROW, :] = weight[:, n * HEAD : (n + 1) * HEAD]
            out_ref[n, QUERY_ROW:HIDDEN_ROW, :] = zeros
            out_ref[n, HIDDEN_ROW:, :] = tile


def fill_payload(place, w_out, near, far):
    return pl.pallas_call(
        fill_body,
        out_shape=jax.ShapeDtypeStruct((2 * Z, ROWS, HEAD), bf16),
        in_specs=[SMEM, VMEM, VMEM, VMEM],
        out_specs=VMEM,
        compiler_params=pltpu.CompilerParams(vmem_limit_bytes=8 << 20),
        name="fill",
    )(place, w_out, near, far)


def query_body(arrived, near_ref, far_ref, payload, out, tile, parts, sent, sem):
    copy = pltpu.make_async_copy(arrived.at[:, pl.ds(128, 8), :], tile, sem.at[0])
    copy.start()
    copy.wait()
    features = tile[...].astype(f32)
    total = jnp.dot(
        features[:, 0, :].astype(bf16), near_ref[...], preferred_element_type=f32
    ) + jnp.dot(features[:, 1, :].astype(bf16), far_ref[...], preferred_element_type=f32)
    high = total.astype(bf16).astype(f32)
    low = total - high
    for h in range(HEADS):
        c, cut = h // 8, slice(h * HEAD, (h + 1) * HEAD)
        parts[c * Z : (c + 1) * Z, h % 8, :] = high[:, cut]
        parts[c * Z : (c + 1) * Z, 8 + h % 8, :] = low[:, cut]
    sent[...] = parts[...].astype(bf16)
    back = pltpu.make_async_copy(sent, out.at[:, pl.ds(QUERY_ROW, 16), :], sem.at[1])
    back.start()
    back.wait()


def query_payload(arrived, near, far, payload):
    return pl.pallas_call(
        query_body,
        out_shape=jax.ShapeDtypeStruct(payload.shape, bf16),
        in_specs=[HBM, VMEM, VMEM, HBM],
        out_specs=HBM,
        input_output_aliases={3: 0},
        scratch_shapes=[
            pltpu.VMEM((Z, 8, HEAD), bf16),
            pltpu.VMEM((2 * Z, 16, HEAD), f32),
            pltpu.VMEM((2 * Z, 16, HEAD), bf16),
            pltpu.SemaphoreType.DMA((2,)),
        ],
        compiler_params=pltpu.CompilerParams(vmem_limit_bytes=8 << 20),
        name="query",
    )(arrived, near, far, payload)


def attend_body(place_ref, len_ref, normed, other, cos_ref, sin_ref, parts, *refs):
    pieces, (out_ref, w_ref, q_ref, rows_ref, sem, q_sem) = refs[:8], refs[8:]
    fetch = pltpu.make_async_copy(parts.at[:, pl.ds(QUERY_ROW, 16), :], q_ref, q_sem.at[0])
    fetch.start()
    fills = [
        pltpu.make_async_copy(rows, rows_ref.at[p], q_sem.at[1 + p])
        for p, rows in enumerate((normed, other))
    ]
    x, core, y_lo = place_ref[1], place_ref[2], place_ref[3]
    copies = [[], []]
    for kind in range(2):
        for n, piece in enumerate(pieces):
            row = y_lo if n < X else 1 - y_lo
            column = (x + X - n % X) & (X - 1)
            for g in range(2):
                copies[kind].append(
                    pltpu.make_async_copy(
                        piece.at[:, pl.ds((kind * 2 + g) * 32, 32), :],
                        w_ref.at[kind, row, :, column, :, pl.ds(g * HEAD, HEAD)],
                        sem.at[kind, n, g],
                    )
                )
    for copy in fills[:1] + copies[0] + fills[1:] + copies[1]:
        copy.start()
    cosine, sine = cos_ref[...], sin_ref[...]
    fetch.wait()
    by_core = [jnp.sum(q_ref[c * Z : (c + 1) * Z].astype(f32), axis=0) for c in range(2)]
    by_core = [both[:8] + both[8:] for both in by_core]
    queries = []
    for p in range(2):
        summed = jnp.where(core == p, by_core[0], by_core[1])
        last = len_ref[p] - 1
        turned = summed * cos_ref[pl.ds(last, 1), :] + pltpu.roll(summed, HEAD // 2, 1) * sin_ref[
            pl.ds(last, 1), :
        ]
        queries.append((turned * (1.0 / math.sqrt(HEAD))).astype(bf16))
    for copy in copies[0]:
        copy.wait()
    weight = w_ref[0].reshape(Y_LO * Z * X * 32, 256)
    sums = []
    for p in range(2):
        fills[p].wait()
        rows = rows_ref[p]
        keys = jnp.dot(rows, weight, preferred_element_type=f32)
        scores = []
        for g in range(2):
            part = keys[:, g * HEAD : (g + 1) * HEAD]
            turned = (part * cosine + pltpu.roll(part, HEAD // 2, 1) * sine).astype(bf16)
            scores.append(
                lax.dot_general(
                    queries[p], turned, (((1,), (1,)), ((), ())), preferred_element_type=f32
                )
            )
        head = lax.broadcasted_iota(jnp.int32, scores[0].shape, 0)
        place = lax.broadcasted_iota(jnp.int32, scores[0].shape, 1)
        scores = jnp.where(head < 4, scores[0], scores[1])
        scores = jnp.where(place < len_ref[p], scores, -jnp.inf)
        powers = jnp.exp(scores - jnp.max(scores, axis=-1, keepdims=True))
        weights = (powers / jnp.sum(powers, axis=-1, keepdims=True)).astype(bf16)
        sums.append(jnp.dot(weights, rows, preferred_element_type=f32))
    u = jnp.concatenate(sums, axis=0)
    first = u.astype(bf16)
    rest = u - first.astype(f32)
    second = rest.astype(bf16)
    third = (rest - second.astype(f32)).astype(bf16)
    for copy in copies[1]:
        copy.wait()
    weight = w_ref[1].reshape(Y_LO * Z * X * 32, 256)
    parts = [jnp.dot(t, weight, preferred_element_type=f32) for t in (third, second, first)]
    total = parts[0] + parts[1] + parts[2]
    head = lax.broadcasted_iota(jnp.int32, (16, HEAD), 0)
    context = jnp.where((head & 7) < 4, total[:, :HEAD], total[:, HEAD:])
    turned = jnp.concatenate([context[8:], context[:8]], axis=0)
    context = jnp.where(core == 0, context, turned).astype(bf16)
    out_ref[...] = jnp.broadcast_to(context[None], out_ref.shape)


def attend(place, lengths, normed, other, cosine, sine, parts, pieces):
    return pl.pallas_call(
        attend_body,
        out_shape=jax.ShapeDtypeStruct((2 * Z, 16, HEAD), bf16),
        in_specs=[SMEM, SMEM, HBM, HBM, VMEM, VMEM] + [HBM] * 9,
        out_specs=VMEM,
        scratch_shapes=[
            pltpu.VMEM((2, Y_LO, Z, X, 32, 256), bf16),
            pltpu.VMEM((2 * Z, 16, HEAD), bf16),
            pltpu.VMEM((2, *normed.shape), bf16),
            pltpu.SemaphoreType.DMA((2, 8, 2)),
            pltpu.SemaphoreType.DMA((3,)),
        ],
        compiler_params=pltpu.CompilerParams(vmem_limit_bytes=60 << 20),
        name="attend",
    )(place, lengths, normed, other, cosine, sine, parts, *pieces)


def local(
    hidden, lengths, list_ids, list_owner, attn_gain, final_gain, w_query, w_key, w_value, w_out
):
    _, seq_len, width = hidden.shape
    dp, fsdp = lax.axis_index("dp"), lax.axis_index("fsdp")
    core, x = dp & 1, (dp >> 1) & (X - 1)
    y_lo = fsdp >> 4
    place = jnp.stack([lengths[0] - 1, x, core, y_lo]).astype(jnp.int32)

    outgoing, last_input = open_payload(place, hidden, attn_gain, w_key, w_value)

    w_query_other = lax.ppermute(w_query, "fsdp", Y_LO_SWAP)
    both_lengths = jnp.concatenate([lengths, lax.ppermute(lengths, "dp", CORE_SWAP)])
    rows, outgoing = lax.optimization_barrier((hidden[0], outgoing))
    arrived = lax.all_to_all(outgoing, "fsdp", 0, 0, tiled=True, axis_index_groups=Z_GROUPS)
    floats = rows.astype(f32)
    normed = (
        floats * lax.rsqrt(jnp.mean(floats * floats, axis=-1, keepdims=True) + 1e-05) * attn_gain
    ).astype(bf16)
    other = lax.ppermute(normed, "dp", CORE_SWAP)
    cosine, sine = rope_tables(jnp.arange(seq_len), HEAD)
    last_other = lax.ppermute(last_input, "fsdp", Y_LO_SWAP)
    payload = fill_payload(place, w_out, last_input, last_other)
    arrived, w_query_other, other, both_lengths, cosine, sine, payload = lax.optimization_barrier(
        (arrived, w_query_other, other, both_lengths, cosine, sine, payload)
    )

    plus = lax.ppermute(arrived, "dp", x_shift(1))
    minus = lax.ppermute(arrived, "dp", x_shift(-1))
    far = lax.ppermute(arrived, "dp", x_shift(2))
    y_own = lax.ppermute(arrived, BOTH, y_shift(-1))

    w_query_other, plus, minus = lax.optimization_barrier((w_query_other, plus, minus))
    payload = query_payload(arrived, w_query, w_query_other, payload)
    parts = lax.all_to_all(payload, BOTH, 0, 0, tiled=True, axis_index_groups=CORE_Z_GROUPS)

    plus, minus, far, y_own = lax.optimization_barrier((plus, minus, far, y_own))
    y_plus = lax.ppermute(plus, BOTH, y_shift(1))
    y_minus = lax.ppermute(minus, BOTH, y_shift(-1))
    y_far = lax.ppermute(far, BOTH, y_shift(1))

    pieces = (arrived, plus, far, minus, y_own, y_plus, y_far, y_minus)
    context = attend(place, both_lengths, normed, other, cosine, sine, parts, pieces)
    contexts = lax.all_to_all(context, "fsdp", 0, 0, tiled=True)

    weight = jnp.transpose(parts[:, :QUERY_ROW].reshape(2, Z, 32, HEAD), (1, 0, 2, 3))
    weight = weight.reshape(2 * Z * 32, HEAD)
    weight = jnp.where(core == y_lo, weight, lax.ppermute(weight, BOTH, CROSS_SWAP))
    inputs = lax.dynamic_slice(parts, (core * Z, HIDDEN_ROW, 0), (Z, 2, HEAD)).astype(f32)
    inputs = jnp.where(y_lo == 0, inputs, inputs[:, ::-1])
    inputs = jnp.transpose(inputs, (1, 0, 2)).reshape(2 * Z, HEAD)

    slabs = width // HEAD
    contexts = contexts.reshape(slabs, 2, 8 * HEAD)
    halves = jnp.einsum("sad,dn->asn", contexts, weight, preferred_element_type=f32)
    kept = lax.dynamic_index_in_dim(halves, core, 0, keepdims=False)
    given = lax.dynamic_index_in_dim(halves, 1 - core, 0, keepdims=False)
    residual = inputs + (kept + lax.ppermute(given, "dp", CORE_SWAP))
    gain = lax.dynamic_slice(final_gain, (fsdp * HEAD,), (HEAD,))
    scaled = residual * gain
    partial = jnp.sum(scaled * scaled, axis=-1)
    squares = lax.all_to_all(
        jnp.broadcast_to(partial[None, None, :], (slabs, 1, slabs)), "fsdp", 0, 0, tiled=True
    )
    mean = jnp.sum(squares, axis=0)[0] / width
    slab = (scaled * lax.rsqrt(mean + 1e-06)[:, None]).astype(bf16)

    owner_count = lax.axis_size("dp")
    capacity = 4
    list_index = jnp.arange(list_owner.shape[0])
    owners = jnp.sum(
        jnp.where(list_ids[:, None] == list_index[None, :], list_owner[None, :], 0), axis=1
    )
    owner_marks = (owners[:, None] == jnp.arange(owner_count)[None, :]).astype(jnp.int32)
    slot_rank = jnp.sum((jnp.cumsum(owner_marks, axis=0) - owner_marks) * owner_marks, axis=1)
    select = (
        (owners[None, None, :] == jnp.arange(owner_count)[:, None, None])
        & (slot_rank[None, None, :] == jnp.arange(capacity)[None, :, None])
    ).astype(bf16)
    outgoing = jnp.einsum("osr,rd->osd", select, slab, preferred_element_type=f32).astype(bf16)
    return lax.all_to_all(outgoing[:, None], "dp", split_axis=0, concat_axis=1, tiled=True)


def solution(mesh):
    in_specs = (
        P(("dp", "fsdp"), None, None),
        P(("dp", "fsdp")),
        P("dp"),
        P(),
        P(),
        P(),
        P("fsdp", None),
        P("fsdp", None),
        P("fsdp", None),
        P("fsdp", None),
    )
    out_specs = P("dp", None, None, "fsdp")
    return jax.shard_map(local, mesh=mesh, in_specs=in_specs, out_specs=out_specs, check_vma=False)
```

```python
import math

import jax
import jax.numpy as jnp
from jax import lax
from jax.experimental import pallas as pl
from jax.experimental.pallas import tpu as pltpu
from jax.sharding import PartitionSpec as P

HEADS = 16
KV_HEADS = 4
HEAD = 128
X = 4
Y_LO = 2
Z = 16
BOTH = ("dp", "fsdp")

bf16 = jnp.bfloat16
f32 = jnp.float32
VMEM = pl.BlockSpec(memory_space=pltpu.VMEM)
SMEM = pl.BlockSpec(memory_space=pltpu.SMEM)
HBM = pl.BlockSpec(memory_space=pltpu.HBM)


def dp_index(y_hi, x, core):
    return (y_hi * X + x) * 2 + core


def fsdp_index(y_lo, z):
    return y_lo * Z + z


Z_GROUPS = [[fsdp_index(yl, z) for z in range(Z)] for yl in range(Y_LO)]
CORE_Z_GROUPS = [
    [dp_index(yh, x, c) * 32 + fsdp_index(yl, z) for c in range(2) for z in range(Z)]
    for yh in range(2)
    for x in range(X)
    for yl in range(Y_LO)
]
CROSS_SWAP = [
    (
        dp_index(yh, x, c) * 32 + fsdp_index(1 - c, z),
        dp_index(yh, x, 1 - c) * 32 + fsdp_index(c, z),
    )
    for yh in range(2)
    for x in range(X)
    for c in range(2)
    for z in range(Z)
]
CORE_SWAP = [(d, d ^ 1) for d in range(16)]
Y_LO_SWAP = [(i, i ^ Z) for i in range(32)]


def rope_tables(positions, head_width):
    halfway = head_width // 2
    frequency = 10000.0 ** (-jnp.arange(halfway, dtype=f32) * 2.0 / head_width)
    angles = positions.astype(f32)[..., None] * frequency
    cosine, sine = jnp.cos(angles), jnp.sin(angles)
    return (
        jnp.concatenate([cosine, cosine], axis=-1),
        jnp.concatenate([-sine, sine], axis=-1),
    )


def unit_body(place_ref, w_key, w_value, out, sem):
    columns = pl.ds(pl.multiple_of(place_ref[2] * 256, 256), 256)
    copies = [
        pltpu.make_async_copy(w.at[:, columns], out.at[:, pl.ds(k * 256, 256)], sem.at[k])
        for k, w in enumerate((w_key, w_value))
    ]
    for copy in copies:
        copy.start()
    for copy in copies:
        copy.wait()


def core_unit(place, w_key, w_value):
    return pl.pallas_call(
        unit_body,
        out_shape=jax.ShapeDtypeStruct((w_key.shape[0], 512), bf16),
        in_specs=[SMEM, HBM, HBM],
        out_specs=HBM,
        scratch_shapes=[pltpu.SemaphoreType.DMA((2,))],
        compiler_params=pltpu.CompilerParams(vmem_limit_bytes=1 << 20),
        name="unit",
    )(place, w_key, w_value)


def pair_body(near, far, out, sem):
    copies = [pltpu.make_async_copy(rows, out.at[k], sem.at[k]) for k, rows in enumerate((near, far))]
    for copy in copies:
        copy.start()
    for copy in copies:
        copy.wait()


def pair(near, far):
    return pl.pallas_call(
        pair_body,
        out_shape=jax.ShapeDtypeStruct((2, *near.shape), bf16),
        in_specs=[HBM, HBM],
        out_specs=HBM,
        scratch_shapes=[pltpu.SemaphoreType.DMA((2,))],
        compiler_params=pltpu.CompilerParams(vmem_limit_bytes=1 << 20),
        name="pair",
    )(near, far)


def open_body(place_ref, hidden, gain_ref, out_ref, last_ref, block, sem):
    last, y_lo = place_ref[0], place_ref[3]
    first = pl.multiple_of((last >> 3) << 3, 8)
    copy = pltpu.make_async_copy(hidden.at[0, pl.ds(first, 8)], block, sem.at[0])
    copy.start()
    copy.wait()
    floats = block[...].astype(f32)
    pick = lax.broadcasted_iota(jnp.int32, floats.shape, 0) == (last & 7)
    row = jnp.sum(jnp.where(pick, floats, 0.0), axis=0, keepdims=True)
    last_ref[...] = row.astype(bf16)
    normed = row * lax.rsqrt(jnp.mean(row * row, axis=-1, keepdims=True) + 1e-05) * gain_ref[...]
    normed = normed.astype(bf16).astype(f32)
    half = normed.shape[1] // 2
    place = lax.broadcasted_iota(jnp.int32, (8, HEAD), 0)
    for z in range(Z):
        low = normed[:, z * HEAD : (z + 1) * HEAD]
        high = normed[:, half + z * HEAD : half + (z + 1) * HEAD]
        mine = jnp.where(y_lo == 0, low, high)
        other = jnp.where(y_lo == 0, high, low)
        tile = jnp.where(place == 0, mine, jnp.where(place == 1, other, 0.0))
        out_ref[z] = tile.astype(bf16)


def open_payload(place, hidden, gain):
    width = hidden.shape[2]
    return pl.pallas_call(
        open_body,
        out_shape=(
            jax.ShapeDtypeStruct((Z, 8, HEAD), bf16),
            jax.ShapeDtypeStruct((1, width), bf16),
        ),
        in_specs=[SMEM, HBM, VMEM],
        out_specs=(VMEM, VMEM),
        scratch_shapes=[pltpu.VMEM((8, width), bf16), pltpu.SemaphoreType.DMA((1,))],
        compiler_params=pltpu.CompilerParams(vmem_limit_bytes=4 << 20),
        name="open",
    )(place, hidden, gain[None, :])


ROWS = 56
QUERY_ROW = 32
HIDDEN_ROW = 48


def fill_body(place_ref, w_out_ref, near_ref, far_ref, out_ref):
    core, y_lo = place_ref[2], place_ref[3]
    weight = w_out_ref[...].astype(f32)
    weight = jnp.where(core == 0, weight[:32], weight[32:]).astype(bf16)
    row = lax.broadcasted_iota(jnp.int32, (8, HEAD), 0)
    half = Z * HEAD
    near, far = (
        jnp.where(y_lo == 0, rows[:, :half], rows[:, half:])
        for rows in (near_ref[...].astype(f32), far_ref[...].astype(f32))
    )
    zeros = jnp.zeros((HIDDEN_ROW - QUERY_ROW, HEAD), bf16)
    for z in range(Z):
        cut = slice(z * HEAD, (z + 1) * HEAD)
        tile = jnp.where(row == 0, near[:, cut], jnp.where(row == 1, far[:, cut], 0.0)).astype(bf16)
        for c in range(2):
            n = c * Z + z
            out_ref[n, :QUERY_ROW, :] = weight[:, n * HEAD : (n + 1) * HEAD]
            out_ref[n, QUERY_ROW:HIDDEN_ROW, :] = zeros
            out_ref[n, HIDDEN_ROW:, :] = tile


def fill_payload(place, w_out, near, far):
    return pl.pallas_call(
        fill_body,
        out_shape=jax.ShapeDtypeStruct((2 * Z, ROWS, HEAD), bf16),
        in_specs=[SMEM, VMEM, VMEM, VMEM],
        out_specs=VMEM,
        compiler_params=pltpu.CompilerParams(vmem_limit_bytes=8 << 20),
        name="fill",
    )(place, w_out, near, far)


def query_body(arrived_ref, near_ref, far_ref, payload, out, parts, sent, sem):
    features = arrived_ref[...].astype(f32)
    total = jnp.dot(
        features[:, 0, :].astype(bf16), near_ref[...], preferred_element_type=f32
    ) + jnp.dot(features[:, 1, :].astype(bf16), far_ref[...], preferred_element_type=f32)
    high = total.astype(bf16).astype(f32)
    low = total - high
    for h in range(HEADS):
        c, cut = h // 8, slice(h * HEAD, (h + 1) * HEAD)
        parts[c * Z : (c + 1) * Z, h % 8, :] = high[:, cut]
        parts[c * Z : (c + 1) * Z, 8 + h % 8, :] = low[:, cut]
    sent[...] = parts[...].astype(bf16)
    back = pltpu.make_async_copy(sent, out.at[:, pl.ds(QUERY_ROW, 16), :], sem.at[0])
    back.start()
    back.wait()


def query_payload(arrived, near, far, payload):
    return pl.pallas_call(
        query_body,
        out_shape=jax.ShapeDtypeStruct(payload.shape, bf16),
        in_specs=[VMEM, VMEM, VMEM, HBM],
        out_specs=HBM,
        input_output_aliases={3: 0},
        scratch_shapes=[
            pltpu.VMEM((2 * Z, 16, HEAD), f32),
            pltpu.VMEM((2 * Z, 16, HEAD), bf16),
            pltpu.SemaphoreType.DMA((1,)),
        ],
        compiler_params=pltpu.CompilerParams(vmem_limit_bytes=8 << 20),
        name="query",
    )(arrived, near, far, payload)


def attend_body(place_ref, len_ref, normed, other, cos_ref, sin_ref, parts, gathered, out_ref, w_ref, q_ref, rows_ref, sem, q_sem):
    fetch = pltpu.make_async_copy(parts.at[:, pl.ds(QUERY_ROW, 16), :], q_ref, q_sem.at[0])
    fetch.start()
    fills = [
        pltpu.make_async_copy(rows, rows_ref.at[p], q_sem.at[1 + p])
        for p, rows in enumerate((normed, other))
    ]
    core, y_lo = place_ref[2], place_ref[3]
    copies = [
        [
            pltpu.make_async_copy(
                gathered.at[:, n, :, pl.ds(kind * 256, 256)],
                w_ref.at[kind, y_lo if n == 0 else 1 - y_lo],
                sem.at[kind, n],
            )
            for n in range(2)
        ]
        for kind in range(2)
    ]
    for copy in fills[:1] + copies[0] + fills[1:] + copies[1]:
        copy.start()
    cosine, sine = cos_ref[...], sin_ref[...]
    fetch.wait()
    by_core = [jnp.sum(q_ref[c * Z : (c + 1) * Z].astype(f32), axis=0) for c in range(2)]
    by_core = [both[:8] + both[8:] for both in by_core]
    queries = []
    for p in range(2):
        summed = jnp.where(core == p, by_core[0], by_core[1])
        last = len_ref[p] - 1
        turned = summed * cos_ref[pl.ds(last, 1), :] + pltpu.roll(summed, HEAD // 2, 1) * sin_ref[
            pl.ds(last, 1), :
        ]
        queries.append((turned * (1.0 / math.sqrt(HEAD))).astype(bf16))
    for copy in copies[0]:
        copy.wait()
    weight = w_ref[0].reshape(Y_LO * Z * HEAD, 256)
    sums = []
    for p in range(2):
        fills[p].wait()
        rows = rows_ref[p]
        keys = jnp.dot(rows, weight, preferred_element_type=f32)
        scores = []
        for g in range(2):
            part = keys[:, g * HEAD : (g + 1) * HEAD]
            turned = (part * cosine + pltpu.roll(part, HEAD // 2, 1) * sine).astype(bf16)
            scores.append(
                lax.dot_general(
                    queries[p], turned, (((1,), (1,)), ((), ())), preferred_element_type=f32
                )
            )
        head = lax.broadcasted_iota(jnp.int32, scores[0].shape, 0)
        place = lax.broadcasted_iota(jnp.int32, scores[0].shape, 1)
        scores = jnp.where(head < 4, scores[0], scores[1])
        scores = jnp.where(place < len_ref[p], scores, -jnp.inf)
        powers = jnp.exp(scores - jnp.max(scores, axis=-1, keepdims=True))
        weights = (powers / jnp.sum(powers, axis=-1, keepdims=True)).astype(bf16)
        sums.append(jnp.dot(weights, rows, preferred_element_type=f32))
    u = jnp.concatenate(sums, axis=0)
    first = u.astype(bf16)
    rest = u - first.astype(f32)
    second = rest.astype(bf16)
    third = (rest - second.astype(f32)).astype(bf16)
    for copy in copies[1]:
        copy.wait()
    weight = w_ref[1].reshape(Y_LO * Z * HEAD, 256)
    parts = [jnp.dot(t, weight, preferred_element_type=f32) for t in (third, second, first)]
    total = parts[0] + parts[1] + parts[2]
    head = lax.broadcasted_iota(jnp.int32, (16, HEAD), 0)
    context = jnp.where((head & 7) < 4, total[:, :HEAD], total[:, HEAD:])
    turned = jnp.concatenate([context[8:], context[:8]], axis=0)
    context = jnp.where(core == 0, context, turned).astype(bf16)
    out_ref[...] = jnp.broadcast_to(context[None], out_ref.shape)


def attend(place, lengths, normed, other, cosine, sine, parts, gathered):
    return pl.pallas_call(
        attend_body,
        out_shape=jax.ShapeDtypeStruct((2 * Z, 16, HEAD), bf16),
        in_specs=[SMEM, SMEM, HBM, HBM, VMEM, VMEM, HBM, HBM],
        out_specs=VMEM,
        scratch_shapes=[
            pltpu.VMEM((2, Y_LO, Z, HEAD, 256), bf16),
            pltpu.VMEM((2 * Z, 16, HEAD), bf16),
            pltpu.VMEM((2, *normed.shape), bf16),
            pltpu.SemaphoreType.DMA((2, 2)),
            pltpu.SemaphoreType.DMA((3,)),
        ],
        compiler_params=pltpu.CompilerParams(vmem_limit_bytes=60 << 20),
        name="attend",
    )(place, lengths, normed, other, cosine, sine, parts, gathered)


def local(
    hidden, lengths, list_ids, list_owner, attn_gain, final_gain, w_query, w_key, w_value, w_out
):
    _, seq_len, width = hidden.shape
    dp, fsdp = lax.axis_index("dp"), lax.axis_index("fsdp")
    core, x = dp & 1, (dp >> 1) & (X - 1)
    y_lo = fsdp >> 4
    place = jnp.stack([lengths[0] - 1, x, core, y_lo]).astype(jnp.int32)

    unit = core_unit(place, w_key, w_value)
    units = pair(unit, lax.ppermute(unit, "fsdp", Y_LO_SWAP))
    gathered = lax.all_gather(units, "fsdp", axis=0, tiled=False, axis_index_groups=Z_GROUPS)

    unit, hidden = lax.optimization_barrier((unit, hidden))
    outgoing, last_input = open_payload(place, hidden, attn_gain)
    units, outgoing = lax.optimization_barrier((units, outgoing))
    arrived = lax.all_to_all(outgoing, "fsdp", 0, 0, tiled=True, axis_index_groups=Z_GROUPS)

    w_query_other = lax.ppermute(w_query, "fsdp", Y_LO_SWAP)
    both_lengths = jnp.concatenate([lengths, lax.ppermute(lengths, "dp", CORE_SWAP)])
    last_other = lax.ppermute(last_input, "fsdp", Y_LO_SWAP)
    payload = fill_payload(place, w_out, last_input, last_other)

    payload = query_payload(arrived, w_query, w_query_other, payload)
    parts = lax.all_to_all(payload, BOTH, 0, 0, tiled=True, axis_index_groups=CORE_Z_GROUPS)

    rows, _ = lax.optimization_barrier((hidden[0], outgoing))
    floats = rows.astype(f32)
    normed = (
        floats * lax.rsqrt(jnp.mean(floats * floats, axis=-1, keepdims=True) + 1e-05) * attn_gain
    ).astype(bf16)
    other = lax.ppermute(normed, "dp", CORE_SWAP)
    cosine, sine = rope_tables(jnp.arange(seq_len), HEAD)
    context = attend(place, both_lengths, normed, other, cosine, sine, parts, gathered)
    contexts = lax.all_to_all(context, "fsdp", 0, 0, tiled=True)

    weight = jnp.transpose(parts[:, :QUERY_ROW].reshape(2, Z, 32, HEAD), (1, 0, 2, 3))
    weight = weight.reshape(2 * Z * 32, HEAD)
    weight = jnp.where(core == y_lo, weight, lax.ppermute(weight, BOTH, CROSS_SWAP))
    inputs = lax.dynamic_slice(parts, (core * Z, HIDDEN_ROW, 0), (Z, 2, HEAD)).astype(f32)
    inputs = jnp.where(y_lo == 0, inputs, inputs[:, ::-1])
    inputs = jnp.transpose(inputs, (1, 0, 2)).reshape(2 * Z, HEAD)

    slabs = width // HEAD
    contexts = contexts.reshape(slabs, 2, 8 * HEAD)
    halves = jnp.einsum("sad,dn->asn", contexts, weight, preferred_element_type=f32)
    kept = lax.dynamic_index_in_dim(halves, core, 0, keepdims=False)
    given = lax.dynamic_index_in_dim(halves, 1 - core, 0, keepdims=False)
    residual = inputs + (kept + lax.ppermute(given, "dp", CORE_SWAP))
    gain = lax.dynamic_slice(final_gain, (fsdp * HEAD,), (HEAD,))
    scaled = residual * gain
    partial = jnp.sum(scaled * scaled, axis=-1)
    squares = lax.all_to_all(
        jnp.broadcast_to(partial[None, None, :], (slabs, 1, slabs)), "fsdp", 0, 0, tiled=True
    )
    mean = jnp.sum(squares, axis=0)[0] / width
    slab = (scaled * lax.rsqrt(mean + 1e-06)[:, None]).astype(bf16)

    owner_count = lax.axis_size("dp")
    capacity = 4
    list_index = jnp.arange(list_owner.shape[0])
    owners = jnp.sum(
        jnp.where(list_ids[:, None] == list_index[None, :], list_owner[None, :], 0), axis=1
    )
    owner_marks = (owners[:, None] == jnp.arange(owner_count)[None, :]).astype(jnp.int32)
    slot_rank = jnp.sum((jnp.cumsum(owner_marks, axis=0) - owner_marks) * owner_marks, axis=1)
    select = (
        (owners[None, None, :] == jnp.arange(owner_count)[:, None, None])
        & (slot_rank[None, None, :] == jnp.arange(capacity)[None, :, None])
    ).astype(bf16)
    outgoing = jnp.einsum("osr,rd->osd", select, slab, preferred_element_type=f32).astype(bf16)
    return lax.all_to_all(outgoing[:, None], "dp", split_axis=0, concat_axis=1, tiled=True)


def solution(mesh):
    in_specs = (
        P(("dp", "fsdp"), None, None),
        P(("dp", "fsdp")),
        P("dp"),
        P(),
        P(),
        P(),
        P("fsdp", None),
        P("fsdp", None),
        P("fsdp", None),
        P("fsdp", None),
    )
    out_specs = P("dp", None, None, "fsdp")
    return jax.shard_map(local, mesh=mesh, in_specs=in_specs, out_specs=out_specs, check_vma=False)
```

```python
import math

import jax
import jax.numpy as jnp
from jax import lax
from jax.experimental import pallas as pl
from jax.experimental.pallas import tpu as pltpu
from jax.sharding import PartitionSpec as P

HEADS = 16
KV_HEADS = 4
HEAD = 128
X = 4
Y_LO = 2
Z = 16
BOTH = ("dp", "fsdp")

bf16 = jnp.bfloat16
f32 = jnp.float32
VMEM = pl.BlockSpec(memory_space=pltpu.VMEM)
SMEM = pl.BlockSpec(memory_space=pltpu.SMEM)
HBM = pl.BlockSpec(memory_space=pltpu.HBM)


def dp_index(y_hi, x, core):
    return (y_hi * X + x) * 2 + core


def fsdp_index(y_lo, z):
    return y_lo * Z + z


Z_GROUPS = [[fsdp_index(yl, z) for z in range(Z)] for yl in range(Y_LO)]
CORE_Z_GROUPS = [
    [dp_index(yh, x, c) * 32 + fsdp_index(yl, z) for c in range(2) for z in range(Z)]
    for yh in range(2)
    for x in range(X)
    for yl in range(Y_LO)
]
CROSS_SWAP = [
    (
        dp_index(yh, x, c) * 32 + fsdp_index(1 - c, z),
        dp_index(yh, x, 1 - c) * 32 + fsdp_index(c, z),
    )
    for yh in range(2)
    for x in range(X)
    for c in range(2)
    for z in range(Z)
]
CORE_SWAP = [(d, d ^ 1) for d in range(16)]
Y_LO_SWAP = [(i, i ^ Z) for i in range(32)]


def y_shift(step):
    pairs = []
    for y in range(4):
        to = (y + step) % 4
        for x in range(X):
            for z in range(Z):
                for c in range(2):
                    pairs.append(
                        (
                            dp_index(y // 2, x, c) * 32 + fsdp_index(y % 2, z),
                            dp_index(to // 2, x, c) * 32 + fsdp_index(to % 2, z),
                        )
                    )
    return pairs


def rope_tables(positions, head_width):
    halfway = head_width // 2
    frequency = 10000.0 ** (-jnp.arange(halfway, dtype=f32) * 2.0 / head_width)
    angles = positions.astype(f32)[..., None] * frequency
    cosine, sine = jnp.cos(angles), jnp.sin(angles)
    return (
        jnp.concatenate([cosine, cosine], axis=-1),
        jnp.concatenate([-sine, sine], axis=-1),
    )


def unit_body(place_ref, w_key, w_value, out, sem):
    columns = pl.ds(pl.multiple_of(place_ref[2] * 256, 256), 256)
    copies = [
        pltpu.make_async_copy(w.at[:, columns], out.at[:, pl.ds(k * 256, 256)], sem.at[k])
        for k, w in enumerate((w_key, w_value))
    ]
    for copy in copies:
        copy.start()
    for copy in copies:
        copy.wait()


def core_unit(place, w_key, w_value):
    return pl.pallas_call(
        unit_body,
        out_shape=jax.ShapeDtypeStruct((w_key.shape[0], 512), bf16),
        in_specs=[SMEM, HBM, HBM],
        out_specs=HBM,
        scratch_shapes=[pltpu.SemaphoreType.DMA((2,))],
        compiler_params=pltpu.CompilerParams(vmem_limit_bytes=1 << 20),
        name="unit",
    )(place, w_key, w_value)


def open_body(place_ref, hidden, gain_ref, out_ref, last_ref, block, sem):
    last, y_lo = place_ref[0], place_ref[3]
    first = pl.multiple_of((last >> 3) << 3, 8)
    copy = pltpu.make_async_copy(hidden.at[0, pl.ds(first, 8)], block, sem.at[0])
    copy.start()
    copy.wait()
    floats = block[...].astype(f32)
    pick = lax.broadcasted_iota(jnp.int32, floats.shape, 0) == (last & 7)
    row = jnp.sum(jnp.where(pick, floats, 0.0), axis=0, keepdims=True)
    last_ref[...] = row.astype(bf16)
    normed = row * lax.rsqrt(jnp.mean(row * row, axis=-1, keepdims=True) + 1e-05) * gain_ref[...]
    normed = normed.astype(bf16).astype(f32)
    half = normed.shape[1] // 2
    place = lax.broadcasted_iota(jnp.int32, (8, HEAD), 0)
    for z in range(Z):
        low = normed[:, z * HEAD : (z + 1) * HEAD]
        high = normed[:, half + z * HEAD : half + (z + 1) * HEAD]
        mine = jnp.where(y_lo == 0, low, high)
        other = jnp.where(y_lo == 0, high, low)
        tile = jnp.where(place == 0, mine, jnp.where(place == 1, other, 0.0))
        out_ref[z] = tile.astype(bf16)


def open_payload(place, hidden, gain):
    width = hidden.shape[2]
    return pl.pallas_call(
        open_body,
        out_shape=(
            jax.ShapeDtypeStruct((Z, 8, HEAD), bf16),
            jax.ShapeDtypeStruct((1, width), bf16),
        ),
        in_specs=[SMEM, HBM, VMEM],
        out_specs=(VMEM, VMEM),
        scratch_shapes=[pltpu.VMEM((8, width), bf16), pltpu.SemaphoreType.DMA((1,))],
        compiler_params=pltpu.CompilerParams(vmem_limit_bytes=4 << 20),
        name="open",
    )(place, hidden, gain[None, :])


ROWS = 56
QUERY_ROW = 32
HIDDEN_ROW = 48


def fill_body(place_ref, w_out_ref, near_ref, far_ref, out_ref):
    core, y_lo = place_ref[2], place_ref[3]
    weight = w_out_ref[...].astype(f32)
    weight = jnp.where(core == 0, weight[:32], weight[32:]).astype(bf16)
    row = lax.broadcasted_iota(jnp.int32, (8, HEAD), 0)
    half = Z * HEAD
    near, far = (
        jnp.where(y_lo == 0, rows[:, :half], rows[:, half:])
        for rows in (near_ref[...].astype(f32), far_ref[...].astype(f32))
    )
    zeros = jnp.zeros((HIDDEN_ROW - QUERY_ROW, HEAD), bf16)
    for z in range(Z):
        cut = slice(z * HEAD, (z + 1) * HEAD)
        tile = jnp.where(row == 0, near[:, cut], jnp.where(row == 1, far[:, cut], 0.0)).astype(bf16)
        for c in range(2):
            n = c * Z + z
            out_ref[n, :QUERY_ROW, :] = weight[:, n * HEAD : (n + 1) * HEAD]
            out_ref[n, QUERY_ROW:HIDDEN_ROW, :] = zeros
            out_ref[n, HIDDEN_ROW:, :] = tile


def fill_payload(place, w_out, near, far):
    return pl.pallas_call(
        fill_body,
        out_shape=jax.ShapeDtypeStruct((2 * Z, ROWS, HEAD), bf16),
        in_specs=[SMEM, VMEM, VMEM, VMEM],
        out_specs=VMEM,
        compiler_params=pltpu.CompilerParams(vmem_limit_bytes=8 << 20),
        name="fill",
    )(place, w_out, near, far)


def query_body(arrived_ref, near_ref, far_ref, payload, out, parts, sent, sem):
    features = arrived_ref[...].astype(f32)
    total = jnp.dot(
        features[:, 0, :].astype(bf16), near_ref[...], preferred_element_type=f32
    ) + jnp.dot(features[:, 1, :].astype(bf16), far_ref[...], preferred_element_type=f32)
    high = total.astype(bf16).astype(f32)
    low = total - high
    for h in range(HEADS):
        c, cut = h // 8, slice(h * HEAD, (h + 1) * HEAD)
        parts[c * Z : (c + 1) * Z, h % 8, :] = high[:, cut]
        parts[c * Z : (c + 1) * Z, 8 + h % 8, :] = low[:, cut]
    sent[...] = parts[...].astype(bf16)
    back = pltpu.make_async_copy(sent, out.at[:, pl.ds(QUERY_ROW, 16), :], sem.at[0])
    back.start()
    back.wait()


def query_payload(arrived, near, far, payload):
    return pl.pallas_call(
        query_body,
        out_shape=jax.ShapeDtypeStruct(payload.shape, bf16),
        in_specs=[VMEM, VMEM, VMEM, HBM],
        out_specs=HBM,
        input_output_aliases={3: 0},
        scratch_shapes=[
            pltpu.VMEM((2 * Z, 16, HEAD), f32),
            pltpu.VMEM((2 * Z, 16, HEAD), bf16),
            pltpu.SemaphoreType.DMA((1,)),
        ],
        compiler_params=pltpu.CompilerParams(vmem_limit_bytes=8 << 20),
        name="query",
    )(arrived, near, far, payload)


def load_rows(own, low, high, w_ref, kind, y_lo, sem):
    return [
        pltpu.make_async_copy(own.at[:, :, pl.ds(kind * 256, 256)], w_ref.at[y_lo], sem.at[0]),
        pltpu.make_async_copy(low, w_ref.at[1 - y_lo, pl.ds(0, Z // 2)], sem.at[1]),
        pltpu.make_async_copy(high, w_ref.at[1 - y_lo, pl.ds(Z // 2, Z // 2)], sem.at[2]),
    ]


def attend_body(
    place_ref, len_ref, normed, other, cos_ref, sin_ref, parts, own, low, high, out_ref, w_ref, q_ref, rows_ref, sem, q_sem
):
    core, y_lo = place_ref[2], place_ref[3]
    copies = load_rows(own, low, high, w_ref, 0, y_lo, sem)
    fetch = pltpu.make_async_copy(parts.at[:, pl.ds(QUERY_ROW, 16), :], q_ref, q_sem.at[0])
    fills = [
        pltpu.make_async_copy(rows, rows_ref.at[p], q_sem.at[1 + p])
        for p, rows in enumerate((normed, other))
    ]
    for copy in [fetch] + fills[:1] + copies + fills[1:]:
        copy.start()
    cosine, sine = cos_ref[...], sin_ref[...]
    fetch.wait()
    by_core = [jnp.sum(q_ref[c * Z : (c + 1) * Z].astype(f32), axis=0) for c in range(2)]
    by_core = [both[:8] + both[8:] for both in by_core]
    queries = []
    for p in range(2):
        summed = jnp.where(core == p, by_core[0], by_core[1])
        last = len_ref[p] - 1
        turned = summed * cos_ref[pl.ds(last, 1), :] + pltpu.roll(summed, HEAD // 2, 1) * sin_ref[
            pl.ds(last, 1), :
        ]
        queries.append((turned * (1.0 / math.sqrt(HEAD))).astype(bf16))
    for copy in copies:
        copy.wait()
    weight = w_ref[...].reshape(Y_LO * Z * HEAD, 256)
    for p in range(2):
        fills[p].wait()
        rows = rows_ref[p]
        keys = jnp.dot(rows, weight, preferred_element_type=f32)
        scores = []
        for g in range(2):
            part = keys[:, g * HEAD : (g + 1) * HEAD]
            turned = (part * cosine + pltpu.roll(part, HEAD // 2, 1) * sine).astype(bf16)
            scores.append(
                lax.dot_general(
                    queries[p], turned, (((1,), (1,)), ((), ())), preferred_element_type=f32
                )
            )
        head = lax.broadcasted_iota(jnp.int32, scores[0].shape, 0)
        place = lax.broadcasted_iota(jnp.int32, scores[0].shape, 1)
        scores = jnp.where(head < 4, scores[0], scores[1])
        scores = jnp.where(place < len_ref[p], scores, -jnp.inf)
        powers = jnp.exp(scores - jnp.max(scores, axis=-1, keepdims=True))
        weights = (powers / jnp.sum(powers, axis=-1, keepdims=True)).astype(bf16)
        out_ref[p * 8 : (p + 1) * 8, :] = jnp.dot(weights, rows, preferred_element_type=f32)


def attend(place, lengths, normed, other, cosine, sine, parts, pieces):
    return pl.pallas_call(
        attend_body,
        out_shape=jax.ShapeDtypeStruct((16, normed.shape[1]), f32),
        in_specs=[SMEM, SMEM, HBM, HBM, VMEM, VMEM] + [HBM] * 4,
        out_specs=VMEM,
        scratch_shapes=[
            pltpu.VMEM((Y_LO, Z, HEAD, 256), bf16),
            pltpu.VMEM((2 * Z, 16, HEAD), bf16),
            pltpu.VMEM((2, *normed.shape), bf16),
            pltpu.SemaphoreType.DMA((3,)),
            pltpu.SemaphoreType.DMA((3,)),
        ],
        compiler_params=pltpu.CompilerParams(vmem_limit_bytes=48 << 20),
        name="attend",
    )(place, lengths, normed, other, cosine, sine, parts, *pieces)


def weigh_body(place_ref, u_ref, own, low, high, out_ref, w_ref, sem):
    core, y_lo = place_ref[2], place_ref[3]
    copies = load_rows(own, low, high, w_ref, 1, y_lo, sem)
    for copy in copies:
        copy.start()
    u = u_ref[...]
    first = u.astype(bf16)
    rest = u - first.astype(f32)
    second = rest.astype(bf16)
    third = (rest - second.astype(f32)).astype(bf16)
    for copy in copies:
        copy.wait()
    weight = w_ref[...].reshape(Y_LO * Z * HEAD, 256)
    parts = [jnp.dot(t, weight, preferred_element_type=f32) for t in (third, second, first)]
    total = parts[0] + parts[1] + parts[2]
    head = lax.broadcasted_iota(jnp.int32, (16, HEAD), 0)
    context = jnp.where((head & 7) < 4, total[:, :HEAD], total[:, HEAD:])
    turned = jnp.concatenate([context[8:], context[:8]], axis=0)
    context = jnp.where(core == 0, context, turned).astype(bf16)
    out_ref[...] = jnp.broadcast_to(context[None], out_ref.shape)


def weigh(place, u, pieces):
    return pl.pallas_call(
        weigh_body,
        out_shape=jax.ShapeDtypeStruct((2 * Z, 16, HEAD), bf16),
        in_specs=[SMEM, VMEM, HBM, HBM, HBM],
        out_specs=VMEM,
        scratch_shapes=[
            pltpu.VMEM((Y_LO, Z, HEAD, 256), bf16),
            pltpu.SemaphoreType.DMA((3,)),
        ],
        compiler_params=pltpu.CompilerParams(vmem_limit_bytes=32 << 20),
        name="weigh",
    )(place, u, *pieces)


def local(
    hidden, lengths, list_ids, list_owner, attn_gain, final_gain, w_query, w_key, w_value, w_out
):
    _, seq_len, width = hidden.shape
    dp, fsdp = lax.axis_index("dp"), lax.axis_index("fsdp")
    core, x = dp & 1, (dp >> 1) & (X - 1)
    y_lo = fsdp >> 4
    place = jnp.stack([lengths[0] - 1, x, core, y_lo]).astype(jnp.int32)

    unit = core_unit(place, w_key, w_value)
    gathered = lax.all_gather(unit, "fsdp", axis=0, tiled=False, axis_index_groups=Z_GROUPS)

    unit, hidden = lax.optimization_barrier((unit, hidden))
    outgoing, last_input = open_payload(place, hidden, attn_gain)
    arrived = lax.all_to_all(outgoing, "fsdp", 0, 0, tiled=True, axis_index_groups=Z_GROUPS)
    w_query_other = lax.ppermute(w_query, "fsdp", Y_LO_SWAP)
    last_other = lax.ppermute(last_input, "fsdp", Y_LO_SWAP)
    payload = fill_payload(place, w_out, last_input, last_other)

    payload = query_payload(arrived, w_query, w_query_other, payload)
    parts = lax.all_to_all(payload, BOTH, 0, 0, tiled=True, axis_index_groups=CORE_Z_GROUPS)

    rows, lengths, _ = lax.optimization_barrier((hidden[0], lengths, payload))
    both_lengths = jnp.concatenate([lengths, lax.ppermute(lengths, "dp", CORE_SWAP)])
    floats = rows.astype(f32)
    normed = (
        floats * lax.rsqrt(jnp.mean(floats * floats, axis=-1, keepdims=True) + 1e-05) * attn_gain
    ).astype(bf16)
    other = lax.ppermute(normed, "dp", CORE_SWAP)
    cosine, sine = rope_tables(jnp.arange(seq_len), HEAD)

    weight = jnp.transpose(parts[:, :QUERY_ROW].reshape(2, Z, 32, HEAD), (1, 0, 2, 3))
    weight = weight.reshape(2 * Z * 32, HEAD)
    weight = jnp.where(core == y_lo, weight, lax.ppermute(weight, BOTH, CROSS_SWAP))
    inputs = lax.dynamic_slice(parts, (core * Z, HIDDEN_ROW, 0), (Z, 2, HEAD)).astype(f32)
    inputs = jnp.where(y_lo == 0, inputs, inputs[:, ::-1])
    inputs = jnp.transpose(inputs, (1, 0, 2)).reshape(2 * Z, HEAD)

    half = Z // 2
    key_rows, value_rows = gathered[:, :, :256], gathered[:, :, 256:]
    key_low = lax.ppermute(key_rows[:half], BOTH, y_shift(-1))
    key_high = lax.ppermute(key_rows[half:], BOTH, y_shift(1))
    value_low = lax.ppermute(value_rows[:half], BOTH, y_shift(-1))
    value_high = lax.ppermute(value_rows[half:], BOTH, y_shift(1))

    place, weight, inputs = lax.optimization_barrier((place, weight, inputs))
    u = attend(
        place, both_lengths, normed, other, cosine, sine, parts, (gathered, key_low, key_high)
    )
    context = weigh(place, u, (gathered, value_low, value_high))
    contexts = lax.all_to_all(context, "fsdp", 0, 0, tiled=True)

    slabs = width // HEAD
    contexts = contexts.reshape(slabs, 2, 8 * HEAD)
    halves = jnp.einsum("sad,dn->asn", contexts, weight, preferred_element_type=f32)
    kept = lax.dynamic_index_in_dim(halves, core, 0, keepdims=False)
    given = lax.dynamic_index_in_dim(halves, 1 - core, 0, keepdims=False)
    residual = inputs + (kept + lax.ppermute(given, "dp", CORE_SWAP))
    gain = lax.dynamic_slice(final_gain, (fsdp * HEAD,), (HEAD,))
    scaled = residual * gain
    partial = jnp.sum(scaled * scaled, axis=-1)
    squares = lax.all_to_all(
        jnp.broadcast_to(partial[None, None, :], (slabs, 1, slabs)), "fsdp", 0, 0, tiled=True
    )
    mean = jnp.sum(squares, axis=0)[0] / width
    slab = (scaled * lax.rsqrt(mean + 1e-06)[:, None]).astype(bf16)

    owner_count = lax.axis_size("dp")
    capacity = 4
    list_index = jnp.arange(list_owner.shape[0])
    owners = jnp.sum(
        jnp.where(list_ids[:, None] == list_index[None, :], list_owner[None, :], 0), axis=1
    )
    owner_marks = (owners[:, None] == jnp.arange(owner_count)[None, :]).astype(jnp.int32)
    slot_rank = jnp.sum((jnp.cumsum(owner_marks, axis=0) - owner_marks) * owner_marks, axis=1)
    select = (
        (owners[None, None, :] == jnp.arange(owner_count)[:, None, None])
        & (slot_rank[None, None, :] == jnp.arange(capacity)[None, :, None])
    ).astype(bf16)
    outgoing = jnp.einsum("osr,rd->osd", select, slab, preferred_element_type=f32).astype(bf16)
    return lax.all_to_all(outgoing[:, None], "dp", split_axis=0, concat_axis=1, tiled=True)


def solution(mesh):
    in_specs = (
        P(("dp", "fsdp"), None, None),
        P(("dp", "fsdp")),
        P("dp"),
        P(),
        P(),
        P(),
        P("fsdp", None),
        P("fsdp", None),
        P("fsdp", None),
        P("fsdp", None),
    )
    out_specs = P("dp", None, None, "fsdp")
    return jax.shard_map(local, mesh=mesh, in_specs=in_specs, out_specs=out_specs, check_vma=False)
```

```python
import math

import jax
import jax.numpy as jnp
from jax import lax
from jax.experimental import pallas as pl
from jax.experimental.pallas import tpu as pltpu
from jax.sharding import PartitionSpec as P

HEADS = 16
KV_HEADS = 4
HEAD = 128
X = 4
Y_LO = 2
Z = 16
BOTH = ("dp", "fsdp")

bf16 = jnp.bfloat16
f32 = jnp.float32
VMEM = pl.BlockSpec(memory_space=pltpu.VMEM)
SMEM = pl.BlockSpec(memory_space=pltpu.SMEM)
HBM = pl.BlockSpec(memory_space=pltpu.HBM)


def dp_index(y_hi, x, core):
    return (y_hi * X + x) * 2 + core


def fsdp_index(y_lo, z):
    return y_lo * Z + z


Z_GROUPS = [[fsdp_index(yl, z) for z in range(Z)] for yl in range(Y_LO)]
X_GROUPS = [[dp_index(yh, x, c) for x in range(X)] for yh in range(2) for c in range(2)]
CORE_Z_GROUPS = [
    [dp_index(yh, x, c) * 32 + fsdp_index(yl, z) for c in range(2) for z in range(Z)]
    for yh in range(2)
    for x in range(X)
    for yl in range(Y_LO)
]
CROSS_SWAP = [
    (
        dp_index(yh, x, c) * 32 + fsdp_index(1 - c, z),
        dp_index(yh, x, 1 - c) * 32 + fsdp_index(c, z),
    )
    for yh in range(2)
    for x in range(X)
    for c in range(2)
    for z in range(Z)
]
CORE_SWAP = [(d, d ^ 1) for d in range(16)]
Y_LO_SWAP = [(i, i ^ Z) for i in range(32)]


def rope_tables(positions, head_width):
    halfway = head_width // 2
    frequency = 10000.0 ** (-jnp.arange(halfway, dtype=f32) * 2.0 / head_width)
    angles = positions.astype(f32)[..., None] * frequency
    cosine, sine = jnp.cos(angles), jnp.sin(angles)
    return (
        jnp.concatenate([cosine, cosine], axis=-1),
        jnp.concatenate([-sine, sine], axis=-1),
    )


def unit_body(place_ref, w_key, w_value, out, sem):
    columns = pl.ds(pl.multiple_of(place_ref[2] * 256, 256), 256)
    copies = [
        pltpu.make_async_copy(w.at[:, columns], out.at[:, pl.ds(k * 256, 256)], sem.at[k])
        for k, w in enumerate((w_key, w_value))
    ]
    for copy in copies:
        copy.start()
    for copy in copies:
        copy.wait()


def core_unit(place, w_key, w_value):
    return pl.pallas_call(
        unit_body,
        out_shape=jax.ShapeDtypeStruct((w_key.shape[0], 512), bf16),
        in_specs=[SMEM, HBM, HBM],
        out_specs=HBM,
        scratch_shapes=[pltpu.SemaphoreType.DMA((2,))],
        compiler_params=pltpu.CompilerParams(vmem_limit_bytes=1 << 20),
        name="unit",
    )(place, w_key, w_value)


def pair_body(near, far, out, sem):
    copies = [pltpu.make_async_copy(rows, out.at[k], sem.at[k]) for k, rows in enumerate((near, far))]
    for copy in copies:
        copy.start()
    for copy in copies:
        copy.wait()


def pair(near, far):
    return pl.pallas_call(
        pair_body,
        out_shape=jax.ShapeDtypeStruct((2, *near.shape), bf16),
        in_specs=[HBM, HBM],
        out_specs=HBM,
        scratch_shapes=[pltpu.SemaphoreType.DMA((2,))],
        compiler_params=pltpu.CompilerParams(vmem_limit_bytes=1 << 20),
        name="pair",
    )(near, far)


def open_body(place_ref, hidden, gain_ref, out_ref, last_ref, block, sem):
    last, y_lo = place_ref[0], place_ref[3]
    first = pl.multiple_of((last >> 3) << 3, 8)
    copy = pltpu.make_async_copy(hidden.at[0, pl.ds(first, 8)], block, sem.at[0])
    copy.start()
    copy.wait()
    floats = block[...].astype(f32)
    pick = lax.broadcasted_iota(jnp.int32, floats.shape, 0) == (last & 7)
    row = jnp.sum(jnp.where(pick, floats, 0.0), axis=0, keepdims=True)
    last_ref[...] = row.astype(bf16)
    normed = row * lax.rsqrt(jnp.mean(row * row, axis=-1, keepdims=True) + 1e-05) * gain_ref[...]
    normed = normed.astype(bf16).astype(f32)
    half = normed.shape[1] // 2
    place = lax.broadcasted_iota(jnp.int32, (8, HEAD), 0)
    for z in range(Z):
        low = normed[:, z * HEAD : (z + 1) * HEAD]
        high = normed[:, half + z * HEAD : half + (z + 1) * HEAD]
        mine = jnp.where(y_lo == 0, low, high)
        other = jnp.where(y_lo == 0, high, low)
        tile = jnp.where(place == 0, mine, jnp.where(place == 1, other, 0.0))
        out_ref[z] = tile.astype(bf16)


def open_payload(place, hidden, gain):
    width = hidden.shape[2]
    return pl.pallas_call(
        open_body,
        out_shape=(
            jax.ShapeDtypeStruct((Z, 8, HEAD), bf16),
            jax.ShapeDtypeStruct((1, width), bf16),
        ),
        in_specs=[SMEM, HBM, VMEM],
        out_specs=(VMEM, VMEM),
        scratch_shapes=[pltpu.VMEM((8, width), bf16), pltpu.SemaphoreType.DMA((1,))],
        compiler_params=pltpu.CompilerParams(vmem_limit_bytes=4 << 20),
        name="open",
    )(place, hidden, gain[None, :])


ROWS = 32
WEIGHT_ROW = 16
HIDDEN_ROW = 24


def fill_body(place_ref, w_out_ref, near_ref, far_ref, out_ref):
    x, core, y_lo = place_ref[1], place_ref[2], place_ref[3]
    rows = w_out_ref[...].astype(f32)
    weight = rows[:8]
    for n in range(1, 2 * X):
        weight = jnp.where(core * X + x == n, rows[n * 8 : n * 8 + 8], weight)
    row = lax.broadcasted_iota(jnp.int32, (8, HEAD), 0)
    half = Z * HEAD
    near, far = (
        jnp.where(y_lo == 0, rows[:, :half], rows[:, half:])
        for rows in (near_ref[...].astype(f32), far_ref[...].astype(f32))
    )
    for z in range(Z):
        cut = slice(z * HEAD, (z + 1) * HEAD)
        tile = jnp.where(row == 0, near[:, cut], jnp.where(row == 1, far[:, cut], 0.0))
        for c in range(2):
            n = c * Z + z
            both = jnp.concatenate([weight[:, n * HEAD : (n + 1) * HEAD], tile], axis=0)
            out_ref[n, :WEIGHT_ROW, :] = jnp.zeros((WEIGHT_ROW, HEAD), bf16)
            out_ref[n, WEIGHT_ROW:, :] = both.astype(bf16)


def fill_payload(place, w_out, near, far):
    return pl.pallas_call(
        fill_body,
        out_shape=jax.ShapeDtypeStruct((2 * Z, ROWS, HEAD), bf16),
        in_specs=[SMEM, VMEM, VMEM, VMEM],
        out_specs=VMEM,
        compiler_params=pltpu.CompilerParams(vmem_limit_bytes=8 << 20),
        name="fill",
    )(place, w_out, near, far)


def query_body(arrived_ref, near_ref, far_ref, payload, out, parts, sent, sem):
    features = arrived_ref[...].astype(f32)
    total = jnp.dot(
        features[:, 0, :].astype(bf16), near_ref[...], preferred_element_type=f32
    ) + jnp.dot(features[:, 1, :].astype(bf16), far_ref[...], preferred_element_type=f32)
    high = total.astype(bf16).astype(f32)
    low = total - high
    for h in range(HEADS):
        c, cut = h // 8, slice(h * HEAD, (h + 1) * HEAD)
        parts[c * Z : (c + 1) * Z, h % 8, :] = high[:, cut]
        parts[c * Z : (c + 1) * Z, 8 + h % 8, :] = low[:, cut]
    sent[...] = parts[...].astype(bf16)
    back = pltpu.make_async_copy(sent, out.at[:, pl.ds(0, 16), :], sem.at[0])
    back.start()
    back.wait()


def query_payload(arrived, near, far, payload):
    return pl.pallas_call(
        query_body,
        out_shape=jax.ShapeDtypeStruct(payload.shape, bf16),
        in_specs=[VMEM, VMEM, VMEM, HBM],
        out_specs=HBM,
        input_output_aliases={3: 0},
        scratch_shapes=[
            pltpu.VMEM((2 * Z, 16, HEAD), f32),
            pltpu.VMEM((2 * Z, 16, HEAD), bf16),
            pltpu.SemaphoreType.DMA((1,)),
        ],
        compiler_params=pltpu.CompilerParams(vmem_limit_bytes=8 << 20),
        name="query",
    )(arrived, near, far, payload)


def attend_body(
    place_ref, len_ref, normed_ref, other_ref, cos_ref, sin_ref, parts, gathered, out_ref, w_ref, q_ref, sem, q_sem
):
    fetch = pltpu.make_async_copy(parts.at[:, pl.ds(0, 16), :], q_ref, q_sem.at[0])
    fetch.start()
    core, y_lo = place_ref[2], place_ref[3]
    copies = [
        [
            pltpu.make_async_copy(
                gathered.at[:, n, :, pl.ds(kind * 256, 256)],
                w_ref.at[kind, y_lo if n == 0 else 1 - y_lo],
                sem.at[kind, n],
            )
            for n in range(2)
        ]
        for kind in range(2)
    ]
    for copy in copies[0] + copies[1]:
        copy.start()
    cosine, sine = cos_ref[...], sin_ref[...]
    fetch.wait()
    by_core = [jnp.sum(q_ref[c * Z : (c + 1) * Z].astype(f32), axis=0) for c in range(2)]
    by_core = [both[:8] + both[8:] for both in by_core]
    queries = []
    for p in range(2):
        summed = jnp.where(core == p, by_core[0], by_core[1])
        last = len_ref[p] - 1
        turned = summed * cos_ref[pl.ds(last, 1), :] + pltpu.roll(summed, HEAD // 2, 1) * sin_ref[
            pl.ds(last, 1), :
        ]
        queries.append((turned * (1.0 / math.sqrt(HEAD))).astype(bf16))
    for copy in copies[0]:
        copy.wait()
    weight = w_ref[0].reshape(Y_LO * Z * HEAD, 256)
    sums = []
    for p, rows_ref in enumerate((normed_ref, other_ref)):
        rows = rows_ref[...]
        keys = jnp.dot(rows, weight, preferred_element_type=f32)
        scores = []
        for g in range(2):
            part = keys[:, g * HEAD : (g + 1) * HEAD]
            turned = (part * cosine + pltpu.roll(part, HEAD // 2, 1) * sine).astype(bf16)
            scores.append(
                lax.dot_general(
                    queries[p], turned, (((1,), (1,)), ((), ())), preferred_element_type=f32
                )
            )
        head = lax.broadcasted_iota(jnp.int32, scores[0].shape, 0)
        place = lax.broadcasted_iota(jnp.int32, scores[0].shape, 1)
        scores = jnp.where(head < 4, scores[0], scores[1])
        scores = jnp.where(place < len_ref[p], scores, -jnp.inf)
        powers = jnp.exp(scores - jnp.max(scores, axis=-1, keepdims=True))
        weights = (powers / jnp.sum(powers, axis=-1, keepdims=True)).astype(bf16)
        sums.append(jnp.dot(weights, rows, preferred_element_type=f32))
    u = jnp.concatenate(sums, axis=0)
    first = u.astype(bf16)
    rest = u - first.astype(f32)
    second = rest.astype(bf16)
    third = (rest - second.astype(f32)).astype(bf16)
    for copy in copies[1]:
        copy.wait()
    weight = w_ref[1].reshape(Y_LO * Z * HEAD, 256)
    parts = [jnp.dot(t, weight, preferred_element_type=f32) for t in (third, second, first)]
    total = parts[0] + parts[1] + parts[2]
    head = lax.broadcasted_iota(jnp.int32, (16, HEAD), 0)
    context = jnp.where((head & 7) < 4, total[:, :HEAD], total[:, HEAD:])
    turned = jnp.concatenate([context[8:], context[:8]], axis=0)
    context = jnp.where(core == 0, context, turned).astype(bf16)
    out_ref[...] = jnp.broadcast_to(context[None], out_ref.shape)


def attend(place, lengths, normed, other, cosine, sine, parts, gathered):
    return pl.pallas_call(
        attend_body,
        out_shape=jax.ShapeDtypeStruct((2 * Z, 16, HEAD), bf16),
        in_specs=[SMEM, SMEM, VMEM, VMEM, VMEM, VMEM, HBM, HBM],
        out_specs=VMEM,
        scratch_shapes=[
            pltpu.VMEM((2, Y_LO, Z, HEAD, 256), bf16),
            pltpu.VMEM((2 * Z, 16, HEAD), bf16),
            pltpu.SemaphoreType.DMA((2, 2)),
            pltpu.SemaphoreType.DMA((1,)),
        ],
        compiler_params=pltpu.CompilerParams(vmem_limit_bytes=48 << 20),
        name="attend",
    )(place, lengths, normed, other, cosine, sine, parts, gathered)


def local(
    hidden, lengths, list_ids, list_owner, attn_gain, final_gain, w_query, w_key, w_value, w_out
):
    _, seq_len, width = hidden.shape
    dp, fsdp = lax.axis_index("dp"), lax.axis_index("fsdp")
    core, x = dp & 1, (dp >> 1) & (X - 1)
    y_lo = fsdp >> 4
    place = jnp.stack([lengths[0] - 1, x, core, y_lo]).astype(jnp.int32)

    unit = core_unit(place, w_key, w_value)
    units = pair(unit, lax.ppermute(unit, "fsdp", Y_LO_SWAP))
    gathered = lax.all_gather(units, "fsdp", axis=0, tiled=False, axis_index_groups=Z_GROUPS)

    unit, hidden = lax.optimization_barrier((unit, hidden))
    outgoing, last_input = open_payload(place, hidden, attn_gain)
    units, outgoing = lax.optimization_barrier((units, outgoing))
    arrived = lax.all_to_all(outgoing, "fsdp", 0, 0, tiled=True, axis_index_groups=Z_GROUPS)
    w_query_other = lax.ppermute(w_query, "fsdp", Y_LO_SWAP)
    last_other = lax.ppermute(last_input, "fsdp", Y_LO_SWAP)
    payload = fill_payload(place, w_out, last_input, last_other)

    payload = query_payload(arrived, w_query, w_query_other, payload)
    parts = lax.all_to_all(payload, BOTH, 0, 0, tiled=True, axis_index_groups=CORE_Z_GROUPS)

    rows, lengths, _ = lax.optimization_barrier((hidden[0], lengths, payload))
    both_lengths = jnp.concatenate([lengths, lax.ppermute(lengths, "dp", CORE_SWAP)])
    floats = rows.astype(f32)
    normed = (
        floats * lax.rsqrt(jnp.mean(floats * floats, axis=-1, keepdims=True) + 1e-05) * attn_gain
    ).astype(bf16)
    other = lax.ppermute(normed, "dp", CORE_SWAP)
    cosine, sine = rope_tables(jnp.arange(seq_len), HEAD)

    weight = lax.all_gather(
        parts[:, WEIGHT_ROW:HIDDEN_ROW], "dp", axis=0, tiled=False, axis_index_groups=X_GROUPS
    ).reshape(X, 2, Z, 8, HEAD)
    weight = jnp.transpose(weight, (2, 1, 0, 3, 4)).reshape(2 * Z * 32, HEAD)
    weight = jnp.where(core == y_lo, weight, lax.ppermute(weight, BOTH, CROSS_SWAP))
    inputs = lax.dynamic_slice(parts, (core * Z, HIDDEN_ROW, 0), (Z, 2, HEAD)).astype(f32)
    inputs = jnp.where(y_lo == 0, inputs, inputs[:, ::-1])
    inputs = jnp.transpose(inputs, (1, 0, 2)).reshape(2 * Z, HEAD)

    gathered, weight, inputs, both_lengths, normed, other, cosine, sine = lax.optimization_barrier(
        (gathered, weight, inputs, both_lengths, normed, other, cosine, sine)
    )
    context = attend(place, both_lengths, normed, other, cosine, sine, parts, gathered)
    contexts = lax.all_to_all(context, "fsdp", 0, 0, tiled=True)

    slabs = width // HEAD
    contexts = contexts.reshape(slabs, 2, 8 * HEAD)
    halves = jnp.einsum("sad,dn->asn", contexts, weight, preferred_element_type=f32)
    kept = lax.dynamic_index_in_dim(halves, core, 0, keepdims=False)
    given = lax.dynamic_index_in_dim(halves, 1 - core, 0, keepdims=False)
    residual = inputs + (kept + lax.ppermute(given, "dp", CORE_SWAP))
    gain = lax.dynamic_slice(final_gain, (fsdp * HEAD,), (HEAD,))
    scaled = residual * gain
    partial = jnp.sum(scaled * scaled, axis=-1)
    squares = lax.all_to_all(
        jnp.broadcast_to(partial[None, None, :], (slabs, 1, slabs)), "fsdp", 0, 0, tiled=True
    )
    mean = jnp.sum(squares, axis=0)[0] / width
    slab = (scaled * lax.rsqrt(mean + 1e-06)[:, None]).astype(bf16)

    owner_count = lax.axis_size("dp")
    capacity = 4
    list_index = jnp.arange(list_owner.shape[0])
    owners = jnp.sum(
        jnp.where(list_ids[:, None] == list_index[None, :], list_owner[None, :], 0), axis=1
    )
    owner_marks = (owners[:, None] == jnp.arange(owner_count)[None, :]).astype(jnp.int32)
    slot_rank = jnp.sum((jnp.cumsum(owner_marks, axis=0) - owner_marks) * owner_marks, axis=1)
    select = (
        (owners[None, None, :] == jnp.arange(owner_count)[:, None, None])
        & (slot_rank[None, None, :] == jnp.arange(capacity)[None, :, None])
    ).astype(bf16)
    outgoing = jnp.einsum("osr,rd->osd", select, slab, preferred_element_type=f32).astype(bf16)
    return lax.all_to_all(outgoing[:, None], "dp", split_axis=0, concat_axis=1, tiled=True)


def solution(mesh):
    in_specs = (
        P(("dp", "fsdp"), None, None),
        P(("dp", "fsdp")),
        P("dp"),
        P(),
        P(),
        P(),
        P("fsdp", None),
        P("fsdp", None),
        P("fsdp", None),
        P("fsdp", None),
    )
    out_specs = P("dp", None, None, "fsdp")
    return jax.shard_map(local, mesh=mesh, in_specs=in_specs, out_specs=out_specs, check_vma=False)
```

```python
import math

import jax
import jax.numpy as jnp
from jax import lax
from jax.experimental import pallas as pl
from jax.experimental.pallas import tpu as pltpu
from jax.sharding import PartitionSpec as P

HEADS = 16
KV_HEADS = 4
HEAD = 128
X = 4
Y_LO = 2
Z = 16
BOTH = ("dp", "fsdp")

bf16 = jnp.bfloat16
f32 = jnp.float32
VMEM = pl.BlockSpec(memory_space=pltpu.VMEM)
SMEM = pl.BlockSpec(memory_space=pltpu.SMEM)
HBM = pl.BlockSpec(memory_space=pltpu.HBM)


def dp_index(y_hi, x, core):
    return (y_hi * X + x) * 2 + core


def fsdp_index(y_lo, z):
    return y_lo * Z + z


Z_GROUPS = [[fsdp_index(yl, z) for z in range(Z)] for yl in range(Y_LO)]
CORE_Z_GROUPS = [
    [dp_index(yh, x, c) * 32 + fsdp_index(yl, z) for c in range(2) for z in range(Z)]
    for yh in range(2)
    for x in range(X)
    for yl in range(Y_LO)
]
CROSS_SWAP = [
    (
        dp_index(yh, x, c) * 32 + fsdp_index(1 - c, z),
        dp_index(yh, x, 1 - c) * 32 + fsdp_index(c, z),
    )
    for yh in range(2)
    for x in range(X)
    for c in range(2)
    for z in range(Z)
]
CORE_SWAP = [(d, d ^ 1) for d in range(16)]
Y_LO_SWAP = [(i, i ^ Z) for i in range(32)]


def x_shift(step):
    return [
        (dp_index(yh, x, c), dp_index(yh, (x + step) % X, c))
        for yh in range(2)
        for x in range(X)
        for c in range(2)
    ]


def y_shift(step):
    pairs = []
    for y in range(4):
        to = (y + step) % 4
        for x in range(X):
            for z in range(Z):
                for c in range(2):
                    pairs.append(
                        (
                            dp_index(y // 2, x, c) * 32 + fsdp_index(y % 2, z),
                            dp_index(to // 2, x, c) * 32 + fsdp_index(to % 2, z),
                        )
                    )
    return pairs


def rope_tables(positions, head_width):
    halfway = head_width // 2
    frequency = 10000.0 ** (-jnp.arange(halfway, dtype=f32) * 2.0 / head_width)
    angles = positions.astype(f32)[..., None] * frequency
    cosine, sine = jnp.cos(angles), jnp.sin(angles)
    return (
        jnp.concatenate([cosine, cosine], axis=-1),
        jnp.concatenate([-sine, sine], axis=-1),
    )


UNIT = 128


def open_body(place_ref, hidden, gain_ref, w_key, w_value, out_ref, last_ref, block, keys, values, sem):
    last, x, core = place_ref[0], place_ref[1], place_ref[2]
    first = pl.multiple_of((last >> 3) << 3, 8)
    rows = pl.ds(pl.multiple_of(x * 32, 32), 32)
    columns = pl.ds(pl.multiple_of(core * 256, 256), 256)
    copies = [
        pltpu.make_async_copy(hidden.at[0, pl.ds(first, 8)], block, sem.at[0]),
        pltpu.make_async_copy(w_key.at[rows, columns], keys, sem.at[1]),
        pltpu.make_async_copy(w_value.at[rows, columns], values, sem.at[2]),
    ]
    for copy in copies:
        copy.start()
    copies[0].wait()
    floats = block[...].astype(f32)
    pick = lax.broadcasted_iota(jnp.int32, floats.shape, 0) == (last & 7)
    row = jnp.sum(jnp.where(pick, floats, 0.0), axis=0, keepdims=True)
    last_ref[...] = row.astype(bf16)
    normed = row * lax.rsqrt(jnp.mean(row * row, axis=-1, keepdims=True) + 1e-05) * gain_ref[...]
    tokens = [normed[:, n * HEAD : (n + 1) * HEAD] for n in range(2 * Z)]
    out_ref[UNIT:, :] = jnp.concatenate(tokens, axis=0).astype(bf16)
    copies[1].wait()
    copies[2].wait()
    for k, w in enumerate((keys, values)):
        for g in range(2):
            n = (2 * k + g) * 32
            out_ref[n : n + 32, :] = w[:, g * HEAD : (g + 1) * HEAD]


def open_unit(place, hidden, gain, w_key, w_value):
    width = hidden.shape[2]
    return pl.pallas_call(
        open_body,
        out_shape=(
            jax.ShapeDtypeStruct((UNIT + 2 * Z, HEAD), bf16),
            jax.ShapeDtypeStruct((1, width), bf16),
        ),
        in_specs=[SMEM, HBM, VMEM, HBM, HBM],
        out_specs=(VMEM, VMEM),
        scratch_shapes=[
            pltpu.VMEM((8, width), bf16),
            pltpu.VMEM((32, 256), bf16),
            pltpu.VMEM((32, 256), bf16),
            pltpu.SemaphoreType.DMA((3,)),
        ],
        compiler_params=pltpu.CompilerParams(vmem_limit_bytes=62 << 20),
        name="open",
    )(place, hidden, gain[None, :], w_key, w_value)


ROWS = 48
QUERY_ROW = 32


def query_body(place_ref, tokens_ref, near_ref, far_ref, w_out_ref, out_ref, parts):
    core, y_lo, z = place_ref[2], place_ref[3], place_ref[4]
    rows = w_out_ref[...].astype(f32)
    weight = jnp.where(core == 0, rows[:32], rows[32:]).astype(bf16)
    tokens = tokens_ref[...].astype(f32)
    place = lax.broadcasted_iota(jnp.int32, tokens.shape, 1)
    near, far = (
        jnp.sum(jnp.where(place == y * Z + z, tokens, 0.0), axis=1).astype(bf16)
        for y in (y_lo, 1 - y_lo)
    )
    total = jnp.dot(near, near_ref[...], preferred_element_type=f32) + jnp.dot(
        far, far_ref[...], preferred_element_type=f32
    )
    high = total.astype(bf16).astype(f32)
    low = total - high
    for h in range(HEADS):
        c, cut = h // 8, slice(h * HEAD, (h + 1) * HEAD)
        parts[c * Z : (c + 1) * Z, h % 8, :] = high[:, cut]
        parts[c * Z : (c + 1) * Z, 8 + h % 8, :] = low[:, cut]
    out_ref[:, QUERY_ROW:, :] = parts[...].astype(bf16)
    for n in range(2 * Z):
        out_ref[n, :QUERY_ROW, :] = weight[:, n * HEAD : (n + 1) * HEAD]


def query_payload(place, tokens, near, far, w_out):
    return pl.pallas_call(
        query_body,
        out_shape=jax.ShapeDtypeStruct((2 * Z, ROWS, HEAD), bf16),
        in_specs=[SMEM, VMEM, VMEM, VMEM, VMEM],
        out_specs=VMEM,
        scratch_shapes=[pltpu.VMEM((2 * Z, 16, HEAD), f32)],
        compiler_params=pltpu.CompilerParams(vmem_limit_bytes=12 << 20),
        name="query",
    )(place, tokens, near, far, w_out)


def attend_body(place_ref, len_ref, normed, other, cos_ref, sin_ref, last_ref, parts, *refs):
    pieces, (out_ref, w_ref, q_ref, rows_ref, sem, q_sem) = refs[:8], refs[8:]
    fetch = pltpu.make_async_copy(parts.at[:, pl.ds(QUERY_ROW, 16), :], q_ref, q_sem.at[0])
    fetch.start()
    fills = [
        pltpu.make_async_copy(rows, rows_ref.at[p], q_sem.at[1 + p])
        for p, rows in enumerate((normed, other))
    ]
    x, core, y_lo = place_ref[1], place_ref[2], place_ref[3]
    copies = [[], []]
    for kind in range(2):
        for n, piece in enumerate(pieces):
            row = y_lo if n < X else 1 - y_lo
            column = (x + X - n % X) & (X - 1)
            for g in range(2):
                copies[kind].append(
                    pltpu.make_async_copy(
                        piece.at[:, pl.ds((kind * 2 + g) * 32, 32), :],
                        w_ref.at[kind, row, :, column, :, pl.ds(g * HEAD, HEAD)],
                        sem.at[kind, n, g],
                    )
                )
    for copy in fills[:1] + copies[0] + fills[1:] + copies[1]:
        copy.start()
    cosine, sine = cos_ref[...], sin_ref[...]
    fetch.wait()
    by_core = [jnp.sum(q_ref[c * Z : (c + 1) * Z].astype(f32), axis=0) for c in range(2)]
    by_core = [both[:8] + both[8:] for both in by_core]
    queries = []
    for p in range(2):
        summed = jnp.where(core == p, by_core[0], by_core[1])
        last = len_ref[p] - 1
        turned = summed * cos_ref[pl.ds(last, 1), :] + pltpu.roll(summed, HEAD // 2, 1) * sin_ref[
            pl.ds(last, 1), :
        ]
        queries.append((turned * (1.0 / math.sqrt(HEAD))).astype(bf16))
    for copy in copies[0]:
        copy.wait()
    weight = w_ref[0].reshape(Y_LO * Z * X * 32, 256)
    sums = []
    for p in range(2):
        fills[p].wait()
        rows = rows_ref[p]
        keys = jnp.dot(rows, weight, preferred_element_type=f32)
        scores = []
        for g in range(2):
            part = keys[:, g * HEAD : (g + 1) * HEAD]
            turned = (part * cosine + pltpu.roll(part, HEAD // 2, 1) * sine).astype(bf16)
            scores.append(
                lax.dot_general(
                    queries[p], turned, (((1,), (1,)), ((), ())), preferred_element_type=f32
                )
            )
        head = lax.broadcasted_iota(jnp.int32, scores[0].shape, 0)
        place = lax.broadcasted_iota(jnp.int32, scores[0].shape, 1)
        scores = jnp.where(head < 4, scores[0], scores[1])
        scores = jnp.where(place < len_ref[p], scores, -jnp.inf)
        powers = jnp.exp(scores - jnp.max(scores, axis=-1, keepdims=True))
        weights = (powers / jnp.sum(powers, axis=-1, keepdims=True)).astype(bf16)
        sums.append(jnp.dot(weights, rows, preferred_element_type=f32))
    u = jnp.concatenate(sums, axis=0)
    first = u.astype(bf16)
    rest = u - first.astype(f32)
    second = rest.astype(bf16)
    third = (rest - second.astype(f32)).astype(bf16)
    for copy in copies[1]:
        copy.wait()
    weight = w_ref[1].reshape(Y_LO * Z * X * 32, 256)
    parts = [jnp.dot(t, weight, preferred_element_type=f32) for t in (third, second, first)]
    total = parts[0] + parts[1] + parts[2]
    head = lax.broadcasted_iota(jnp.int32, (16, HEAD), 0)
    context = jnp.where((head & 7) < 4, total[:, :HEAD], total[:, HEAD:])
    turned = jnp.concatenate([context[8:], context[:8]], axis=0)
    context = jnp.where(core == 0, context, turned).astype(bf16)
    last = last_ref[...].astype(f32)
    for n in range(2 * Z):
        out_ref[n, :16, :] = context
        tile = jnp.broadcast_to(last[:, n * HEAD : (n + 1) * HEAD], (8, HEAD))
        out_ref[n, 16:, :] = tile.astype(bf16)


def attend(place, lengths, normed, other, cosine, sine, last, parts, pieces):
    return pl.pallas_call(
        attend_body,
        out_shape=jax.ShapeDtypeStruct((2 * Z, 24, HEAD), bf16),
        in_specs=[SMEM, SMEM, HBM, HBM, VMEM, VMEM, VMEM] + [HBM] * 9,
        out_specs=VMEM,
        scratch_shapes=[
            pltpu.VMEM((2, Y_LO, Z, X, 32, 256), bf16),
            pltpu.VMEM((2 * Z, 16, HEAD), bf16),
            pltpu.VMEM((2, *normed.shape), bf16),
            pltpu.SemaphoreType.DMA((2, 8, 2)),
            pltpu.SemaphoreType.DMA((3,)),
        ],
        compiler_params=pltpu.CompilerParams(vmem_limit_bytes=60 << 20),
        name="attend",
    )(place, lengths, normed, other, cosine, sine, last, parts, *pieces)


def local(
    hidden, lengths, list_ids, list_owner, attn_gain, final_gain, w_query, w_key, w_value, w_out
):
    _, seq_len, width = hidden.shape
    dp, fsdp = lax.axis_index("dp"), lax.axis_index("fsdp")
    core, x = dp & 1, (dp >> 1) & (X - 1)
    y_lo = fsdp >> 4
    z = fsdp & (Z - 1)
    place = jnp.stack([lengths[0] - 1, x, core, y_lo, z]).astype(jnp.int32)

    w_query_other = lax.ppermute(w_query, "fsdp", Y_LO_SWAP)
    unit, last_input = open_unit(place, hidden, attn_gain, w_key, w_value)
    arrived = lax.all_gather(unit, "fsdp", axis=0, tiled=False, axis_index_groups=Z_GROUPS)
    own, tokens = arrived[:, :UNIT], arrived[:, UNIT:]

    payload = query_payload(place, tokens, w_query, w_query_other, w_out)
    own, payload = lax.optimization_barrier((own, payload))
    parts = lax.all_to_all(payload, BOTH, 0, 0, tiled=True, axis_index_groups=CORE_Z_GROUPS)

    plus = lax.ppermute(own, "dp", x_shift(1))
    minus = lax.ppermute(own, "dp", x_shift(-1))
    far = lax.ppermute(own, "dp", x_shift(2))
    y_own = lax.ppermute(own, BOTH, y_shift(-1))
    y_plus = lax.ppermute(plus, BOTH, y_shift(1))
    y_minus = lax.ppermute(minus, BOTH, y_shift(1))
    y_far = lax.ppermute(far, BOTH, y_shift(-1))

    rows, lengths, _ = lax.optimization_barrier((hidden[0], lengths, payload))
    both_lengths = jnp.concatenate([lengths, lax.ppermute(lengths, "dp", CORE_SWAP)])
    floats = rows.astype(f32)
    normed = (
        floats * lax.rsqrt(jnp.mean(floats * floats, axis=-1, keepdims=True) + 1e-05) * attn_gain
    ).astype(bf16)
    other = lax.ppermute(normed, "dp", CORE_SWAP)
    cosine, sine = rope_tables(jnp.arange(seq_len), HEAD)

    weight = jnp.transpose(parts[:, :QUERY_ROW].reshape(2, Z, 32, HEAD), (1, 0, 2, 3))
    weight = weight.reshape(2 * Z * 32, HEAD)
    weight = jnp.where(core == y_lo, weight, lax.ppermute(weight, BOTH, CROSS_SWAP))

    place, weight = lax.optimization_barrier((place, weight))
    pieces = (own, plus, far, minus, y_own, y_plus, y_far, y_minus)
    context = attend(
        place, both_lengths, normed, other, cosine, sine, last_input, parts, pieces
    )
    contexts = lax.all_to_all(context, "fsdp", 0, 0, tiled=True)

    slabs = width // HEAD
    inputs = contexts[:, 16].astype(f32)
    contexts = contexts[:, :16].reshape(slabs, 2, 8 * HEAD)
    halves = jnp.einsum("sad,dn->asn", contexts, weight, preferred_element_type=f32)
    kept = lax.dynamic_index_in_dim(halves, core, 0, keepdims=False)
    given = lax.dynamic_index_in_dim(halves, 1 - core, 0, keepdims=False)
    residual = inputs + (kept + lax.ppermute(given, "dp", CORE_SWAP))
    gain = lax.dynamic_slice(final_gain, (fsdp * HEAD,), (HEAD,))
    scaled = residual * gain
    partial = jnp.sum(scaled * scaled, axis=-1)
    squares = lax.all_to_all(
        jnp.broadcast_to(partial[None, None, :], (slabs, 1, slabs)), "fsdp", 0, 0, tiled=True
    )
    mean = jnp.sum(squares, axis=0)[0] / width
    slab = (scaled * lax.rsqrt(mean + 1e-06)[:, None]).astype(bf16)

    owner_count = lax.axis_size("dp")
    capacity = 4
    list_index = jnp.arange(list_owner.shape[0])
    owners = jnp.sum(
        jnp.where(list_ids[:, None] == list_index[None, :], list_owner[None, :], 0), axis=1
    )
    owner_marks = (owners[:, None] == jnp.arange(owner_count)[None, :]).astype(jnp.int32)
    slot_rank = jnp.sum((jnp.cumsum(owner_marks, axis=0) - owner_marks) * owner_marks, axis=1)
    select = (
        (owners[None, None, :] == jnp.arange(owner_count)[:, None, None])
        & (slot_rank[None, None, :] == jnp.arange(capacity)[None, :, None])
    ).astype(bf16)
    outgoing = jnp.einsum("osr,rd->osd", select, slab, preferred_element_type=f32).astype(bf16)
    return lax.all_to_all(outgoing[:, None], "dp", split_axis=0, concat_axis=1, tiled=True)


def solution(mesh):
    in_specs = (
        P(("dp", "fsdp"), None, None),
        P(("dp", "fsdp")),
        P("dp"),
        P(),
        P(),
        P(),
        P("fsdp", None),
        P("fsdp", None),
        P("fsdp", None),
        P("fsdp", None),
    )
    out_specs = P("dp", None, None, "fsdp")
    return jax.shard_map(local, mesh=mesh, in_specs=in_specs, out_specs=out_specs, check_vma=False)
```

```python
import math

import jax
import jax.numpy as jnp
from jax import lax
from jax.experimental import pallas as pl
from jax.experimental.pallas import tpu as pltpu
from jax.sharding import PartitionSpec as P

HEADS = 16
KV_HEADS = 4
HEAD = 128
X = 4
Y_LO = 2
Z = 16
BOTH = ("dp", "fsdp")

bf16 = jnp.bfloat16
f32 = jnp.float32
VMEM = pl.BlockSpec(memory_space=pltpu.VMEM)
SMEM = pl.BlockSpec(memory_space=pltpu.SMEM)
HBM = pl.BlockSpec(memory_space=pltpu.HBM)


def dp_index(y_hi, x, core):
    return (y_hi * X + x) * 2 + core


def fsdp_index(y_lo, z):
    return y_lo * Z + z


Z_GROUPS = [[fsdp_index(yl, z) for z in range(Z)] for yl in range(Y_LO)]
X_GROUPS = [[dp_index(yh, x, c) for x in range(X)] for yh in range(2) for c in range(2)]
CORE_Z_GROUPS = [
    [dp_index(yh, x, c) * 32 + fsdp_index(yl, z) for c in range(2) for z in range(Z)]
    for yh in range(2)
    for x in range(X)
    for yl in range(Y_LO)
]
CROSS_SWAP = [
    (
        dp_index(yh, x, c) * 32 + fsdp_index(1 - c, z),
        dp_index(yh, x, 1 - c) * 32 + fsdp_index(c, z),
    )
    for yh in range(2)
    for x in range(X)
    for c in range(2)
    for z in range(Z)
]
CORE_SWAP = [(d, d ^ 1) for d in range(16)]
Y_LO_SWAP = [(i, i ^ Z) for i in range(32)]


def rope_tables(positions, head_width):
    halfway = head_width // 2
    frequency = 10000.0 ** (-jnp.arange(halfway, dtype=f32) * 2.0 / head_width)
    angles = positions.astype(f32)[..., None] * frequency
    cosine, sine = jnp.cos(angles), jnp.sin(angles)
    return (
        jnp.concatenate([cosine, cosine], axis=-1),
        jnp.concatenate([-sine, sine], axis=-1),
    )


def unit_body(place_ref, w_key, w_value, out, sem):
    columns = pl.ds(pl.multiple_of(place_ref[2] * 256, 256), 256)
    copies = [
        pltpu.make_async_copy(w.at[:, columns], out.at[:, pl.ds(k * 256, 256)], sem.at[k])
        for k, w in enumerate((w_key, w_value))
    ]
    for copy in copies:
        copy.start()
    for copy in copies:
        copy.wait()


def core_unit(place, w_key, w_value):
    return pl.pallas_call(
        unit_body,
        out_shape=jax.ShapeDtypeStruct((w_key.shape[0], 512), bf16),
        in_specs=[SMEM, HBM, HBM],
        out_specs=HBM,
        scratch_shapes=[pltpu.SemaphoreType.DMA((2,))],
        compiler_params=pltpu.CompilerParams(vmem_limit_bytes=62 << 20),
        name="unit",
    )(place, w_key, w_value)


def pair_body(near, far, out, sem):
    copies = [pltpu.make_async_copy(rows, out.at[k], sem.at[k]) for k, rows in enumerate((near, far))]
    for copy in copies:
        copy.start()
    for copy in copies:
        copy.wait()


def pair(near, far):
    return pl.pallas_call(
        pair_body,
        out_shape=jax.ShapeDtypeStruct((2, *near.shape), bf16),
        in_specs=[HBM, HBM],
        out_specs=HBM,
        scratch_shapes=[pltpu.SemaphoreType.DMA((2,))],
        compiler_params=pltpu.CompilerParams(vmem_limit_bytes=62 << 20),
        name="pair",
    )(near, far)


def open_body(place_ref, hidden, gain_ref, out_ref, last_ref, block, sem):
    last, y_lo = place_ref[0], place_ref[3]
    first = pl.multiple_of((last >> 3) << 3, 8)
    copy = pltpu.make_async_copy(hidden.at[0, pl.ds(first, 8)], block, sem.at[0])
    copy.start()
    copy.wait()
    floats = block[...].astype(f32)
    pick = lax.broadcasted_iota(jnp.int32, floats.shape, 0) == (last & 7)
    row = jnp.sum(jnp.where(pick, floats, 0.0), axis=0, keepdims=True)
    last_ref[...] = row.astype(bf16)
    normed = row * lax.rsqrt(jnp.mean(row * row, axis=-1, keepdims=True) + 1e-05) * gain_ref[...]
    normed = normed.astype(bf16).astype(f32)
    half = normed.shape[1] // 2
    place = lax.broadcasted_iota(jnp.int32, (8, HEAD), 0)
    for z in range(Z):
        low = normed[:, z * HEAD : (z + 1) * HEAD]
        high = normed[:, half + z * HEAD : half + (z + 1) * HEAD]
        mine = jnp.where(y_lo == 0, low, high)
        other = jnp.where(y_lo == 0, high, low)
        tile = jnp.where(place == 0, mine, jnp.where(place == 1, other, 0.0))
        out_ref[z] = tile.astype(bf16)


def open_payload(place, hidden, gain):
    width = hidden.shape[2]
    return pl.pallas_call(
        open_body,
        out_shape=(
            jax.ShapeDtypeStruct((Z, 8, HEAD), bf16),
            jax.ShapeDtypeStruct((1, width), bf16),
        ),
        in_specs=[SMEM, HBM, VMEM],
        out_specs=(VMEM, VMEM),
        scratch_shapes=[pltpu.VMEM((8, width), bf16), pltpu.SemaphoreType.DMA((1,))],
        compiler_params=pltpu.CompilerParams(vmem_limit_bytes=62 << 20),
        name="open",
    )(place, hidden, gain[None, :])


ROWS = 24
WEIGHT_ROW = 16


def query_body(place_ref, arrived_ref, near_ref, far_ref, w_out_ref, out_ref, parts):
    x, core = place_ref[1], place_ref[2]
    rows = w_out_ref[...].astype(f32)
    weight = rows[:8]
    for n in range(1, 2 * X):
        weight = jnp.where(core * X + x == n, rows[n * 8 : n * 8 + 8], weight)
    weight = weight.astype(bf16)
    features = arrived_ref[...].astype(f32)
    total = jnp.dot(
        features[:, 0, :].astype(bf16), near_ref[...], preferred_element_type=f32
    ) + jnp.dot(features[:, 1, :].astype(bf16), far_ref[...], preferred_element_type=f32)
    high = total.astype(bf16).astype(f32)
    low = total - high
    for h in range(HEADS):
        c, cut = h // 8, slice(h * HEAD, (h + 1) * HEAD)
        parts[c * Z : (c + 1) * Z, h % 8, :] = high[:, cut]
        parts[c * Z : (c + 1) * Z, 8 + h % 8, :] = low[:, cut]
    out_ref[:, :WEIGHT_ROW, :] = parts[...].astype(bf16)
    for n in range(2 * Z):
        out_ref[n, WEIGHT_ROW:, :] = weight[:, n * HEAD : (n + 1) * HEAD]


def query_payload(place, arrived, near, far, w_out):
    return pl.pallas_call(
        query_body,
        out_shape=jax.ShapeDtypeStruct((2 * Z, ROWS, HEAD), bf16),
        in_specs=[SMEM, VMEM, VMEM, VMEM, VMEM],
        out_specs=VMEM,
        scratch_shapes=[pltpu.VMEM((2 * Z, 16, HEAD), f32)],
        compiler_params=pltpu.CompilerParams(vmem_limit_bytes=12 << 20),
        name="query",
    )(place, arrived, near, far, w_out)


def attend_body(
    place_ref, len_ref, normed_ref, other_ref, cos_ref, sin_ref, last_ref, parts, gathered, out_ref, w_ref, q_ref, sem, q_sem
):
    fetch = pltpu.make_async_copy(parts.at[:, pl.ds(0, 16), :], q_ref, q_sem.at[0])
    fetch.start()
    core, y_lo = place_ref[2], place_ref[3]
    copies = [
        [
            pltpu.make_async_copy(
                gathered.at[:, n, :, pl.ds(kind * 256, 256)],
                w_ref.at[kind, y_lo if n == 0 else 1 - y_lo],
                sem.at[kind, n],
            )
            for n in range(2)
        ]
        for kind in range(2)
    ]
    for copy in copies[0] + copies[1]:
        copy.start()
    cosine, sine = cos_ref[...], sin_ref[...]
    fetch.wait()
    by_core = [jnp.sum(q_ref[c * Z : (c + 1) * Z].astype(f32), axis=0) for c in range(2)]
    by_core = [both[:8] + both[8:] for both in by_core]
    queries = []
    for p in range(2):
        summed = jnp.where(core == p, by_core[0], by_core[1])
        last = len_ref[p] - 1
        turned = summed * cos_ref[pl.ds(last, 1), :] + pltpu.roll(summed, HEAD // 2, 1) * sin_ref[
            pl.ds(last, 1), :
        ]
        queries.append((turned * (1.0 / math.sqrt(HEAD))).astype(bf16))
    for copy in copies[0]:
        copy.wait()
    weight = w_ref[0].reshape(Y_LO * Z * HEAD, 256)
    sums = []
    for p, rows_ref in enumerate((normed_ref, other_ref)):
        rows = rows_ref[...]
        keys = jnp.dot(rows, weight, preferred_element_type=f32)
        scores = []
        for g in range(2):
            part = keys[:, g * HEAD : (g + 1) * HEAD]
            turned = (part * cosine + pltpu.roll(part, HEAD // 2, 1) * sine).astype(bf16)
            scores.append(
                lax.dot_general(
                    queries[p], turned, (((1,), (1,)), ((), ())), preferred_element_type=f32
                )
            )
        head = lax.broadcasted_iota(jnp.int32, scores[0].shape, 0)
        place = lax.broadcasted_iota(jnp.int32, scores[0].shape, 1)
        scores = jnp.where(head < 4, scores[0], scores[1])
        scores = jnp.where(place < len_ref[p], scores, -jnp.inf)
        powers = jnp.exp(scores - jnp.max(scores, axis=-1, keepdims=True))
        weights = (powers / jnp.sum(powers, axis=-1, keepdims=True)).astype(bf16)
        sums.append(jnp.dot(weights, rows, preferred_element_type=f32))
    u = jnp.concatenate(sums, axis=0)
    first = u.astype(bf16)
    rest = u - first.astype(f32)
    second = rest.astype(bf16)
    third = (rest - second.astype(f32)).astype(bf16)
    for copy in copies[1]:
        copy.wait()
    weight = w_ref[1].reshape(Y_LO * Z * HEAD, 256)
    stacked = jnp.dot(
        jnp.concatenate([third, second, first], axis=0), weight, preferred_element_type=f32
    )
    total = stacked[:16] + stacked[16:32] + stacked[32:]
    head = lax.broadcasted_iota(jnp.int32, (16, HEAD), 0)
    context = jnp.where((head & 7) < 4, total[:, :HEAD], total[:, HEAD:])
    turned = jnp.concatenate([context[8:], context[:8]], axis=0)
    context = jnp.where(core == 0, context, turned).astype(bf16)
    last = last_ref[...].astype(f32)
    for n in range(2 * Z):
        out_ref[n, :16, :] = context
        tile = jnp.broadcast_to(last[:, n * HEAD : (n + 1) * HEAD], (8, HEAD))
        out_ref[n, 16:, :] = tile.astype(bf16)


def attend(place, lengths, normed, other, cosine, sine, last, parts, gathered):
    return pl.pallas_call(
        attend_body,
        out_shape=jax.ShapeDtypeStruct((2 * Z, 24, HEAD), bf16),
        in_specs=[SMEM, SMEM, VMEM, VMEM, VMEM, VMEM, VMEM, HBM, HBM],
        out_specs=VMEM,
        scratch_shapes=[
            pltpu.VMEM((2, Y_LO, Z, HEAD, 256), bf16),
            pltpu.VMEM((2 * Z, 16, HEAD), bf16),
            pltpu.SemaphoreType.DMA((2, 2)),
            pltpu.SemaphoreType.DMA((1,)),
        ],
        compiler_params=pltpu.CompilerParams(vmem_limit_bytes=48 << 20),
        name="attend",
    )(place, lengths, normed, other, cosine, sine, last, parts, gathered)


def local(
    hidden, lengths, list_ids, list_owner, attn_gain, final_gain, w_query, w_key, w_value, w_out
):
    _, seq_len, width = hidden.shape
    dp, fsdp = lax.axis_index("dp"), lax.axis_index("fsdp")
    core, x = dp & 1, (dp >> 1) & (X - 1)
    y_lo = fsdp >> 4
    place = jnp.stack([lengths[0] - 1, x, core, y_lo]).astype(jnp.int32)

    unit = core_unit(place, w_key, w_value)
    units = pair(unit, lax.ppermute(unit, "fsdp", Y_LO_SWAP))
    gathered = lax.all_gather(units, "fsdp", axis=0, tiled=False, axis_index_groups=Z_GROUPS)

    unit, hidden = lax.optimization_barrier((unit, hidden))
    outgoing, last_input = open_payload(place, hidden, attn_gain)
    units, outgoing = lax.optimization_barrier((units, outgoing))
    arrived = lax.all_to_all(outgoing, "fsdp", 0, 0, tiled=True, axis_index_groups=Z_GROUPS)
    w_query_other = lax.ppermute(w_query, "fsdp", Y_LO_SWAP)

    payload = query_payload(place, arrived, w_query, w_query_other, w_out)
    parts = lax.all_to_all(payload, BOTH, 0, 0, tiled=True, axis_index_groups=CORE_Z_GROUPS)

    rows, lengths, parts = lax.optimization_barrier((hidden[0], lengths, parts))
    both_lengths = jnp.concatenate([lengths, lax.ppermute(lengths, "dp", CORE_SWAP)])
    floats = rows.astype(f32)
    normed = (
        floats * lax.rsqrt(jnp.mean(floats * floats, axis=-1, keepdims=True) + 1e-05) * attn_gain
    ).astype(bf16)
    other = lax.ppermute(normed, "dp", CORE_SWAP)
    cosine, sine = rope_tables(jnp.arange(seq_len), HEAD)

    weight = lax.all_gather(
        parts[:, WEIGHT_ROW:], "dp", axis=0, tiled=False, axis_index_groups=X_GROUPS
    ).reshape(X, 2, Z, 8, HEAD)
    weight = jnp.transpose(weight, (2, 1, 0, 3, 4)).reshape(2 * Z * 32, HEAD)
    weight = jnp.where(core == y_lo, weight, lax.ppermute(weight, BOTH, CROSS_SWAP))
    gathered, weight, both_lengths, normed, other, cosine, sine = lax.optimization_barrier(
        (gathered, weight, both_lengths, normed, other, cosine, sine)
    )
    context = attend(place, both_lengths, normed, other, cosine, sine, last_input, parts, gathered)
    contexts = lax.all_to_all(context, "fsdp", 0, 0, tiled=True)

    slabs = width // HEAD
    inputs = contexts[:, 16].astype(f32)
    contexts = contexts[:, :16].reshape(slabs, 2, 8 * HEAD)
    halves = jnp.einsum("sad,dn->asn", contexts, weight, preferred_element_type=f32)
    kept = lax.dynamic_index_in_dim(halves, core, 0, keepdims=False)
    given = lax.dynamic_index_in_dim(halves, 1 - core, 0, keepdims=False)
    residual = inputs + (kept + lax.ppermute(given, "dp", CORE_SWAP))
    gain = lax.dynamic_slice(final_gain, (fsdp * HEAD,), (HEAD,))
    scaled = residual * gain
    partial = jnp.sum(scaled * scaled, axis=-1)
    squares = lax.all_to_all(
        jnp.broadcast_to(partial[None, None, :], (slabs, 1, slabs)), "fsdp", 0, 0, tiled=True
    )
    mean = jnp.sum(squares, axis=0)[0] / width
    slab = (scaled * lax.rsqrt(mean + 1e-06)[:, None]).astype(bf16)

    owner_count = lax.axis_size("dp")
    capacity = 4
    list_index = jnp.arange(list_owner.shape[0])
    owners = jnp.sum(
        jnp.where(list_ids[:, None] == list_index[None, :], list_owner[None, :], 0), axis=1
    )
    owner_marks = (owners[:, None] == jnp.arange(owner_count)[None, :]).astype(jnp.int32)
    slot_rank = jnp.sum((jnp.cumsum(owner_marks, axis=0) - owner_marks) * owner_marks, axis=1)
    select = (
        (owners[None, None, :] == jnp.arange(owner_count)[:, None, None])
        & (slot_rank[None, None, :] == jnp.arange(capacity)[None, :, None])
    ).astype(bf16)
    outgoing = jnp.einsum("osr,rd->osd", select, slab, preferred_element_type=f32).astype(bf16)
    return lax.all_to_all(outgoing[:, None], "dp", split_axis=0, concat_axis=1, tiled=True)


def solution(mesh):
    in_specs = (
        P(("dp", "fsdp"), None, None),
        P(("dp", "fsdp")),
        P("dp"),
        P(),
        P(),
        P(),
        P("fsdp", None),
        P("fsdp", None),
        P("fsdp", None),
        P("fsdp", None),
    )
    out_specs = P("dp", None, None, "fsdp")
    return jax.shard_map(local, mesh=mesh, in_specs=in_specs, out_specs=out_specs, check_vma=False)
```

```python
import math

import jax
import jax.numpy as jnp
from jax import lax
from jax.experimental import pallas as pl
from jax.experimental.pallas import tpu as pltpu
from jax.sharding import PartitionSpec as P

HEADS = 16
KV_HEADS = 4
HEAD = 128
X = 4
Y_LO = 2
Z = 16
BOTH = ("dp", "fsdp")

bf16 = jnp.bfloat16
f32 = jnp.float32
VMEM = pl.BlockSpec(memory_space=pltpu.VMEM)
SMEM = pl.BlockSpec(memory_space=pltpu.SMEM)
HBM = pl.BlockSpec(memory_space=pltpu.HBM)


def dp_index(y_hi, x, core):
    return (y_hi * X + x) * 2 + core


def fsdp_index(y_lo, z):
    return y_lo * Z + z


Z_GROUPS = [[fsdp_index(yl, z) for z in range(Z)] for yl in range(Y_LO)]
X_GROUPS = [[dp_index(yh, x, c) for x in range(X)] for yh in range(2) for c in range(2)]
CORE_Z_GROUPS = [
    [dp_index(yh, x, c) * 32 + fsdp_index(yl, z) for c in range(2) for z in range(Z)]
    for yh in range(2)
    for x in range(X)
    for yl in range(Y_LO)
]
CROSS_SWAP = [
    (
        dp_index(yh, x, c) * 32 + fsdp_index(1 - c, z),
        dp_index(yh, x, 1 - c) * 32 + fsdp_index(c, z),
    )
    for yh in range(2)
    for x in range(X)
    for c in range(2)
    for z in range(Z)
]
CORE_SWAP = [(d, d ^ 1) for d in range(16)]
Y_LO_SWAP = [(i, i ^ Z) for i in range(32)]


def rope_tables(positions, head_width):
    halfway = head_width // 2
    frequency = 10000.0 ** (-jnp.arange(halfway, dtype=f32) * 2.0 / head_width)
    angles = positions.astype(f32)[..., None] * frequency
    cosine, sine = jnp.cos(angles), jnp.sin(angles)
    return (
        jnp.concatenate([cosine, cosine], axis=-1),
        jnp.concatenate([-sine, sine], axis=-1),
    )


def unit_body(place_ref, key_ref, value_ref, out_ref):
    core = place_ref[2]
    for k, w in enumerate((key_ref, value_ref)):
        columns = pl.multiple_of(core * 256, 256)
        out_ref[:, k * 256 : (k + 1) * 256] = w[:, pl.ds(columns, 256)]


def core_unit(place, w_key, w_value):
    return pl.pallas_call(
        unit_body,
        out_shape=jax.ShapeDtypeStruct((w_key.shape[0], 512), bf16),
        in_specs=[SMEM, VMEM, VMEM],
        out_specs=VMEM,
        compiler_params=pltpu.CompilerParams(vmem_limit_bytes=62 << 20),
        name="unit",
    )(place, w_key, w_value)


def pair_body(near_ref, far_ref, out_ref):
    out_ref[0] = near_ref[...]
    out_ref[1] = far_ref[...]


def pair(near, far):
    return pl.pallas_call(
        pair_body,
        out_shape=jax.ShapeDtypeStruct((2, *near.shape), bf16),
        in_specs=[VMEM, VMEM],
        out_specs=VMEM,
        compiler_params=pltpu.CompilerParams(vmem_limit_bytes=8 << 20),
        name="pair",
    )(near, far)


def open_body(place_ref, hidden, gain_ref, out_ref, last_ref, block, sem):
    last, y_lo = place_ref[0], place_ref[3]
    first = pl.multiple_of((last >> 3) << 3, 8)
    copy = pltpu.make_async_copy(hidden.at[0, pl.ds(first, 8)], block, sem.at[0])
    copy.start()
    copy.wait()
    floats = block[...].astype(f32)
    pick = lax.broadcasted_iota(jnp.int32, floats.shape, 0) == (last & 7)
    row = jnp.sum(jnp.where(pick, floats, 0.0), axis=0, keepdims=True)
    last_ref[...] = row.astype(bf16)
    normed = row * lax.rsqrt(jnp.mean(row * row, axis=-1, keepdims=True) + 1e-05) * gain_ref[...]
    normed = normed.astype(bf16).astype(f32)
    half = normed.shape[1] // 2
    place = lax.broadcasted_iota(jnp.int32, (8, HEAD), 0)
    for z in range(Z):
        low = normed[:, z * HEAD : (z + 1) * HEAD]
        high = normed[:, half + z * HEAD : half + (z + 1) * HEAD]
        mine = jnp.where(y_lo == 0, low, high)
        other = jnp.where(y_lo == 0, high, low)
        tile = jnp.where(place == 0, mine, jnp.where(place == 1, other, 0.0))
        out_ref[z] = tile.astype(bf16)


def open_payload(place, hidden, gain):
    width = hidden.shape[2]
    return pl.pallas_call(
        open_body,
        out_shape=(
            jax.ShapeDtypeStruct((Z, 8, HEAD), bf16),
            jax.ShapeDtypeStruct((1, width), bf16),
        ),
        in_specs=[SMEM, HBM, VMEM],
        out_specs=(VMEM, VMEM),
        scratch_shapes=[pltpu.VMEM((8, width), bf16), pltpu.SemaphoreType.DMA((1,))],
        compiler_params=pltpu.CompilerParams(vmem_limit_bytes=62 << 20),
        name="open",
    )(place, hidden, gain[None, :])


ROWS = 24
WEIGHT_ROW = 16


def query_body(place_ref, arrived_ref, near_ref, far_ref, w_out_ref, out_ref, parts):
    x, core = place_ref[1], place_ref[2]
    rows = w_out_ref[...].astype(f32)
    weight = rows[:8]
    for n in range(1, 2 * X):
        weight = jnp.where(core * X + x == n, rows[n * 8 : n * 8 + 8], weight)
    weight = weight.astype(bf16)
    features = arrived_ref[...].astype(f32)
    total = jnp.dot(
        features[:, 0, :].astype(bf16), near_ref[...], preferred_element_type=f32
    ) + jnp.dot(features[:, 1, :].astype(bf16), far_ref[...], preferred_element_type=f32)
    high = total.astype(bf16).astype(f32)
    low = total - high
    for h in range(HEADS):
        c, cut = h // 8, slice(h * HEAD, (h + 1) * HEAD)
        parts[c * Z : (c + 1) * Z, h % 8, :] = high[:, cut]
        parts[c * Z : (c + 1) * Z, 8 + h % 8, :] = low[:, cut]
    out_ref[:, :WEIGHT_ROW, :] = parts[...].astype(bf16)
    for n in range(2 * Z):
        out_ref[n, WEIGHT_ROW:, :] = weight[:, n * HEAD : (n + 1) * HEAD]


def query_payload(place, arrived, near, far, w_out):
    return pl.pallas_call(
        query_body,
        out_shape=jax.ShapeDtypeStruct((2 * Z, ROWS, HEAD), bf16),
        in_specs=[SMEM, VMEM, VMEM, VMEM, VMEM],
        out_specs=VMEM,
        scratch_shapes=[pltpu.VMEM((2 * Z, 16, HEAD), f32)],
        compiler_params=pltpu.CompilerParams(vmem_limit_bytes=12 << 20),
        name="query",
    )(place, arrived, near, far, w_out)


def attend_body(
    place_ref, len_ref, normed_ref, other_ref, cos_ref, sin_ref, last_ref, parts, gathered, out_ref, w_ref, q_ref, sem, q_sem
):
    fetch = pltpu.make_async_copy(parts.at[:, pl.ds(0, 16), :], q_ref, q_sem.at[0])
    fetch.start()
    core, y_lo = place_ref[2], place_ref[3]
    copies = [
        [
            pltpu.make_async_copy(
                gathered.at[:, n, :, pl.ds(kind * 256, 256)],
                w_ref.at[kind, y_lo if n == 0 else 1 - y_lo],
                sem.at[kind, n],
            )
            for n in range(2)
        ]
        for kind in range(2)
    ]
    for copy in copies[0] + copies[1]:
        copy.start()
    cosine, sine = cos_ref[...], sin_ref[...]
    fetch.wait()
    by_core = [jnp.sum(q_ref[c * Z : (c + 1) * Z].astype(f32), axis=0) for c in range(2)]
    by_core = [both[:8] + both[8:] for both in by_core]
    queries = []
    for p in range(2):
        summed = jnp.where(core == p, by_core[0], by_core[1])
        last = len_ref[p] - 1
        turned = summed * cos_ref[pl.ds(last, 1), :] + pltpu.roll(summed, HEAD // 2, 1) * sin_ref[
            pl.ds(last, 1), :
        ]
        queries.append((turned * (1.0 / math.sqrt(HEAD))).astype(bf16))
    for copy in copies[0]:
        copy.wait()
    weight = w_ref[0].reshape(Y_LO * Z * HEAD, 256)
    sums = []
    for p, rows_ref in enumerate((normed_ref, other_ref)):
        rows = rows_ref[...]
        keys = jnp.dot(rows, weight, preferred_element_type=f32)
        scores = []
        for g in range(2):
            part = keys[:, g * HEAD : (g + 1) * HEAD]
            turned = (part * cosine + pltpu.roll(part, HEAD // 2, 1) * sine).astype(bf16)
            scores.append(
                lax.dot_general(
                    queries[p], turned, (((1,), (1,)), ((), ())), preferred_element_type=f32
                )
            )
        head = lax.broadcasted_iota(jnp.int32, scores[0].shape, 0)
        place = lax.broadcasted_iota(jnp.int32, scores[0].shape, 1)
        scores = jnp.where(head < 4, scores[0], scores[1])
        scores = jnp.where(place < len_ref[p], scores, -jnp.inf)
        powers = jnp.exp(scores - jnp.max(scores, axis=-1, keepdims=True))
        weights = (powers / jnp.sum(powers, axis=-1, keepdims=True)).astype(bf16)
        sums.append(jnp.dot(weights, rows, preferred_element_type=f32))
    u = jnp.concatenate(sums, axis=0)
    first = u.astype(bf16)
    rest = u - first.astype(f32)
    second = rest.astype(bf16)
    third = (rest - second.astype(f32)).astype(bf16)
    for copy in copies[1]:
        copy.wait()
    weight = w_ref[1].reshape(Y_LO * Z * HEAD, 256)
    stacked = jnp.dot(
        jnp.concatenate([third, second, first], axis=0), weight, preferred_element_type=f32
    )
    total = stacked[:16] + stacked[16:32] + stacked[32:]
    head = lax.broadcasted_iota(jnp.int32, (16, HEAD), 0)
    context = jnp.where((head & 7) < 4, total[:, :HEAD], total[:, HEAD:])
    turned = jnp.concatenate([context[8:], context[:8]], axis=0)
    context = jnp.where(core == 0, context, turned).astype(bf16)
    last = last_ref[...].astype(f32)
    for n in range(2 * Z):
        out_ref[n, :16, :] = context
        tile = jnp.broadcast_to(last[:, n * HEAD : (n + 1) * HEAD], (8, HEAD))
        out_ref[n, 16:, :] = tile.astype(bf16)


def attend(place, lengths, normed, other, cosine, sine, last, parts, gathered):
    return pl.pallas_call(
        attend_body,
        out_shape=jax.ShapeDtypeStruct((2 * Z, 24, HEAD), bf16),
        in_specs=[SMEM, SMEM, VMEM, VMEM, VMEM, VMEM, VMEM, HBM, HBM],
        out_specs=VMEM,
        scratch_shapes=[
            pltpu.VMEM((2, Y_LO, Z, HEAD, 256), bf16),
            pltpu.VMEM((2 * Z, 16, HEAD), bf16),
            pltpu.SemaphoreType.DMA((2, 2)),
            pltpu.SemaphoreType.DMA((1,)),
        ],
        compiler_params=pltpu.CompilerParams(vmem_limit_bytes=48 << 20),
        name="attend",
    )(place, lengths, normed, other, cosine, sine, last, parts, gathered)


def local(
    hidden, lengths, list_ids, list_owner, attn_gain, final_gain, w_query, w_key, w_value, w_out
):
    _, seq_len, width = hidden.shape
    dp, fsdp = lax.axis_index("dp"), lax.axis_index("fsdp")
    core, x = dp & 1, (dp >> 1) & (X - 1)
    y_lo = fsdp >> 4
    place = jnp.stack([lengths[0] - 1, x, core, y_lo]).astype(jnp.int32)

    unit = core_unit(place, w_key, w_value)
    units = pair(unit, lax.ppermute(unit, "fsdp", Y_LO_SWAP))
    gathered = lax.all_gather(units, "fsdp", axis=0, tiled=False, axis_index_groups=Z_GROUPS)

    unit, hidden = lax.optimization_barrier((unit, hidden))
    outgoing, last_input = open_payload(place, hidden, attn_gain)
    units, outgoing = lax.optimization_barrier((units, outgoing))
    arrived = lax.all_to_all(outgoing, "fsdp", 0, 0, tiled=True, axis_index_groups=Z_GROUPS)
    w_query_other = lax.ppermute(w_query, "fsdp", Y_LO_SWAP)

    payload = query_payload(place, arrived, w_query, w_query_other, w_out)
    parts = lax.all_to_all(payload, BOTH, 0, 0, tiled=True, axis_index_groups=CORE_Z_GROUPS)

    rows, lengths, parts = lax.optimization_barrier((hidden[0], lengths, parts))
    both_lengths = jnp.concatenate([lengths, lax.ppermute(lengths, "dp", CORE_SWAP)])
    floats = rows.astype(f32)
    normed = (
        floats * lax.rsqrt(jnp.mean(floats * floats, axis=-1, keepdims=True) + 1e-05) * attn_gain
    ).astype(bf16)
    other = lax.ppermute(normed, "dp", CORE_SWAP)
    cosine, sine = rope_tables(jnp.arange(seq_len), HEAD)

    weight = lax.all_gather(
        parts[:, WEIGHT_ROW:], "dp", axis=0, tiled=False, axis_index_groups=X_GROUPS
    ).reshape(X, 2, Z, 8, HEAD)
    weight = jnp.transpose(weight, (2, 1, 0, 3, 4)).reshape(2 * Z * 32, HEAD)
    weight = jnp.where(core == y_lo, weight, lax.ppermute(weight, BOTH, CROSS_SWAP))
    gathered, weight, both_lengths, normed, other, cosine, sine = lax.optimization_barrier(
        (gathered, weight, both_lengths, normed, other, cosine, sine)
    )
    context = attend(place, both_lengths, normed, other, cosine, sine, last_input, parts, gathered)
    contexts = lax.all_to_all(context, "fsdp", 0, 0, tiled=True)

    slabs = width // HEAD
    inputs = contexts[:, 16].astype(f32)
    contexts = contexts[:, :16].reshape(slabs, 2, 8 * HEAD)
    halves = jnp.einsum("sad,dn->asn", contexts, weight, preferred_element_type=f32)
    kept = lax.dynamic_index_in_dim(halves, core, 0, keepdims=False)
    given = lax.dynamic_index_in_dim(halves, 1 - core, 0, keepdims=False)
    residual = inputs + (kept + lax.ppermute(given, "dp", CORE_SWAP))
    gain = lax.dynamic_slice(final_gain, (fsdp * HEAD,), (HEAD,))
    scaled = residual * gain
    partial = jnp.sum(scaled * scaled, axis=-1)
    squares = lax.all_to_all(
        jnp.broadcast_to(partial[None, None, :], (slabs, 1, slabs)), "fsdp", 0, 0, tiled=True
    )
    mean = jnp.sum(squares, axis=0)[0] / width
    slab = (scaled * lax.rsqrt(mean + 1e-06)[:, None]).astype(bf16)

    owner_count = lax.axis_size("dp")
    capacity = 4
    list_index = jnp.arange(list_owner.shape[0])
    owners = jnp.sum(
        jnp.where(list_ids[:, None] == list_index[None, :], list_owner[None, :], 0), axis=1
    )
    owner_marks = (owners[:, None] == jnp.arange(owner_count)[None, :]).astype(jnp.int32)
    slot_rank = jnp.sum((jnp.cumsum(owner_marks, axis=0) - owner_marks) * owner_marks, axis=1)
    select = (
        (owners[None, None, :] == jnp.arange(owner_count)[:, None, None])
        & (slot_rank[None, None, :] == jnp.arange(capacity)[None, :, None])
    ).astype(bf16)
    outgoing = jnp.einsum("osr,rd->osd", select, slab, preferred_element_type=f32).astype(bf16)
    return lax.all_to_all(outgoing[:, None], "dp", split_axis=0, concat_axis=1, tiled=True)


def solution(mesh):
    in_specs = (
        P(("dp", "fsdp"), None, None),
        P(("dp", "fsdp")),
        P("dp"),
        P(),
        P(),
        P(),
        P("fsdp", None),
        P("fsdp", None),
        P("fsdp", None),
        P("fsdp", None),
    )
    out_specs = P("dp", None, None, "fsdp")
    return jax.shard_map(local, mesh=mesh, in_specs=in_specs, out_specs=out_specs, check_vma=False)
```

```python
import math

import jax
import jax.numpy as jnp
from jax import lax
from jax.experimental import pallas as pl
from jax.experimental.pallas import tpu as pltpu
from jax.sharding import PartitionSpec as P

HEADS = 16
KV_HEADS = 4
HEAD = 128
X = 4
Y_LO = 2
Z = 16
BOTH = ("dp", "fsdp")

bf16 = jnp.bfloat16
f32 = jnp.float32
VMEM = pl.BlockSpec(memory_space=pltpu.VMEM)
SMEM = pl.BlockSpec(memory_space=pltpu.SMEM)
HBM = pl.BlockSpec(memory_space=pltpu.HBM)


def dp_index(y_hi, x, core):
    return (y_hi * X + x) * 2 + core


def fsdp_index(y_lo, z):
    return y_lo * Z + z


Z_GROUPS = [[fsdp_index(yl, z) for z in range(Z)] for yl in range(Y_LO)]
X_GROUPS = [[dp_index(yh, x, c) for x in range(X)] for yh in range(2) for c in range(2)]
CORE_Z_GROUPS = [
    [dp_index(yh, x, c) * 32 + fsdp_index(yl, z) for c in range(2) for z in range(Z)]
    for yh in range(2)
    for x in range(X)
    for yl in range(Y_LO)
]
CROSS_SWAP = [
    (
        dp_index(yh, x, c) * 32 + fsdp_index(1 - c, z),
        dp_index(yh, x, 1 - c) * 32 + fsdp_index(c, z),
    )
    for yh in range(2)
    for x in range(X)
    for c in range(2)
    for z in range(Z)
]
CORE_SWAP = [(d, d ^ 1) for d in range(16)]
Y_LO_SWAP = [(i, i ^ Z) for i in range(32)]


def rope_tables(positions, head_width):
    halfway = head_width // 2
    frequency = 10000.0 ** (-jnp.arange(halfway, dtype=f32) * 2.0 / head_width)
    angles = positions.astype(f32)[..., None] * frequency
    cosine, sine = jnp.cos(angles), jnp.sin(angles)
    return (
        jnp.concatenate([cosine, cosine], axis=-1),
        jnp.concatenate([-sine, sine], axis=-1),
    )


def unit_body(place_ref, key_ref, value_ref, out_ref):
    core = place_ref[2]
    for k, w in enumerate((key_ref, value_ref)):
        columns = pl.multiple_of(core * 256, 256)
        out_ref[:, k * 256 : (k + 1) * 256] = w[:, pl.ds(columns, 256)]


def core_unit(place, w_key, w_value):
    return pl.pallas_call(
        unit_body,
        out_shape=jax.ShapeDtypeStruct((w_key.shape[0], 512), bf16),
        in_specs=[SMEM, VMEM, VMEM],
        out_specs=VMEM,
        compiler_params=pltpu.CompilerParams(vmem_limit_bytes=62 << 20),
        name="unit",
    )(place, w_key, w_value)


def pair_body(near_ref, far_ref, out_ref):
    out_ref[0] = near_ref[...]
    out_ref[1] = far_ref[...]


def pair(near, far):
    return pl.pallas_call(
        pair_body,
        out_shape=jax.ShapeDtypeStruct((2, *near.shape), bf16),
        in_specs=[VMEM, VMEM],
        out_specs=VMEM,
        compiler_params=pltpu.CompilerParams(vmem_limit_bytes=8 << 20),
        name="pair",
    )(near, far)


def open_body(place_ref, hidden, gain_ref, out_ref, block, sem):
    last, y_lo = place_ref[0], place_ref[3]
    first = pl.multiple_of((last >> 3) << 3, 8)
    copy = pltpu.make_async_copy(hidden.at[0, pl.ds(first, 8)], block, sem.at[0])
    copy.start()
    copy.wait()
    floats = block[...].astype(f32)
    pick = lax.broadcasted_iota(jnp.int32, floats.shape, 0) == (last & 7)
    row = jnp.sum(jnp.where(pick, floats, 0.0), axis=0, keepdims=True)
    normed = row * lax.rsqrt(jnp.mean(row * row, axis=-1, keepdims=True) + 1e-05) * gain_ref[...]
    normed = normed.astype(bf16).astype(f32)
    half = normed.shape[1] // 2
    place = lax.broadcasted_iota(jnp.int32, (8, HEAD), 0)
    near, far = (
        [jnp.where(y_lo == y, v[:, :half], v[:, half:]) for v in (normed, row)] for y in range(2)
    )
    for z in range(Z):
        tile = jnp.zeros((8, HEAD), f32)
        for n, v in enumerate((near[0], far[0], near[1], far[1])):
            tile = jnp.where(place == n, v[:, z * HEAD : (z + 1) * HEAD], tile)
        out_ref[z] = tile.astype(bf16)


def open_payload(place, hidden, gain):
    width = hidden.shape[2]
    return pl.pallas_call(
        open_body,
        out_shape=jax.ShapeDtypeStruct((Z, 8, HEAD), bf16),
        in_specs=[SMEM, HBM, VMEM],
        out_specs=VMEM,
        scratch_shapes=[pltpu.VMEM((8, width), bf16), pltpu.SemaphoreType.DMA((1,))],
        compiler_params=pltpu.CompilerParams(vmem_limit_bytes=62 << 20),
        name="open",
    )(place, hidden, gain[None, :])


ROWS = 24
WEIGHT_ROW = 16


def query_body(place_ref, arrived_ref, near_ref, far_ref, w_out_ref, out_ref, parts):
    x, core = place_ref[1], place_ref[2]
    rows = w_out_ref[...].astype(f32)
    weight = rows[:8]
    for n in range(1, 2 * X):
        weight = jnp.where(core * X + x == n, rows[n * 8 : n * 8 + 8], weight)
    weight = weight.astype(bf16)
    features = arrived_ref[...].astype(f32)
    total = jnp.dot(
        features[:, 0, :].astype(bf16), near_ref[...], preferred_element_type=f32
    ) + jnp.dot(features[:, 1, :].astype(bf16), far_ref[...], preferred_element_type=f32)
    high = total.astype(bf16).astype(f32)
    low = total - high
    for h in range(HEADS):
        c, cut = h // 8, slice(h * HEAD, (h + 1) * HEAD)
        parts[c * Z : (c + 1) * Z, h % 8, :] = high[:, cut]
        parts[c * Z : (c + 1) * Z, 8 + h % 8, :] = low[:, cut]
    out_ref[:, :WEIGHT_ROW, :] = parts[...].astype(bf16)
    for n in range(2 * Z):
        out_ref[n, WEIGHT_ROW:, :] = weight[:, n * HEAD : (n + 1) * HEAD]


def query_payload(place, arrived, near, far, w_out):
    return pl.pallas_call(
        query_body,
        out_shape=jax.ShapeDtypeStruct((2 * Z, ROWS, HEAD), bf16),
        in_specs=[SMEM, VMEM, VMEM, VMEM, VMEM],
        out_specs=VMEM,
        scratch_shapes=[pltpu.VMEM((2 * Z, 16, HEAD), f32)],
        compiler_params=pltpu.CompilerParams(vmem_limit_bytes=12 << 20),
        name="query",
    )(place, arrived, near, far, w_out)


def attend_body(
    place_ref, len_ref, normed_ref, other_ref, cos_ref, sin_ref, parts, gathered, out_ref, w_ref, q_ref, sem, q_sem
):
    fetch = pltpu.make_async_copy(parts.at[:, pl.ds(0, 16), :], q_ref, q_sem.at[0])
    fetch.start()
    core, y_lo = place_ref[2], place_ref[3]
    copies = [
        [
            pltpu.make_async_copy(
                gathered.at[:, n, :, pl.ds(kind * 256, 256)],
                w_ref.at[kind, y_lo if n == 0 else 1 - y_lo],
                sem.at[kind, n],
            )
            for n in range(2)
        ]
        for kind in range(2)
    ]
    for copy in copies[0] + copies[1]:
        copy.start()
    cosine, sine = cos_ref[...], sin_ref[...]
    fetch.wait()
    by_core = [jnp.sum(q_ref[c * Z : (c + 1) * Z].astype(f32), axis=0) for c in range(2)]
    by_core = [both[:8] + both[8:] for both in by_core]
    queries = []
    for p in range(2):
        summed = jnp.where(core == p, by_core[0], by_core[1])
        last = len_ref[p] - 1
        turned = summed * cos_ref[pl.ds(last, 1), :] + pltpu.roll(summed, HEAD // 2, 1) * sin_ref[
            pl.ds(last, 1), :
        ]
        queries.append((turned * (1.0 / math.sqrt(HEAD))).astype(bf16))
    for copy in copies[0]:
        copy.wait()
    weight = w_ref[0].reshape(Y_LO * Z * HEAD, 256)
    sums = []
    for p, rows_ref in enumerate((normed_ref, other_ref)):
        rows = rows_ref[...]
        keys = jnp.dot(rows, weight, preferred_element_type=f32)
        scores = []
        for g in range(2):
            part = keys[:, g * HEAD : (g + 1) * HEAD]
            turned = (part * cosine + pltpu.roll(part, HEAD // 2, 1) * sine).astype(bf16)
            scores.append(
                lax.dot_general(
                    queries[p], turned, (((1,), (1,)), ((), ())), preferred_element_type=f32
                )
            )
        head = lax.broadcasted_iota(jnp.int32, scores[0].shape, 0)
        place = lax.broadcasted_iota(jnp.int32, scores[0].shape, 1)
        scores = jnp.where(head < 4, scores[0], scores[1])
        scores = jnp.where(place < len_ref[p], scores, -jnp.inf)
        powers = jnp.exp(scores - jnp.max(scores, axis=-1, keepdims=True))
        weights = (powers / jnp.sum(powers, axis=-1, keepdims=True)).astype(bf16)
        sums.append(jnp.dot(weights, rows, preferred_element_type=f32))
    u = jnp.concatenate(sums, axis=0)
    first = u.astype(bf16)
    rest = u - first.astype(f32)
    second = rest.astype(bf16)
    third = (rest - second.astype(f32)).astype(bf16)
    for copy in copies[1]:
        copy.wait()
    weight = w_ref[1].reshape(Y_LO * Z * HEAD, 256)
    stacked = jnp.dot(
        jnp.concatenate([third, second, first], axis=0), weight, preferred_element_type=f32
    )
    total = stacked[:16] + stacked[16:32] + stacked[32:]
    head = lax.broadcasted_iota(jnp.int32, (16, HEAD), 0)
    context = jnp.where((head & 7) < 4, total[:, :HEAD], total[:, HEAD:])
    turned = jnp.concatenate([context[8:], context[:8]], axis=0)
    context = jnp.where(core == 0, context, turned).astype(bf16)
    out_ref[...] = jnp.broadcast_to(context[None], out_ref.shape)


def attend(place, lengths, normed, other, cosine, sine, parts, gathered):
    return pl.pallas_call(
        attend_body,
        out_shape=jax.ShapeDtypeStruct((2 * Z, 16, HEAD), bf16),
        in_specs=[SMEM, SMEM, VMEM, VMEM, VMEM, VMEM, HBM, HBM],
        out_specs=VMEM,
        scratch_shapes=[
            pltpu.VMEM((2, Y_LO, Z, HEAD, 256), bf16),
            pltpu.VMEM((2 * Z, 16, HEAD), bf16),
            pltpu.SemaphoreType.DMA((2, 2)),
            pltpu.SemaphoreType.DMA((1,)),
        ],
        compiler_params=pltpu.CompilerParams(vmem_limit_bytes=48 << 20),
        name="attend",
    )(place, lengths, normed, other, cosine, sine, parts, gathered)


def local(
    hidden, lengths, list_ids, list_owner, attn_gain, final_gain, w_query, w_key, w_value, w_out
):
    _, seq_len, width = hidden.shape
    dp, fsdp = lax.axis_index("dp"), lax.axis_index("fsdp")
    core, x = dp & 1, (dp >> 1) & (X - 1)
    y_lo = fsdp >> 4
    place = jnp.stack([lengths[0] - 1, x, core, y_lo]).astype(jnp.int32)

    unit = core_unit(place, w_key, w_value)
    units = pair(unit, lax.ppermute(unit, "fsdp", Y_LO_SWAP))
    gathered = lax.all_gather(units, "fsdp", axis=0, tiled=False, axis_index_groups=Z_GROUPS)

    unit, hidden = lax.optimization_barrier((unit, hidden))
    outgoing = open_payload(place, hidden, attn_gain)
    units, outgoing = lax.optimization_barrier((units, outgoing))
    arrived = lax.all_to_all(outgoing, "fsdp", 0, 0, tiled=True, axis_index_groups=Z_GROUPS)
    w_query_other = lax.ppermute(w_query, "fsdp", Y_LO_SWAP)

    payload = query_payload(place, arrived, w_query, w_query_other, w_out)
    parts = lax.all_to_all(payload, BOTH, 0, 0, tiled=True, axis_index_groups=CORE_Z_GROUPS)

    rows, lengths, parts = lax.optimization_barrier((hidden[0], lengths, parts))
    both_lengths = jnp.concatenate([lengths, lax.ppermute(lengths, "dp", CORE_SWAP)])
    floats = rows.astype(f32)
    normed = (
        floats * lax.rsqrt(jnp.mean(floats * floats, axis=-1, keepdims=True) + 1e-05) * attn_gain
    ).astype(bf16)
    other = lax.ppermute(normed, "dp", CORE_SWAP)
    cosine, sine = rope_tables(jnp.arange(seq_len), HEAD)

    weight = lax.all_gather(
        parts[:, WEIGHT_ROW:], "dp", axis=0, tiled=False, axis_index_groups=X_GROUPS
    ).reshape(X, 2, Z, 8, HEAD)
    weight = jnp.transpose(weight, (2, 1, 0, 3, 4)).reshape(2 * Z * 32, HEAD)
    weight = jnp.where(core == y_lo, weight, lax.ppermute(weight, BOTH, CROSS_SWAP))
    near, far = arrived[:, 2], lax.ppermute(arrived[:, 3], "fsdp", Y_LO_SWAP)
    inputs = jnp.concatenate([jnp.where(y_lo == 0, near, far), jnp.where(y_lo == 0, far, near)])
    inputs = inputs.astype(f32)
    gain = lax.dynamic_slice(final_gain, (fsdp * HEAD,), (HEAD,))

    owner_count = lax.axis_size("dp")
    capacity = 4
    list_index = jnp.arange(list_owner.shape[0])
    owners = jnp.sum(
        jnp.where(list_ids[:, None] == list_index[None, :], list_owner[None, :], 0), axis=1
    )
    owner_marks = (owners[:, None] == jnp.arange(owner_count)[None, :]).astype(jnp.int32)
    slot_rank = jnp.sum((jnp.cumsum(owner_marks, axis=0) - owner_marks) * owner_marks, axis=1)
    select = (
        (owners[None, None, :] == jnp.arange(owner_count)[:, None, None])
        & (slot_rank[None, None, :] == jnp.arange(capacity)[None, :, None])
    ).astype(bf16)

    (
        gathered, weight, both_lengths, normed, other, cosine, sine, inputs, gain, select
    ) = lax.optimization_barrier(
        (gathered, weight, both_lengths, normed, other, cosine, sine, inputs, gain, select)
    )
    context = attend(place, both_lengths, normed, other, cosine, sine, parts, gathered)
    contexts = lax.all_to_all(context, "fsdp", 0, 0, tiled=True)

    slabs = width // HEAD
    contexts = contexts.reshape(slabs, 2, 8 * HEAD)
    halves = jnp.einsum("sad,dn->asn", contexts, weight, preferred_element_type=f32)
    kept = lax.dynamic_index_in_dim(halves, core, 0, keepdims=False)
    given = lax.dynamic_index_in_dim(halves, 1 - core, 0, keepdims=False)
    residual = inputs + (kept + lax.ppermute(given, "dp", CORE_SWAP))
    scaled = residual * gain
    partial = jnp.sum(scaled * scaled, axis=-1)
    squares = lax.all_to_all(
        jnp.broadcast_to(partial[None, None, :], (slabs, 1, slabs)), "fsdp", 0, 0, tiled=True
    )
    mean = jnp.sum(squares, axis=0)[0] / width
    slab = (scaled * lax.rsqrt(mean + 1e-06)[:, None]).astype(bf16)

    outgoing = jnp.einsum("osr,rd->osd", select, slab, preferred_element_type=f32).astype(bf16)
    return lax.all_to_all(outgoing[:, None], "dp", split_axis=0, concat_axis=1, tiled=True)


def solution(mesh):
    in_specs = (
        P(("dp", "fsdp"), None, None),
        P(("dp", "fsdp")),
        P("dp"),
        P(),
        P(),
        P(),
        P("fsdp", None),
        P("fsdp", None),
        P("fsdp", None),
        P("fsdp", None),
    )
    out_specs = P("dp", None, None, "fsdp")
    return jax.shard_map(local, mesh=mesh, in_specs=in_specs, out_specs=out_specs, check_vma=False)
```

```python
import math

import jax
import jax.numpy as jnp
from jax import lax
from jax.experimental import pallas as pl
from jax.experimental.pallas import tpu as pltpu
from jax.sharding import PartitionSpec as P

HEADS = 16
KV_HEADS = 4
HEAD = 128
X = 4
Y_LO = 2
Z = 16
BOTH = ("dp", "fsdp")

bf16 = jnp.bfloat16
f32 = jnp.float32
VMEM = pl.BlockSpec(memory_space=pltpu.VMEM)
SMEM = pl.BlockSpec(memory_space=pltpu.SMEM)
HBM = pl.BlockSpec(memory_space=pltpu.HBM)


def dp_index(y_hi, x, core):
    return (y_hi * X + x) * 2 + core


def fsdp_index(y_lo, z):
    return y_lo * Z + z


Z_GROUPS = [[fsdp_index(yl, z) for z in range(Z)] for yl in range(Y_LO)]
X_GROUPS = [[dp_index(yh, x, c) for x in range(X)] for yh in range(2) for c in range(2)]
CORE_Z_GROUPS = [
    [dp_index(yh, x, c) * 32 + fsdp_index(yl, z) for c in range(2) for z in range(Z)]
    for yh in range(2)
    for x in range(X)
    for yl in range(Y_LO)
]
CROSS_SWAP = [
    (
        dp_index(yh, x, c) * 32 + fsdp_index(1 - c, z),
        dp_index(yh, x, 1 - c) * 32 + fsdp_index(c, z),
    )
    for yh in range(2)
    for x in range(X)
    for c in range(2)
    for z in range(Z)
]
CORE_SWAP = [(d, d ^ 1) for d in range(16)]
Y_LO_SWAP = [(i, i ^ Z) for i in range(32)]


def rope_tables(positions, head_width):
    halfway = head_width // 2
    frequency = 10000.0 ** (-jnp.arange(halfway, dtype=f32) * 2.0 / head_width)
    angles = positions.astype(f32)[..., None] * frequency
    cosine, sine = jnp.cos(angles), jnp.sin(angles)
    return (
        jnp.concatenate([cosine, cosine], axis=-1),
        jnp.concatenate([-sine, sine], axis=-1),
    )


def unit_body(place_ref, key_ref, value_ref, out_ref):
    core = place_ref[2]
    for k, w in enumerate((key_ref, value_ref)):
        columns = pl.multiple_of(core * 256, 256)
        out_ref[:, k * 256 : (k + 1) * 256] = w[:, pl.ds(columns, 256)]


def core_unit(place, w_key, w_value):
    return pl.pallas_call(
        unit_body,
        out_shape=jax.ShapeDtypeStruct((w_key.shape[0], 512), bf16),
        in_specs=[SMEM, VMEM, VMEM],
        out_specs=VMEM,
        compiler_params=pltpu.CompilerParams(vmem_limit_bytes=62 << 20),
        name="unit",
    )(place, w_key, w_value)


def pair_body(near_ref, far_ref, out_ref):
    out_ref[0] = near_ref[...]
    out_ref[1] = far_ref[...]


def pair(near, far):
    return pl.pallas_call(
        pair_body,
        out_shape=jax.ShapeDtypeStruct((2, *near.shape), bf16),
        in_specs=[VMEM, VMEM],
        out_specs=VMEM,
        compiler_params=pltpu.CompilerParams(vmem_limit_bytes=62 << 20),
        name="pair",
    )(near, far)


def open_body(place_ref, hidden, gain_ref, out_ref, block, sem):
    last, y_lo = place_ref[0], place_ref[3]
    first = pl.multiple_of((last >> 3) << 3, 8)
    copy = pltpu.make_async_copy(hidden.at[0, pl.ds(first, 8)], block, sem.at[0])
    copy.start()
    copy.wait()
    floats = block[...].astype(f32)
    pick = lax.broadcasted_iota(jnp.int32, floats.shape, 0) == (last & 7)
    row = jnp.sum(jnp.where(pick, floats, 0.0), axis=0, keepdims=True)
    normed = row * lax.rsqrt(jnp.mean(row * row, axis=-1, keepdims=True) + 1e-05) * gain_ref[...]
    normed = normed.astype(bf16).astype(f32)
    half = normed.shape[1] // 2
    place = lax.broadcasted_iota(jnp.int32, (8, HEAD), 0)
    near, far = (
        [jnp.where(y_lo == y, v[:, :half], v[:, half:]) for v in (normed, row)] for y in range(2)
    )
    for z in range(Z):
        tile = jnp.zeros((8, HEAD), f32)
        for n, v in enumerate((near[0], far[0], near[1], far[1])):
            tile = jnp.where(place == n, v[:, z * HEAD : (z + 1) * HEAD], tile)
        out_ref[z] = tile.astype(bf16)


def open_payload(place, hidden, gain):
    width = hidden.shape[2]
    return pl.pallas_call(
        open_body,
        out_shape=jax.ShapeDtypeStruct((Z, 8, HEAD), bf16),
        in_specs=[SMEM, HBM, VMEM],
        out_specs=VMEM,
        scratch_shapes=[pltpu.VMEM((8, width), bf16), pltpu.SemaphoreType.DMA((1,))],
        compiler_params=pltpu.CompilerParams(vmem_limit_bytes=62 << 20),
        name="open",
    )(place, hidden, gain[None, :])


ROWS = 24
WEIGHT_ROW = 16


def query_body(place_ref, arrived_ref, near_ref, far_ref, w_out_ref, out_ref, parts):
    x, core = place_ref[1], place_ref[2]
    rows = w_out_ref[...].astype(f32)
    weight = rows[:8]
    for n in range(1, 2 * X):
        weight = jnp.where(core * X + x == n, rows[n * 8 : n * 8 + 8], weight)
    weight = weight.astype(bf16)
    features = arrived_ref[...].astype(f32)
    total = jnp.dot(
        features[:, 0, :].astype(bf16), near_ref[...], preferred_element_type=f32
    ) + jnp.dot(features[:, 1, :].astype(bf16), far_ref[...], preferred_element_type=f32)
    high = total.astype(bf16).astype(f32)
    low = total - high
    for h in range(HEADS):
        c, cut = h // 8, slice(h * HEAD, (h + 1) * HEAD)
        parts[c * Z : (c + 1) * Z, h % 8, :] = high[:, cut]
        parts[c * Z : (c + 1) * Z, 8 + h % 8, :] = low[:, cut]
    out_ref[:, :WEIGHT_ROW, :] = parts[...].astype(bf16)
    for n in range(2 * Z):
        out_ref[n, WEIGHT_ROW:, :] = weight[:, n * HEAD : (n + 1) * HEAD]


def query_payload(place, arrived, near, far, w_out):
    return pl.pallas_call(
        query_body,
        out_shape=jax.ShapeDtypeStruct((2 * Z, ROWS, HEAD), bf16),
        in_specs=[SMEM, VMEM, VMEM, VMEM, VMEM],
        out_specs=VMEM,
        scratch_shapes=[pltpu.VMEM((2 * Z, 16, HEAD), f32)],
        compiler_params=pltpu.CompilerParams(vmem_limit_bytes=62 << 20),
        name="query",
    )(place, arrived, near, far, w_out)


def attend_body(
    place_ref, len_ref, normed_ref, other_ref, cos_ref, sin_ref, parts, gathered, out_ref, w_ref, q_ref, sem, q_sem
):
    fetch = pltpu.make_async_copy(parts.at[:, pl.ds(0, 16), :], q_ref, q_sem.at[0])
    fetch.start()
    core, y_lo = place_ref[2], place_ref[3]
    copies = [
        [
            pltpu.make_async_copy(
                gathered.at[:, n, :, pl.ds(kind * 256, 256)],
                w_ref.at[kind, y_lo if n == 0 else 1 - y_lo],
                sem.at[kind, n],
            )
            for n in range(2)
        ]
        for kind in range(2)
    ]
    for copy in copies[0] + copies[1]:
        copy.start()
    cosine, sine = cos_ref[...], sin_ref[...]
    fetch.wait()
    by_core = [jnp.sum(q_ref[c * Z : (c + 1) * Z].astype(f32), axis=0) for c in range(2)]
    by_core = [both[:8] + both[8:] for both in by_core]
    queries = []
    for p in range(2):
        summed = jnp.where(core == p, by_core[0], by_core[1])
        last = len_ref[p] - 1
        turned = summed * cos_ref[pl.ds(last, 1), :] + pltpu.roll(summed, HEAD // 2, 1) * sin_ref[
            pl.ds(last, 1), :
        ]
        queries.append((turned * (1.0 / math.sqrt(HEAD))).astype(bf16))
    for copy in copies[0]:
        copy.wait()
    weight = w_ref[0].reshape(Y_LO * Z * HEAD, 256)
    sums = []
    for p, rows_ref in enumerate((normed_ref, other_ref)):
        rows = rows_ref[...]
        keys = jnp.dot(rows, weight, preferred_element_type=f32)
        scores = []
        for g in range(2):
            part = keys[:, g * HEAD : (g + 1) * HEAD]
            turned = (part * cosine + pltpu.roll(part, HEAD // 2, 1) * sine).astype(bf16)
            scores.append(
                lax.dot_general(
                    queries[p], turned, (((1,), (1,)), ((), ())), preferred_element_type=f32
                )
            )
        head = lax.broadcasted_iota(jnp.int32, scores[0].shape, 0)
        place = lax.broadcasted_iota(jnp.int32, scores[0].shape, 1)
        scores = jnp.where(head < 4, scores[0], scores[1])
        scores = jnp.where(place < len_ref[p], scores, -jnp.inf)
        powers = jnp.exp(scores - jnp.max(scores, axis=-1, keepdims=True))
        weights = (powers / jnp.sum(powers, axis=-1, keepdims=True)).astype(bf16)
        sums.append(jnp.dot(weights, rows, preferred_element_type=f32))
    u = jnp.concatenate(sums, axis=0)
    first = u.astype(bf16)
    rest = u - first.astype(f32)
    second = rest.astype(bf16)
    third = (rest - second.astype(f32)).astype(bf16)
    for copy in copies[1]:
        copy.wait()
    weight = w_ref[1].reshape(Y_LO * Z * HEAD, 256)
    stacked = jnp.dot(
        jnp.concatenate([third, second, first], axis=0), weight, preferred_element_type=f32
    )
    total = stacked[:16] + stacked[16:32] + stacked[32:]
    head = lax.broadcasted_iota(jnp.int32, (16, HEAD), 0)
    context = jnp.where((head & 7) < 4, total[:, :HEAD], total[:, HEAD:])
    turned = jnp.concatenate([context[8:], context[:8]], axis=0)
    context = jnp.where(core == 0, context, turned).astype(bf16)
    out_ref[...] = jnp.broadcast_to(context[None], out_ref.shape)


def attend(place, lengths, normed, other, cosine, sine, parts, gathered):
    return pl.pallas_call(
        attend_body,
        out_shape=jax.ShapeDtypeStruct((2 * Z, 16, HEAD), bf16),
        in_specs=[SMEM, SMEM, VMEM, VMEM, VMEM, VMEM, HBM, HBM],
        out_specs=VMEM,
        scratch_shapes=[
            pltpu.VMEM((2, Y_LO, Z, HEAD, 256), bf16),
            pltpu.VMEM((2 * Z, 16, HEAD), bf16),
            pltpu.SemaphoreType.DMA((2, 2)),
            pltpu.SemaphoreType.DMA((1,)),
        ],
        compiler_params=pltpu.CompilerParams(vmem_limit_bytes=48 << 20),
        name="attend",
    )(place, lengths, normed, other, cosine, sine, parts, gathered)


def local(
    hidden, lengths, list_ids, list_owner, attn_gain, final_gain, w_query, w_key, w_value, w_out
):
    _, seq_len, width = hidden.shape
    dp, fsdp = lax.axis_index("dp"), lax.axis_index("fsdp")
    core, x = dp & 1, (dp >> 1) & (X - 1)
    y_lo = fsdp >> 4
    place = jnp.stack([lengths[0] - 1, x, core, y_lo]).astype(jnp.int32)

    unit = core_unit(place, w_key, w_value)
    units = pair(unit, lax.ppermute(unit, "fsdp", Y_LO_SWAP))
    gathered = lax.all_gather(units, "fsdp", axis=0, tiled=False, axis_index_groups=Z_GROUPS)

    unit, hidden = lax.optimization_barrier((unit, hidden))
    outgoing = open_payload(place, hidden, attn_gain)
    units, outgoing = lax.optimization_barrier((units, outgoing))
    arrived = lax.all_to_all(outgoing, "fsdp", 0, 0, tiled=True, axis_index_groups=Z_GROUPS)
    w_query_other = lax.ppermute(w_query, "fsdp", Y_LO_SWAP)

    payload = query_payload(place, arrived, w_query, w_query_other, w_out)
    parts = lax.all_to_all(payload, BOTH, 0, 0, tiled=True, axis_index_groups=CORE_Z_GROUPS)

    both_lengths = jnp.concatenate([lengths, lax.ppermute(lengths, "dp", CORE_SWAP)])
    rows, _ = lax.optimization_barrier((hidden[0], payload))

    def norm(values):
        floats = values.astype(f32)
        return (
            floats * lax.rsqrt(jnp.mean(floats * floats, axis=-1, keepdims=True) + 1e-05) * attn_gain
        ).astype(bf16)

    normed, other = norm(rows), norm(lax.ppermute(rows, "dp", CORE_SWAP))
    parts, normed, other = lax.optimization_barrier((parts, normed, other))
    cosine, sine = rope_tables(jnp.arange(seq_len), HEAD)

    weight = lax.all_gather(
        parts[:, WEIGHT_ROW:], "dp", axis=0, tiled=False, axis_index_groups=X_GROUPS
    ).reshape(X, 2, Z, 8, HEAD)
    weight = jnp.transpose(weight, (2, 1, 0, 3, 4)).reshape(2 * Z * 32, HEAD)
    weight = jnp.where(core == y_lo, weight, lax.ppermute(weight, BOTH, CROSS_SWAP))
    near, far = arrived[:, 2], lax.ppermute(arrived[:, 3], "fsdp", Y_LO_SWAP)
    inputs = jnp.concatenate([jnp.where(y_lo == 0, near, far), jnp.where(y_lo == 0, far, near)])
    inputs = inputs.astype(f32)
    gain = lax.dynamic_slice(final_gain, (fsdp * HEAD,), (HEAD,))

    owner_count = lax.axis_size("dp")
    capacity = 4
    list_index = jnp.arange(list_owner.shape[0])
    owners = jnp.sum(
        jnp.where(list_ids[:, None] == list_index[None, :], list_owner[None, :], 0), axis=1
    )
    owner_marks = (owners[:, None] == jnp.arange(owner_count)[None, :]).astype(jnp.int32)
    slot_rank = jnp.sum((jnp.cumsum(owner_marks, axis=0) - owner_marks) * owner_marks, axis=1)
    select = (
        (owners[None, None, :] == jnp.arange(owner_count)[:, None, None])
        & (slot_rank[None, None, :] == jnp.arange(capacity)[None, :, None])
    ).astype(bf16)

    (
        gathered, weight, both_lengths, normed, other, cosine, sine, inputs, gain, select
    ) = lax.optimization_barrier(
        (gathered, weight, both_lengths, normed, other, cosine, sine, inputs, gain, select)
    )
    context = attend(place, both_lengths, normed, other, cosine, sine, parts, gathered)
    contexts = lax.all_to_all(context, "fsdp", 0, 0, tiled=True)

    slabs = width // HEAD
    contexts = contexts.reshape(slabs, 2, 8 * HEAD)
    halves = jnp.einsum("sad,dn->asn", contexts, weight, preferred_element_type=f32)
    kept = lax.dynamic_index_in_dim(halves, core, 0, keepdims=False)
    given = lax.dynamic_index_in_dim(halves, 1 - core, 0, keepdims=False)
    residual = inputs + (kept + lax.ppermute(given, "dp", CORE_SWAP))
    scaled = residual * gain
    partial = jnp.sum(scaled * scaled, axis=-1)
    squares = lax.all_to_all(
        jnp.broadcast_to(partial[None, None, :], (slabs, 1, slabs)), "fsdp", 0, 0, tiled=True
    )
    mean = jnp.sum(squares, axis=0)[0] / width
    slab = (scaled * lax.rsqrt(mean + 1e-06)[:, None]).astype(bf16)

    outgoing = jnp.einsum("osr,rd->osd", select, slab, preferred_element_type=f32).astype(bf16)
    return lax.all_to_all(outgoing[:, None], "dp", split_axis=0, concat_axis=1, tiled=True)


def solution(mesh):
    in_specs = (
        P(("dp", "fsdp"), None, None),
        P(("dp", "fsdp")),
        P("dp"),
        P(),
        P(),
        P(),
        P("fsdp", None),
        P("fsdp", None),
        P("fsdp", None),
        P("fsdp", None),
    )
    out_specs = P("dp", None, None, "fsdp")
    return jax.shard_map(local, mesh=mesh, in_specs=in_specs, out_specs=out_specs, check_vma=False)
```

```python
import math

import jax
import jax.numpy as jnp
from jax import lax
from jax.experimental import pallas as pl
from jax.experimental.pallas import tpu as pltpu
from jax.sharding import PartitionSpec as P

HEADS = 16
KV_HEADS = 4
HEAD = 128
X = 4
Y_LO = 2
Z = 16
BOTH = ("dp", "fsdp")

bf16 = jnp.bfloat16
f32 = jnp.float32
VMEM = pl.BlockSpec(memory_space=pltpu.VMEM)
SMEM = pl.BlockSpec(memory_space=pltpu.SMEM)
HBM = pl.BlockSpec(memory_space=pltpu.HBM)


def dp_index(y_hi, x, core):
    return (y_hi * X + x) * 2 + core


def fsdp_index(y_lo, z):
    return y_lo * Z + z


Z_GROUPS = [[fsdp_index(yl, z) for z in range(Z)] for yl in range(Y_LO)]
X_GROUPS = [[dp_index(yh, x, c) for x in range(X)] for yh in range(2) for c in range(2)]
CORE_Z_GROUPS = [
    [dp_index(yh, x, c) * 32 + fsdp_index(yl, z) for c in range(2) for z in range(Z)]
    for yh in range(2)
    for x in range(X)
    for yl in range(Y_LO)
]
CROSS_SWAP = [
    (
        dp_index(yh, x, c) * 32 + fsdp_index(1 - c, z),
        dp_index(yh, x, 1 - c) * 32 + fsdp_index(c, z),
    )
    for yh in range(2)
    for x in range(X)
    for c in range(2)
    for z in range(Z)
]
CORE_SWAP = [(d, d ^ 1) for d in range(16)]
Y_LO_SWAP = [(i, i ^ Z) for i in range(32)]


def rope_tables(positions, head_width):
    halfway = head_width // 2
    frequency = 10000.0 ** (-jnp.arange(halfway, dtype=f32) * 2.0 / head_width)
    angles = positions.astype(f32)[..., None] * frequency
    cosine, sine = jnp.cos(angles), jnp.sin(angles)
    return (
        jnp.concatenate([cosine, cosine], axis=-1),
        jnp.concatenate([-sine, sine], axis=-1),
    )


def unit_body(place_ref, key_ref, value_ref, out_ref):
    core = place_ref[2]
    for k, w in enumerate((key_ref, value_ref)):
        columns = pl.multiple_of(core * 256, 256)
        out_ref[:, k * 256 : (k + 1) * 256] = w[:, pl.ds(columns, 256)]


def core_unit(place, w_key, w_value):
    return pl.pallas_call(
        unit_body,
        out_shape=jax.ShapeDtypeStruct((w_key.shape[0], 512), bf16),
        in_specs=[SMEM, VMEM, VMEM],
        out_specs=VMEM,
        compiler_params=pltpu.CompilerParams(vmem_limit_bytes=62 << 20),
        name="unit",
    )(place, w_key, w_value)


def pair_body(near_ref, far_ref, out_ref):
    out_ref[0] = near_ref[...]
    out_ref[1] = far_ref[...]


def pair(near, far):
    return pl.pallas_call(
        pair_body,
        out_shape=jax.ShapeDtypeStruct((2, *near.shape), bf16),
        in_specs=[VMEM, VMEM],
        out_specs=VMEM,
        compiler_params=pltpu.CompilerParams(vmem_limit_bytes=8 << 20),
        name="pair",
    )(near, far)


def open_body(place_ref, hidden, gain_ref, out_ref, block, sem):
    last, y_lo = place_ref[0], place_ref[3]
    first = pl.multiple_of((last >> 3) << 3, 8)
    copy = pltpu.make_async_copy(hidden.at[0, pl.ds(first, 8)], block, sem.at[0])
    copy.start()
    copy.wait()
    floats = block[...].astype(f32)
    pick = lax.broadcasted_iota(jnp.int32, floats.shape, 0) == (last & 7)
    row = jnp.sum(jnp.where(pick, floats, 0.0), axis=0, keepdims=True)
    normed = row * lax.rsqrt(jnp.mean(row * row, axis=-1, keepdims=True) + 1e-05) * gain_ref[...]
    normed = normed.astype(bf16).astype(f32)
    half = normed.shape[1] // 2
    place = lax.broadcasted_iota(jnp.int32, (8, HEAD), 0)
    near, far = (
        [jnp.where(y_lo == y, v[:, :half], v[:, half:]) for v in (normed, row)] for y in range(2)
    )
    for z in range(Z):
        tile = jnp.zeros((8, HEAD), f32)
        for n, v in enumerate((near[0], far[0], near[1], far[1])):
            tile = jnp.where(place == n, v[:, z * HEAD : (z + 1) * HEAD], tile)
        out_ref[z] = tile.astype(bf16)


def open_payload(place, hidden, gain):
    width = hidden.shape[2]
    return pl.pallas_call(
        open_body,
        out_shape=jax.ShapeDtypeStruct((Z, 8, HEAD), bf16),
        in_specs=[SMEM, HBM, VMEM],
        out_specs=VMEM,
        scratch_shapes=[pltpu.VMEM((8, width), bf16), pltpu.SemaphoreType.DMA((1,))],
        compiler_params=pltpu.CompilerParams(vmem_limit_bytes=62 << 20),
        name="open",
    )(place, hidden, gain[None, :])


ROWS = 24
WEIGHT_ROW = 16


def query_body(place_ref, arrived_ref, near_ref, far_ref, w_out_ref, out_ref, parts):
    x, core = place_ref[1], place_ref[2]
    rows = w_out_ref[...].astype(f32)
    weight = rows[:8]
    for n in range(1, 2 * X):
        weight = jnp.where(core * X + x == n, rows[n * 8 : n * 8 + 8], weight)
    weight = weight.astype(bf16)
    features = arrived_ref[...].astype(f32)
    total = jnp.dot(
        features[:, 0, :].astype(bf16), near_ref[...], preferred_element_type=f32
    ) + jnp.dot(features[:, 1, :].astype(bf16), far_ref[...], preferred_element_type=f32)
    high = total.astype(bf16).astype(f32)
    low = total - high
    for h in range(HEADS):
        c, cut = h // 8, slice(h * HEAD, (h + 1) * HEAD)
        parts[c * Z : (c + 1) * Z, h % 8, :] = high[:, cut]
        parts[c * Z : (c + 1) * Z, 8 + h % 8, :] = low[:, cut]
    out_ref[:, :WEIGHT_ROW, :] = parts[...].astype(bf16)
    for n in range(2 * Z):
        out_ref[n, WEIGHT_ROW:, :] = weight[:, n * HEAD : (n + 1) * HEAD]


def query_payload(place, arrived, near, far, w_out):
    return pl.pallas_call(
        query_body,
        out_shape=jax.ShapeDtypeStruct((2 * Z, ROWS, HEAD), bf16),
        in_specs=[SMEM, VMEM, VMEM, VMEM, VMEM],
        out_specs=VMEM,
        scratch_shapes=[pltpu.VMEM((2 * Z, 16, HEAD), f32)],
        compiler_params=pltpu.CompilerParams(vmem_limit_bytes=12 << 20),
        name="query",
    )(place, arrived, near, far, w_out)


def attend_body(
    place_ref, len_ref, normed_ref, other_ref, cos_ref, sin_ref, parts, gathered, out_ref, w_ref, q_ref, sem, q_sem
):
    fetch = pltpu.make_async_copy(parts.at[:, pl.ds(0, 16), :], q_ref, q_sem.at[0])
    fetch.start()
    core, y_lo = place_ref[2], place_ref[3]
    copies = [
        [
            pltpu.make_async_copy(
                gathered.at[:, n, :, pl.ds(kind * 256, 256)],
                w_ref.at[kind, y_lo if n == 0 else 1 - y_lo],
                sem.at[kind, n],
            )
            for n in range(2)
        ]
        for kind in range(2)
    ]
    for copy in copies[0] + copies[1]:
        copy.start()
    cosine, sine = cos_ref[...], sin_ref[...]
    fetch.wait()
    by_core = [jnp.sum(q_ref[c * Z : (c + 1) * Z].astype(f32), axis=0) for c in range(2)]
    by_core = [both[:8] + both[8:] for both in by_core]
    queries = []
    for p in range(2):
        summed = jnp.where(core == p, by_core[0], by_core[1])
        last = len_ref[p] - 1
        turned = summed * cos_ref[pl.ds(last, 1), :] + pltpu.roll(summed, HEAD // 2, 1) * sin_ref[
            pl.ds(last, 1), :
        ]
        queries.append((turned * (1.0 / math.sqrt(HEAD))).astype(bf16))
    for copy in copies[0]:
        copy.wait()
    weight = w_ref[0].reshape(Y_LO * Z * HEAD, 256)
    sums = []
    for p, rows_ref in enumerate((normed_ref, other_ref)):
        rows = rows_ref[...]
        keys = jnp.dot(rows, weight, preferred_element_type=f32)
        scores = []
        for g in range(2):
            part = keys[:, g * HEAD : (g + 1) * HEAD]
            turned = (part * cosine + pltpu.roll(part, HEAD // 2, 1) * sine).astype(bf16)
            scores.append(
                lax.dot_general(
                    queries[p], turned, (((1,), (1,)), ((), ())), preferred_element_type=f32
                )
            )
        head = lax.broadcasted_iota(jnp.int32, scores[0].shape, 0)
        place = lax.broadcasted_iota(jnp.int32, scores[0].shape, 1)
        scores = jnp.where(head < 4, scores[0], scores[1])
        scores = jnp.where(place < len_ref[p], scores, -jnp.inf)
        powers = jnp.exp(scores - jnp.max(scores, axis=-1, keepdims=True))
        weights = (powers / jnp.sum(powers, axis=-1, keepdims=True)).astype(bf16)
        sums.append(jnp.dot(weights, rows, preferred_element_type=f32))
    u = jnp.concatenate(sums, axis=0)
    first = u.astype(bf16)
    rest = u - first.astype(f32)
    second = rest.astype(bf16)
    third = (rest - second.astype(f32)).astype(bf16)
    for copy in copies[1]:
        copy.wait()
    weight = w_ref[1].reshape(Y_LO * Z * HEAD, 256)
    stacked = jnp.dot(
        jnp.concatenate([third, second, first], axis=0), weight, preferred_element_type=f32
    )
    total = stacked[:16] + stacked[16:32] + stacked[32:]
    head = lax.broadcasted_iota(jnp.int32, (16, HEAD), 0)
    context = jnp.where((head & 7) < 4, total[:, :HEAD], total[:, HEAD:])
    turned = jnp.concatenate([context[8:], context[:8]], axis=0)
    context = jnp.where(core == 0, context, turned).astype(bf16)
    out_ref[...] = jnp.broadcast_to(context[None], out_ref.shape)


def attend(place, lengths, normed, other, cosine, sine, parts, gathered):
    return pl.pallas_call(
        attend_body,
        out_shape=jax.ShapeDtypeStruct((2 * Z, 16, HEAD), bf16),
        in_specs=[SMEM, SMEM, VMEM, VMEM, VMEM, VMEM, HBM, HBM],
        out_specs=VMEM,
        scratch_shapes=[
            pltpu.VMEM((2, Y_LO, Z, HEAD, 256), bf16),
            pltpu.VMEM((2 * Z, 16, HEAD), bf16),
            pltpu.SemaphoreType.DMA((2, 2)),
            pltpu.SemaphoreType.DMA((1,)),
        ],
        compiler_params=pltpu.CompilerParams(vmem_limit_bytes=48 << 20),
        name="attend",
    )(place, lengths, normed, other, cosine, sine, parts, gathered)


def local(
    hidden, lengths, list_ids, list_owner, attn_gain, final_gain, w_query, w_key, w_value, w_out
):
    _, seq_len, width = hidden.shape
    dp, fsdp = lax.axis_index("dp"), lax.axis_index("fsdp")
    core, x = dp & 1, (dp >> 1) & (X - 1)
    y_lo = fsdp >> 4
    place = jnp.stack([lengths[0] - 1, x, core, y_lo]).astype(jnp.int32)

    unit = core_unit(place, w_key, w_value)
    units = pair(unit, lax.ppermute(unit, "fsdp", Y_LO_SWAP))
    gathered = lax.all_gather(units, "fsdp", axis=0, tiled=False, axis_index_groups=Z_GROUPS)

    unit, hidden = lax.optimization_barrier((unit, hidden))
    outgoing = open_payload(place, hidden, attn_gain)
    units, outgoing = lax.optimization_barrier((units, outgoing))
    arrived = lax.all_to_all(outgoing, "fsdp", 0, 0, tiled=True, axis_index_groups=Z_GROUPS)
    w_query_other = lax.ppermute(w_query, "fsdp", Y_LO_SWAP)

    payload = query_payload(place, arrived, w_query, w_query_other, w_out)
    parts = lax.all_to_all(payload, BOTH, 0, 0, tiled=True, axis_index_groups=CORE_Z_GROUPS)

    lengths, arrived, _ = lax.optimization_barrier((lengths, arrived, payload))
    far_inputs = lax.ppermute(arrived[:, 3], "fsdp", Y_LO_SWAP)
    both_lengths = jnp.concatenate([lengths, lax.ppermute(lengths, "dp", CORE_SWAP)])
    cosine, sine = rope_tables(jnp.arange(seq_len), HEAD)
    rows, parts, far_inputs, both_lengths, cosine, sine = lax.optimization_barrier(
        (hidden[0], parts, far_inputs, both_lengths, cosine, sine)
    )
    floats = rows.astype(f32)
    normed = (
        floats * lax.rsqrt(jnp.mean(floats * floats, axis=-1, keepdims=True) + 1e-05) * attn_gain
    ).astype(bf16)
    other = lax.ppermute(normed, "dp", CORE_SWAP)

    weight = lax.all_gather(
        parts[:, WEIGHT_ROW:], "dp", axis=0, tiled=False, axis_index_groups=X_GROUPS
    ).reshape(X, 2, Z, 8, HEAD)
    weight = jnp.transpose(weight, (2, 1, 0, 3, 4)).reshape(2 * Z * 32, HEAD)
    weight = jnp.where(core == y_lo, weight, lax.ppermute(weight, BOTH, CROSS_SWAP))
    near, far = arrived[:, 2], far_inputs
    inputs = jnp.concatenate([jnp.where(y_lo == 0, near, far), jnp.where(y_lo == 0, far, near)])
    inputs = inputs.astype(f32)
    gain = lax.dynamic_slice(final_gain, (fsdp * HEAD,), (HEAD,))

    owner_count = lax.axis_size("dp")
    capacity = 4
    list_index = jnp.arange(list_owner.shape[0])
    owners = jnp.sum(
        jnp.where(list_ids[:, None] == list_index[None, :], list_owner[None, :], 0), axis=1
    )
    owner_marks = (owners[:, None] == jnp.arange(owner_count)[None, :]).astype(jnp.int32)
    slot_rank = jnp.sum((jnp.cumsum(owner_marks, axis=0) - owner_marks) * owner_marks, axis=1)
    select = (
        (owners[None, None, :] == jnp.arange(owner_count)[:, None, None])
        & (slot_rank[None, None, :] == jnp.arange(capacity)[None, :, None])
    ).astype(bf16)

    (
        gathered, weight, both_lengths, normed, other, cosine, sine, inputs, gain, select
    ) = lax.optimization_barrier(
        (gathered, weight, both_lengths, normed, other, cosine, sine, inputs, gain, select)
    )
    context = attend(place, both_lengths, normed, other, cosine, sine, parts, gathered)
    contexts = lax.all_to_all(context, "fsdp", 0, 0, tiled=True)

    slabs = width // HEAD
    contexts = contexts.reshape(slabs, 2, 8 * HEAD)
    halves = jnp.einsum("sad,dn->asn", contexts, weight, preferred_element_type=f32)
    kept = lax.dynamic_index_in_dim(halves, core, 0, keepdims=False)
    given = lax.dynamic_index_in_dim(halves, 1 - core, 0, keepdims=False)
    residual = inputs + (kept + lax.ppermute(given, "dp", CORE_SWAP))
    scaled = residual * gain
    partial = jnp.sum(scaled * scaled, axis=-1)
    squares = lax.all_to_all(
        jnp.broadcast_to(partial[None, None, :], (slabs, 1, slabs)), "fsdp", 0, 0, tiled=True
    )
    mean = jnp.sum(squares, axis=0)[0] / width
    slab = (scaled * lax.rsqrt(mean + 1e-06)[:, None]).astype(bf16)

    outgoing = jnp.einsum("osr,rd->osd", select, slab, preferred_element_type=f32).astype(bf16)
    return lax.all_to_all(outgoing[:, None], "dp", split_axis=0, concat_axis=1, tiled=True)


def solution(mesh):
    in_specs = (
        P(("dp", "fsdp"), None, None),
        P(("dp", "fsdp")),
        P("dp"),
        P(),
        P(),
        P(),
        P("fsdp", None),
        P("fsdp", None),
        P("fsdp", None),
        P("fsdp", None),
    )
    out_specs = P("dp", None, None, "fsdp")
    return jax.shard_map(local, mesh=mesh, in_specs=in_specs, out_specs=out_specs, check_vma=False)
```

```python
import math

import jax
import jax.numpy as jnp
from jax import lax
from jax.experimental import pallas as pl
from jax.experimental.pallas import tpu as pltpu
from jax.sharding import PartitionSpec as P

HEADS = 16
KV_HEADS = 4
HEAD = 128
X = 4
Y_LO = 2
Z = 16
BOTH = ("dp", "fsdp")

bf16 = jnp.bfloat16
f32 = jnp.float32
VMEM = pl.BlockSpec(memory_space=pltpu.VMEM)
SMEM = pl.BlockSpec(memory_space=pltpu.SMEM)
HBM = pl.BlockSpec(memory_space=pltpu.HBM)


def dp_index(y_hi, x, core):
    return (y_hi * X + x) * 2 + core


def fsdp_index(y_lo, z):
    return y_lo * Z + z


Z_GROUPS = [[fsdp_index(yl, z) for z in range(Z)] for yl in range(Y_LO)]
X_GROUPS = [[dp_index(yh, x, c) for x in range(X)] for yh in range(2) for c in range(2)]
CORE_Z_GROUPS = [
    [dp_index(yh, x, c) * 32 + fsdp_index(yl, z) for c in range(2) for z in range(Z)]
    for yh in range(2)
    for x in range(X)
    for yl in range(Y_LO)
]
CROSS_SWAP = [
    (
        dp_index(yh, x, c) * 32 + fsdp_index(1 - c, z),
        dp_index(yh, x, 1 - c) * 32 + fsdp_index(c, z),
    )
    for yh in range(2)
    for x in range(X)
    for c in range(2)
    for z in range(Z)
]
CORE_SWAP = [(d, d ^ 1) for d in range(16)]
Y_LO_SWAP = [(i, i ^ Z) for i in range(32)]


def rope_tables(positions, head_width):
    halfway = head_width // 2
    frequency = 10000.0 ** (-jnp.arange(halfway, dtype=f32) * 2.0 / head_width)
    angles = positions.astype(f32)[..., None] * frequency
    cosine, sine = jnp.cos(angles), jnp.sin(angles)
    return (
        jnp.concatenate([cosine, cosine], axis=-1),
        jnp.concatenate([-sine, sine], axis=-1),
    )


def unit_body(place_ref, key_ref, value_ref, out_ref):
    core = place_ref[2]
    for k, w in enumerate((key_ref, value_ref)):
        columns = pl.multiple_of(core * 256, 256)
        out_ref[:, k * 256 : (k + 1) * 256] = w[:, pl.ds(columns, 256)]


def core_unit(place, w_key, w_value):
    return pl.pallas_call(
        unit_body,
        out_shape=jax.ShapeDtypeStruct((w_key.shape[0], 512), bf16),
        in_specs=[SMEM, VMEM, VMEM],
        out_specs=VMEM,
        compiler_params=pltpu.CompilerParams(vmem_limit_bytes=62 << 20),
        name="unit",
    )(place, w_key, w_value)


def pair_body(near_ref, far_ref, out_ref):
    out_ref[0] = near_ref[...]
    out_ref[1] = far_ref[...]


def pair(near, far):
    return pl.pallas_call(
        pair_body,
        out_shape=jax.ShapeDtypeStruct((2, *near.shape), bf16),
        in_specs=[VMEM, VMEM],
        out_specs=VMEM,
        compiler_params=pltpu.CompilerParams(vmem_limit_bytes=8 << 20),
        name="pair",
    )(near, far)


def open_body(place_ref, hidden, gain_ref, out_ref, block, sem):
    last, y_lo = place_ref[0], place_ref[3]
    first = pl.multiple_of((last >> 3) << 3, 8)
    copy = pltpu.make_async_copy(hidden.at[0, pl.ds(first, 8)], block, sem.at[0])
    copy.start()
    copy.wait()
    floats = block[...].astype(f32)
    pick = lax.broadcasted_iota(jnp.int32, floats.shape, 0) == (last & 7)
    row = jnp.sum(jnp.where(pick, floats, 0.0), axis=0, keepdims=True)
    normed = row * lax.rsqrt(jnp.mean(row * row, axis=-1, keepdims=True) + 1e-05) * gain_ref[...]
    normed = normed.astype(bf16).astype(f32)
    half = normed.shape[1] // 2
    place = lax.broadcasted_iota(jnp.int32, (8, HEAD), 0)
    near, far = (
        [jnp.where(y_lo == y, v[:, :half], v[:, half:]) for v in (normed, row)] for y in range(2)
    )
    for z in range(Z):
        tile = jnp.zeros((8, HEAD), f32)
        for n, v in enumerate((near[0], far[0], near[1], far[1])):
            tile = jnp.where(place == n, v[:, z * HEAD : (z + 1) * HEAD], tile)
        out_ref[z] = tile.astype(bf16)


def open_payload(place, hidden, gain):
    width = hidden.shape[2]
    return pl.pallas_call(
        open_body,
        out_shape=jax.ShapeDtypeStruct((Z, 8, HEAD), bf16),
        in_specs=[SMEM, HBM, VMEM],
        out_specs=VMEM,
        scratch_shapes=[pltpu.VMEM((8, width), bf16), pltpu.SemaphoreType.DMA((1,))],
        compiler_params=pltpu.CompilerParams(vmem_limit_bytes=62 << 20),
        name="open",
    )(place, hidden, gain[None, :])


ROWS = 24
WEIGHT_ROW = 16


def query_body(place_ref, arrived_ref, near_ref, far_ref, w_out_ref, out_ref, parts):
    x, core = place_ref[1], place_ref[2]
    rows = w_out_ref[...].astype(f32)
    weight = rows[:8]
    for n in range(1, 2 * X):
        weight = jnp.where(core * X + x == n, rows[n * 8 : n * 8 + 8], weight)
    weight = weight.astype(bf16)
    features = arrived_ref[...].astype(f32)
    total = jnp.dot(
        features[:, 0, :].astype(bf16), near_ref[...], preferred_element_type=f32
    ) + jnp.dot(features[:, 1, :].astype(bf16), far_ref[...], preferred_element_type=f32)
    high = total.astype(bf16).astype(f32)
    low = total - high
    for h in range(HEADS):
        c, cut = h // 8, slice(h * HEAD, (h + 1) * HEAD)
        parts[c * Z : (c + 1) * Z, h % 8, :] = high[:, cut]
        parts[c * Z : (c + 1) * Z, 8 + h % 8, :] = low[:, cut]
    out_ref[:, :WEIGHT_ROW, :] = parts[...].astype(bf16)
    for n in range(2 * Z):
        out_ref[n, WEIGHT_ROW:, :] = weight[:, n * HEAD : (n + 1) * HEAD]


def query_payload(place, arrived, near, far, w_out):
    return pl.pallas_call(
        query_body,
        out_shape=jax.ShapeDtypeStruct((2 * Z, ROWS, HEAD), bf16),
        in_specs=[SMEM, VMEM, VMEM, VMEM, VMEM],
        out_specs=VMEM,
        scratch_shapes=[pltpu.VMEM((2 * Z, 16, HEAD), f32)],
        compiler_params=pltpu.CompilerParams(vmem_limit_bytes=12 << 20),
        name="query",
    )(place, arrived, near, far, w_out)


def attend_body(
    place_ref, len_ref, normed_ref, other, cos_ref, sin_ref, parts, gathered, out_ref, w_ref, q_ref, other_ref, sem, q_sem
):
    fetch = pltpu.make_async_copy(parts.at[:, pl.ds(0, 16), :], q_ref, q_sem.at[0])
    fetch.start()
    core, y_lo = place_ref[2], place_ref[3]
    copies = [
        [
            pltpu.make_async_copy(
                gathered.at[:, n, :, pl.ds(kind * 256, 256)],
                w_ref.at[kind, y_lo if n == 0 else 1 - y_lo],
                sem.at[kind, n],
            )
            for n in range(2)
        ]
        for kind in range(2)
    ]
    fill = pltpu.make_async_copy(other, other_ref, q_sem.at[1])
    for copy in copies[0] + [fill] + copies[1]:
        copy.start()
    cosine, sine = cos_ref[...], sin_ref[...]
    fetch.wait()
    by_core = [jnp.sum(q_ref[c * Z : (c + 1) * Z].astype(f32), axis=0) for c in range(2)]
    by_core = [both[:8] + both[8:] for both in by_core]
    queries = []
    for p in range(2):
        summed = jnp.where(core == p, by_core[0], by_core[1])
        last = len_ref[p] - 1
        turned = summed * cos_ref[pl.ds(last, 1), :] + pltpu.roll(summed, HEAD // 2, 1) * sin_ref[
            pl.ds(last, 1), :
        ]
        queries.append((turned * (1.0 / math.sqrt(HEAD))).astype(bf16))
    for copy in copies[0]:
        copy.wait()
    weight = w_ref[0].reshape(Y_LO * Z * HEAD, 256)
    sums = []
    for p, rows_ref in enumerate((normed_ref, other_ref)):
        if p == 1:
            fill.wait()
        rows = rows_ref[...]
        keys = jnp.dot(rows, weight, preferred_element_type=f32)
        scores = []
        for g in range(2):
            part = keys[:, g * HEAD : (g + 1) * HEAD]
            turned = (part * cosine + pltpu.roll(part, HEAD // 2, 1) * sine).astype(bf16)
            scores.append(
                lax.dot_general(
                    queries[p], turned, (((1,), (1,)), ((), ())), preferred_element_type=f32
                )
            )
        head = lax.broadcasted_iota(jnp.int32, scores[0].shape, 0)
        place = lax.broadcasted_iota(jnp.int32, scores[0].shape, 1)
        scores = jnp.where(head < 4, scores[0], scores[1])
        scores = jnp.where(place < len_ref[p], scores, -jnp.inf)
        powers = jnp.exp(scores - jnp.max(scores, axis=-1, keepdims=True))
        weights = (powers / jnp.sum(powers, axis=-1, keepdims=True)).astype(bf16)
        sums.append(jnp.dot(weights, rows, preferred_element_type=f32))
    u = jnp.concatenate(sums, axis=0)
    first = u.astype(bf16)
    rest = u - first.astype(f32)
    second = rest.astype(bf16)
    third = (rest - second.astype(f32)).astype(bf16)
    for copy in copies[1]:
        copy.wait()
    weight = w_ref[1].reshape(Y_LO * Z * HEAD, 256)
    stacked = jnp.dot(
        jnp.concatenate([third, second, first], axis=0), weight, preferred_element_type=f32
    )
    total = stacked[:16] + stacked[16:32] + stacked[32:]
    head = lax.broadcasted_iota(jnp.int32, (16, HEAD), 0)
    context = jnp.where((head & 7) < 4, total[:, :HEAD], total[:, HEAD:])
    turned = jnp.concatenate([context[8:], context[:8]], axis=0)
    context = jnp.where(core == 0, context, turned).astype(bf16)
    out_ref[...] = jnp.broadcast_to(context[None], out_ref.shape)


def attend(place, lengths, normed, other, cosine, sine, parts, gathered):
    return pl.pallas_call(
        attend_body,
        out_shape=jax.ShapeDtypeStruct((2 * Z, 16, HEAD), bf16),
        in_specs=[SMEM, SMEM, VMEM, HBM, VMEM, VMEM, HBM, HBM],
        out_specs=VMEM,
        scratch_shapes=[
            pltpu.VMEM((2, Y_LO, Z, HEAD, 256), bf16),
            pltpu.VMEM((2 * Z, 16, HEAD), bf16),
            pltpu.VMEM(other.shape, bf16),
            pltpu.SemaphoreType.DMA((2, 2)),
            pltpu.SemaphoreType.DMA((2,)),
        ],
        compiler_params=pltpu.CompilerParams(vmem_limit_bytes=48 << 20),
        name="attend",
    )(place, lengths, normed, other, cosine, sine, parts, gathered)


def local(
    hidden, lengths, list_ids, list_owner, attn_gain, final_gain, w_query, w_key, w_value, w_out
):
    _, seq_len, width = hidden.shape
    dp, fsdp = lax.axis_index("dp"), lax.axis_index("fsdp")
    core, x = dp & 1, (dp >> 1) & (X - 1)
    y_lo = fsdp >> 4
    place = jnp.stack([lengths[0] - 1, x, core, y_lo]).astype(jnp.int32)

    unit = core_unit(place, w_key, w_value)
    units = pair(unit, lax.ppermute(unit, "fsdp", Y_LO_SWAP))
    gathered = lax.all_gather(units, "fsdp", axis=0, tiled=False, axis_index_groups=Z_GROUPS)

    unit, hidden = lax.optimization_barrier((unit, hidden))
    outgoing = open_payload(place, hidden, attn_gain)
    units, outgoing = lax.optimization_barrier((units, outgoing))
    arrived = lax.all_to_all(outgoing, "fsdp", 0, 0, tiled=True, axis_index_groups=Z_GROUPS)
    w_query_other = lax.ppermute(w_query, "fsdp", Y_LO_SWAP)

    payload = query_payload(place, arrived, w_query, w_query_other, w_out)
    parts = lax.all_to_all(payload, BOTH, 0, 0, tiled=True, axis_index_groups=CORE_Z_GROUPS)

    lengths, arrived, _ = lax.optimization_barrier((lengths, arrived, payload))
    far_inputs = lax.ppermute(arrived[:, 3], "fsdp", Y_LO_SWAP)
    both_lengths = jnp.concatenate([lengths, lax.ppermute(lengths, "dp", CORE_SWAP)])
    cosine, sine = rope_tables(jnp.arange(seq_len), HEAD)
    rows, parts, far_inputs, both_lengths, cosine, sine = lax.optimization_barrier(
        (hidden[0], parts, far_inputs, both_lengths, cosine, sine)
    )
    floats = rows.astype(f32)
    normed = (
        floats * lax.rsqrt(jnp.mean(floats * floats, axis=-1, keepdims=True) + 1e-05) * attn_gain
    ).astype(bf16)
    other = lax.ppermute(normed, "dp", CORE_SWAP)

    weight = lax.all_gather(
        parts[:, WEIGHT_ROW:], "dp", axis=0, tiled=False, axis_index_groups=X_GROUPS
    ).reshape(X, 2, Z, 8, HEAD)
    weight = jnp.transpose(weight, (2, 1, 0, 3, 4)).reshape(2 * Z * 32, HEAD)
    weight = jnp.where(core == y_lo, weight, lax.ppermute(weight, BOTH, CROSS_SWAP))
    near, far = arrived[:, 2], far_inputs
    inputs = jnp.concatenate([jnp.where(y_lo == 0, near, far), jnp.where(y_lo == 0, far, near)])
    inputs = inputs.astype(f32)
    gain = lax.dynamic_slice(final_gain, (fsdp * HEAD,), (HEAD,))

    owner_count = lax.axis_size("dp")
    capacity = 4
    list_index = jnp.arange(list_owner.shape[0])
    owners = jnp.sum(
        jnp.where(list_ids[:, None] == list_index[None, :], list_owner[None, :], 0), axis=1
    )
    owner_marks = (owners[:, None] == jnp.arange(owner_count)[None, :]).astype(jnp.int32)
    slot_rank = jnp.sum((jnp.cumsum(owner_marks, axis=0) - owner_marks) * owner_marks, axis=1)
    select = (
        (owners[None, None, :] == jnp.arange(owner_count)[:, None, None])
        & (slot_rank[None, None, :] == jnp.arange(capacity)[None, :, None])
    ).astype(bf16)

    (
        gathered, weight, both_lengths, normed, other, cosine, sine, inputs, gain, select
    ) = lax.optimization_barrier(
        (gathered, weight, both_lengths, normed, other, cosine, sine, inputs, gain, select)
    )
    context = attend(place, both_lengths, normed, other, cosine, sine, parts, gathered)
    contexts = lax.all_to_all(context, "fsdp", 0, 0, tiled=True)

    slabs = width // HEAD
    contexts = contexts.reshape(slabs, 2, 8 * HEAD)
    halves = jnp.einsum("sad,dn->asn", contexts, weight, preferred_element_type=f32)
    kept = lax.dynamic_index_in_dim(halves, core, 0, keepdims=False)
    given = lax.dynamic_index_in_dim(halves, 1 - core, 0, keepdims=False)
    residual = inputs + (kept + lax.ppermute(given, "dp", CORE_SWAP))
    scaled = residual * gain
    partial = jnp.sum(scaled * scaled, axis=-1)
    squares = lax.all_to_all(
        jnp.broadcast_to(partial[None, None, :], (slabs, 1, slabs)), "fsdp", 0, 0, tiled=True
    )
    mean = jnp.sum(squares, axis=0)[0] / width
    slab = (scaled * lax.rsqrt(mean + 1e-06)[:, None]).astype(bf16)

    outgoing = jnp.einsum("osr,rd->osd", select, slab, preferred_element_type=f32).astype(bf16)
    return lax.all_to_all(outgoing[:, None], "dp", split_axis=0, concat_axis=1, tiled=True)


def solution(mesh):
    in_specs = (
        P(("dp", "fsdp"), None, None),
        P(("dp", "fsdp")),
        P("dp"),
        P(),
        P(),
        P(),
        P("fsdp", None),
        P("fsdp", None),
        P("fsdp", None),
        P("fsdp", None),
    )
    out_specs = P("dp", None, None, "fsdp")
    return jax.shard_map(local, mesh=mesh, in_specs=in_specs, out_specs=out_specs, check_vma=False)
```
